32 devices in a mesh: elem: 4 (over z), span: 8 (over y, x, core).
Axes of the slice: x: 2, y: 2, z: 4, core: 2. Of those that a mesh axis runs over, the one named last changes fastest.
Arguments:
- state: float32 [4, 256, 9216], P(None, 'span', 'elem'), may hold values from -6 to 6
- metric: float32 [2, 256], P(None, 'elem'), may hold values from -40 to 40, as said below
- neighbour: int32 [256, 4], P('elem'), may hold values from 0 to 287, as said below
- orient: int32 [256, 4], P('elem'), may hold values from 0 to 1, as said below
- wall: int32 [256, 4], P('elem'), may hold values from 0 to 1, as said below
- rim: int32 [2, 64], P(None, 'elem'), may hold values from 0 to 255, as said below
Outputs:
- updated: float32 [4, 256, 9216], P(None, 'span', 'elem')
The draws below stay inside these ranges and needn't reach their ends.
Inputs may be any that keep to these rules, and one draw needn't show every extreme that they name: neighbour[e, s] is a slot of e's element group's trace pool: e' * 4 + s' for the facing side s' of a local element e' (local index within the group), 256 + r for row r of the lower group's rim, 272 + r for row r of the upper group's rim; on a wall side it is e's own slot. Elements form a channel of 16 rows and 4 columns per group, periodic in x over the groups, in an order drawn per group; elements may be reflected in either reference direction. `orient`: 0 on wall sides. `wall`: 1 exactly on the sides of the first and last rows that face the walls. rim[0, g * 16 + r] is the local slot e * 4 + s of the side of group g's first-column element in row r that faces the lower group; rim[1] likewise for the last column and the upper group. Nonzero; the magnitude of metric[0] is equal along a global column of elements, that of metric[1] along a row; the sign is -1 where the element is reflected in that direction.
All inputs are finite; a program needn't handle non-finite values.
Results may differ from the reference program's by a relative error of at most 0.0003.
Values sent between devices are 32-bit elements; how exact they have to be, the bound alone decides.
No kernel may reach another device: no remote copies, remote signals or barrier semaphores. Data moves between devices by JAX's collectives and lax.ppermute only.
A program may use at most 64 MiB of HBM per device.

```python
import math
import jax
import jax.numpy as jnp
import numpy as np
from jax import lax

MODES = 256
ROWS = 16
COLS_DEV = 4
ELEMENTS = 256


def layout(key):
    base = jax.random.fold_in(key, 11)
    per_group = ROWS * COLS_DEV
    groups = ELEMENTS // per_group
    group_keys = jax.random.split(base, groups)
    slot_cell = jax.vmap(lambda single: jax.random.permutation(single, per_group))(group_keys).astype(jnp.int32)
    cell_slot = jnp.argsort(slot_cell, axis=1, stable=True).astype(jnp.int32)
    flips = jax.random.randint(jax.random.fold_in(base, 5), (groups, per_group, 2), 0, 2).astype(jnp.int32)
    return (slot_cell, cell_slot, flips)


def tables(key):
    slot_cell, cell_slot, flips = layout(key)
    groups, per_group = slot_cell.shape
    column = slot_cell // ROWS
    row_of = slot_cell % ROWS
    flip_x = flips[:, :, 0]
    flip_y = flips[:, :, 1]
    group_ids = jnp.zeros_like(column) + jnp.arange(groups, dtype=jnp.int32)[:, None]
    own_slots = jnp.zeros_like(column) + jnp.arange(per_group, dtype=jnp.int32)[None, :]
    indices = []
    orients = []
    walls = []
    for side in range(4):
        if side < 2:
            upward = jnp.bitwise_xor(flip_x, side) == 1
            stride = jnp.where(upward, 1, -1)
            next_col = column + stride
            inside = (next_col >= 0) & (next_col < COLS_DEV)
            next_group = (group_ids + jnp.where(inside, 0, stride)) % groups
            next_slot = cell_slot[next_group, next_col % COLS_DEV * ROWS + row_of]
            next_fx = flips[next_group, next_slot, 0]
            next_fy = flips[next_group, next_slot, 1]
            facing = jnp.where(upward, next_fx, 1 - next_fx)
            remote = 4 * per_group + jnp.where(upward, ROWS, 0) + row_of
            indices.append(jnp.where(inside, next_slot * 4 + facing, remote))
            orients.append(jnp.where(flip_y != next_fy, 1, 0))
            walls.append(jnp.zeros_like(column))
        else:
            upward = jnp.bitwise_xor(flip_y, side - 2) == 1
            stride = jnp.where(upward, 1, -1)
            next_row = row_of + stride
            inside = (next_row >= 0) & (next_row < ROWS)
            next_slot = cell_slot[group_ids, column * ROWS + next_row % ROWS]
            next_fx = flips[group_ids, next_slot, 0]
            next_fy = flips[group_ids, next_slot, 1]
            facing = 2 + jnp.where(upward, next_fy, 1 - next_fy)
            indices.append(jnp.where(inside, next_slot * 4 + facing, own_slots * 4 + side))
            orients.append(jnp.where(inside & (flip_x != next_fx), 1, 0))
            walls.append(jnp.where(inside, 0, 1))
    row_cells = jnp.arange(ROWS, dtype=jnp.int32)
    lower_slot = cell_slot[:, row_cells]
    lower_fx = jnp.take_along_axis(flip_x, lower_slot, axis=1)
    upper_slot = cell_slot[:, (COLS_DEV - 1) * ROWS + row_cells]
    upper_fx = jnp.take_along_axis(flip_x, upper_slot, axis=1)
    rim_table = jnp.stack([(lower_slot * 4 + lower_fx).reshape(-1), (upper_slot * 4 + 1 - upper_fx).reshape(-1)])
    index_table = jnp.stack(indices, axis=2).reshape(groups * per_group, 4).astype(jnp.int32)
    orient_table = jnp.stack(orients, axis=2).reshape(groups * per_group, 4).astype(jnp.int32)
    wall_table = jnp.stack(walls, axis=2).reshape(groups * per_group, 4).astype(jnp.int32)
    return (index_table, orient_table, wall_table, rim_table.astype(jnp.int32))


def draw_neighbour(key, part):
    return tables(key)[0]


def draw_orient(key, part):
    return tables(key)[1]


def draw_wall(key, part):
    return tables(key)[2]


def draw_rim(key, part):
    return tables(key)[3]


def draw_metric(key, part):
    slot_cell, cell_slot, flips = layout(key)
    groups, per_group = slot_cell.shape
    col_key, row_key = jax.random.split(jax.random.fold_in(key, 29))
    widths = jnp.exp(jax.random.uniform(col_key, (groups * COLS_DEV,), jnp.float32, math.log(10.0), math.log(40.0)))
    heights = jnp.exp(jax.random.uniform(row_key, (ROWS,), jnp.float32, math.log(10.0), math.log(40.0)))
    global_col = slot_cell // ROWS + jnp.arange(groups, dtype=jnp.int32)[:, None] * COLS_DEV
    along_x = widths[global_col] * (1.0 - 2.0 * flips[:, :, 0].astype(jnp.float32))
    along_y = heights[slot_cell % ROWS] * (1.0 - 2.0 * flips[:, :, 1].astype(jnp.float32))
    return jnp.stack([along_x.reshape(-1), along_y.reshape(-1)]).astype(jnp.float32)


def shard_levels(key, dims, pieces, low, largest):
    loudness, own = 1.0, jax.random.fold_in(key, 6)
    for axis_at, blocks in pieces:
        draws = jnp.exp(jax.random.uniform(jax.random.fold_in(own, axis_at), (blocks,), jnp.float32, low / len(pieces), largest / len(pieces)))
        loudness = loudness * jnp.repeat(draws, dims[axis_at] // blocks).reshape([-1 if axis == axis_at else 1 for axis in range(len(dims))])
    return loudness


def scatter_about(rng, shape, spread, limit, pieces=(), kind=jnp.bfloat16):
    values = jax.random.normal(rng, shape, jnp.float32) * spread
    if len(pieces) > 0:
        values = shard_levels(rng, shape, pieces, -0.22, 0.18) * values
    return jnp.clip(values, min=-limit, max=limit).astype(kind)


def setup_inputs(seed: int = 0) -> dict:
    streams_of = jax.random.split(jax.random.key(seed), 7)
    state = scatter_about(streams_of[0], (4, MODES, ELEMENTS * 36), 1.0, 6.0, ((1, 8), (2, 4)), jnp.float32)
    metric = draw_metric(jax.random.fold_in(streams_of[6], 71), 0)
    neighbour = draw_neighbour(jax.random.fold_in(streams_of[6], 71), 0)
    orient = draw_orient(jax.random.fold_in(streams_of[6], 71), 0)
    wall = draw_wall(jax.random.fold_in(streams_of[6], 71), 0)
    rim = draw_rim(jax.random.fold_in(streams_of[6], 71), 0)
    return dict(state=state, metric=metric, neighbour=neighbour, orient=orient, wall=wall, rim=rim)


TIME_STEP = 0.001
VISCOSITY = 0.02
PENALTY = 1.0
HIGHEST = lax.Precision.HIGHEST

def gll_tables():
    near_point = math.sqrt(1.0 / 3.0 - 2.0 * math.sqrt(7.0) / 21.0)
    far_point = math.sqrt(1.0 / 3.0 + 2.0 * math.sqrt(7.0) / 21.0)
    points = np.array([-1.0, -far_point, -near_point, near_point, far_point, 1.0])
    weights = np.array([1.0 / np.prod([points[column] - points[second] for second in range(6) if second != column]) for column in range(6)])
    deriv = np.zeros((6, 6))
    for target in range(6):
        for source in range(6):
            if source != target:
                deriv[target, source] = weights[source] / weights[target] / (points[target] - points[source])
        deriv[target, target] = -np.sum(deriv[target])
    identity = np.eye(6)
    along_x = np.kron(deriv, identity)
    along_y = np.kron(identity, deriv)
    edge_nodes = np.array([[offset for offset in range(6)], [30 + offset for offset in range(6)], [6 * offset for offset in range(6)], [6 * offset + 5 for offset in range(6)]]).reshape(-1)
    lifting = np.zeros((36, 24))
    lifting[edge_nodes, np.arange(24)] = 1.0
    return (jnp.asarray(along_x, jnp.float32), jnp.asarray(along_y, jnp.float32), edge_nodes, jnp.asarray(lifting, jnp.float32))

def spanwise_basis(count):
    mode_index = jnp.arange(count, dtype=jnp.int32)
    planes = jnp.arange(count, dtype=jnp.int32)
    phase = mode_index[:, None] // 2 * planes[None, :] % count
    phase_angle = phase.astype(jnp.float32) * (2.0 * math.pi / count)
    odd_rows = (mode_index % 2 == 1)[:, None]
    basis_table = jnp.where(odd_rows, jnp.sin(phase_angle), jnp.cos(phase_angle)) * math.sqrt(2.0 / count)
    alternate = (1 - 2 * (planes % 2)).astype(jnp.float32) / math.sqrt(count)
    constant = jnp.ones((count,), jnp.float32) / math.sqrt(count)
    basis_table = jnp.where(mode_index[:, None] == 0, constant[None, :], basis_table)
    basis_table = jnp.where(mode_index[:, None] == 1, alternate[None, :], basis_table)
    return basis_table

def spanwise_derivative(modal):
    shape_in = modal.shape
    paired = modal.reshape(shape_in[0], shape_in[1] // 2, 2, shape_in[2])
    wavenumber = jnp.arange(shape_in[1] // 2, dtype=jnp.int32).astype(jnp.float32)[None, :, None]
    return jnp.stack([wavenumber * paired[:, :, 1], -wavenumber * paired[:, :, 0]], axis=2).reshape(shape_in)

def modal_divergence(flux_x, flux_y, along_z, metric_local):
    along_x, along_y, edge_nodes, lifting = gll_tables()
    scale_x = metric_local[0]
    scale_y = metric_local[1]
    grad_x = jnp.einsum('pq,vmqe->vmpe', along_x, flux_x, precision=HIGHEST)
    grad_y = jnp.einsum('pq,vmqe->vmpe', along_y, flux_y, precision=HIGHEST)
    divergence = scale_x * grad_x + scale_y * grad_y + along_z
    sign_x = jnp.sign(scale_x)
    sign_y = jnp.sign(scale_y)
    normal_flux = jnp.concatenate([-sign_x * flux_x[:, :, edge_nodes[0:6]], sign_x * flux_x[:, :, edge_nodes[6:12]], -sign_y * flux_y[:, :, edge_nodes[12:18]], sign_y * flux_y[:, :, edge_nodes[18:24]]], axis=2)
    return (divergence, normal_flux)

def trace_pool(traces):
    shape_in = traces.shape
    return traces.reshape(shape_in[0], shape_in[1], 4, 6, shape_in[3]).transpose(0, 1, 3, 4, 2).reshape(shape_in[0], shape_in[1], 6, 4 * shape_in[3])

def own_pools(state_local, normal_flux):
    edge_nodes = gll_tables()[2]
    return (trace_pool(state_local[:, :, edge_nodes, :]), trace_pool(normal_flux))

def update(state_local, divergence, own_q, own_flux, from_lower, from_upper, neighbour, orient, wall, metric_local, first_mode, total_modes):
    lifting = gll_tables()[3]
    num_vars, modes_here, num_nodes, count = state_local.shape
    pool_q = jnp.concatenate([own_q, from_lower[0], from_upper[0]], axis=3)
    pool_flux = jnp.concatenate([own_flux, from_lower[1], from_upper[1]], axis=3)
    flat_index = neighbour.reshape(-1)
    other_q = jnp.take(pool_q, flat_index, axis=3)
    other_flux = jnp.take(pool_flux, flat_index, axis=3)
    flipped = orient.reshape(-1) == 1
    other_q = jnp.where(flipped, other_q[:, :, ::-1, :], other_q)
    other_flux = jnp.where(flipped, other_flux[:, :, ::-1, :], other_flux)
    mirror = jnp.array([-1.0, -1.0, -1.0, 1.0], jnp.float32).reshape(4, 1, 1, 1)
    walled = wall.reshape(-1) == 1
    other_q = jnp.where(walled, mirror * own_q, other_q)
    other_flux = jnp.where(walled, mirror * own_flux, other_flux)
    magnitude = jnp.abs(jnp.stack([metric_local[0], metric_local[0], metric_local[1], metric_local[1]], axis=1)).reshape(-1) * 15.0
    surface_jump = magnitude * (0.5 * (own_flux + other_flux) - 0.5 * PENALTY * (own_q - other_q))
    unpooled = surface_jump.reshape(num_vars, modes_here, 6, count, 4).transpose(0, 1, 4, 2, 3).reshape(num_vars, modes_here, 24, count)
    surface = jnp.einsum('pq,vmqe->vmpe', lifting, unpooled, precision=HIGHEST)
    mode_index = first_mode + jnp.arange(modes_here, dtype=jnp.int32)
    wavenumber = jnp.where(mode_index == 1, total_modes // 2, mode_index // 2).astype(jnp.float32)
    damping = 1.0 + TIME_STEP * VISCOSITY * wavenumber * wavenumber
    return (state_local + TIME_STEP * (surface - divergence)) / damping[None, :, None, None]

def volume_terms(block):
    state_local, metric_local, rim_local = block
    num_vars, total_modes, num_nodes, count = state_local.shape
    basis_table = spanwise_basis(total_modes)
    physical = jnp.einsum('mn,vmk->vnk', basis_table, state_local.reshape(num_vars, total_modes, num_nodes * count), precision=HIGHEST)
    fields = jnp.concatenate([physical[0:1] * physical, physical[1:2] * physical, physical[2:3] * physical], axis=0)
    modal = jnp.einsum('mn,vnk->vmk', basis_table, fields, precision=HIGHEST)
    shape_back = (num_vars, total_modes, num_nodes, count)
    along_z = spanwise_derivative(modal[8:12]).reshape(shape_back)
    divergence, normal_flux = modal_divergence(modal[0:4].reshape(shape_back), modal[4:8].reshape(shape_back), along_z, metric_local)
    own_q, own_flux = own_pools(state_local, normal_flux)
    to_upper = jnp.stack([jnp.take(own_q, rim_local[1], axis=3), jnp.take(own_flux, rim_local[1], axis=3)])
    to_lower = jnp.stack([jnp.take(own_q, rim_local[0], axis=3), jnp.take(own_flux, rim_local[0], axis=3)])
    return (divergence, normal_flux, to_upper, to_lower)

def reference(state, metric, neighbour, orient, wall, rim):
    num_vars, total_modes, flat_size = state.shape
    num_nodes = 36
    total_elems = flat_size // num_nodes
    state_nodes = jnp.transpose(state.reshape(num_vars, total_modes, total_elems, num_nodes), (0, 1, 3, 2))
    groups = rim.shape[1] // ROWS
    per_group = total_elems // groups
    blocks = jnp.moveaxis(state_nodes.reshape(num_vars, total_modes, num_nodes, groups, per_group), 3, 0)
    metrics = jnp.moveaxis(metric.reshape(2, groups, per_group), 1, 0)
    rims = jnp.moveaxis(rim.reshape(2, groups, ROWS), 1, 0)
    divergence, normal_flux, to_upper, to_lower = lax.map(volume_terms, (blocks, metrics, rims))
    from_lower = jnp.roll(to_upper, 1, axis=0)
    from_upper = jnp.roll(to_lower, -1, axis=0)
    neighbours = neighbour.reshape(groups, per_group, 4)
    orients = orient.reshape(groups, per_group, 4)
    walls = wall.reshape(groups, per_group, 4)

    def finish(block):
        state_local, divergence_local, flux_local, lower_local, upper_local, neighbour_local, orient_local, wall_local, metric_local = block
        own_q, own_flux = own_pools(state_local, flux_local)
        return update(state_local, divergence_local, own_q, own_flux, lower_local, upper_local, neighbour_local, orient_local, wall_local, metric_local, 0, total_modes)
    result = lax.map(finish, (blocks, divergence, normal_flux, from_lower, from_upper, neighbours, orients, walls, metrics))
    result_nodes = jnp.moveaxis(result, 0, 3).reshape(num_vars, total_modes, num_nodes, total_elems)
    return jnp.transpose(result_nodes, (0, 1, 3, 2)).reshape(num_vars, total_modes, flat_size)
```

```python
import functools
import math

import jax
import jax.numpy as jnp
import numpy as np
from jax import lax
from jax.experimental import pallas as pl
from jax.experimental.pallas import tpu as pltpu
from jax.sharding import PartitionSpec as P

TIME_STEP = 0.001
VISCOSITY = 0.02
PENALTY = 1.0
HIGHEST = lax.Precision.HIGHEST
SIDE = 6
NODES = SIDE * SIDE
LANES = 128
SUB = 8


def gll_matrix():
    near_point = math.sqrt(1.0 / 3.0 - 2.0 * math.sqrt(7.0) / 21.0)
    far_point = math.sqrt(1.0 / 3.0 + 2.0 * math.sqrt(7.0) / 21.0)
    points = np.array([-1.0, -far_point, -near_point, near_point, far_point, 1.0])
    weights = np.array(
        [
            1.0
            / np.prod([points[column] - points[second] for second in range(6) if second != column])
            for column in range(6)
        ]
    )
    deriv = np.zeros((6, 6))
    for target in range(6):
        for source in range(6):
            if source != target:
                deriv[target, source] = (
                    weights[source] / weights[target] / (points[target] - points[source])
                )
        deriv[target, target] = -np.sum(deriv[target])
    return deriv


def basis_matrix(count):
    mode = np.arange(count)[:, None]
    plane = np.arange(count)[None, :]
    angle = (mode // 2 * plane % count) * (2.0 * math.pi / count)
    table = np.where(mode % 2 == 1, np.sin(angle), np.cos(angle)) * math.sqrt(2.0 / count)
    table = np.where(mode == 0, 1.0 / math.sqrt(count), table)
    return np.where(mode == 1, (1.0 - 2.0 * (plane % 2)) / math.sqrt(count), table)


def halves(table):
    table = np.asarray(table, np.float32)
    high = table.astype(jnp.bfloat16)
    low = (table - high.astype(np.float32)).astype(jnp.bfloat16)
    return high, low


def forward_tables(count):
    return halves(basis_matrix(count))


def backward_tables(count):
    basis = basis_matrix(count)
    wave = np.arange(count) // 2
    swapped = np.empty_like(basis)
    swapped[0::2] = wave[0::2, None] * basis[1::2]
    swapped[1::2] = -wave[1::2, None] * basis[0::2]
    damp_wave = np.where(np.arange(count) == 1, count // 2, wave).astype(np.float64)
    factor = TIME_STEP / (1.0 + TIME_STEP * VISCOSITY * damp_wave * damp_wave)
    return halves(factor[:, None] * np.concatenate([basis, -swapped], axis=1))


def split(value):
    high = value.astype(jnp.bfloat16)
    low = (value - high.astype(jnp.float32)).astype(jnp.bfloat16)
    return high, low


def mm(a, b):
    return lax.dot_general(a, b, (((1,), (0,)), ((), ())), preferred_element_type=jnp.float32)


def mm_nt(a, b):
    return lax.dot_general(a, b, (((1,), (1,)), ((), ())), preferred_element_type=jnp.float32)


def regroup(parts, lane):
    quarter = LANES // 4
    low_half = lane < 2 * quarter
    rolled = [pltpu.roll(part, 2 * quarter, 1) for part in parts]
    first = [
        jnp.where(low_half, parts[0], rolled[2]),
        jnp.where(low_half, parts[1], rolled[3]),
        jnp.where(low_half, rolled[0], parts[2]),
        jnp.where(low_half, rolled[1], parts[3]),
    ]
    even = lane // quarter % 2 == 0
    out = []
    for pair in (0, 2):
        a, b = first[pair], first[pair + 1]
        out.append(jnp.where(even, a, pltpu.roll(b, quarter, 1)))
        out.append(jnp.where(even, pltpu.roll(a, LANES - quarter, 1), b))
    return out


def spread_kernel(dims, where_ref, near_ref, wall_ref, rim_ref, metric_ref, state_ref, *refs):
    rows, cols, share, span = dims
    sends = refs[:span]
    pick_ref, facts_ref, flat = refs[span : span + 3]
    me = where_ref[0]
    elems = rows * cols
    lane = lax.broadcasted_iota(jnp.int32, (1, LANES), 1) % elems
    before = None
    for row in range(rows):
        cell = rim_ref[0, row] >> 2
        face = rim_ref[0, row] & 1
        here = []
        for col in range(cols):
            if row == 0:
                flip_y = wall_ref[3, cell]
            else:
                flip_y = jnp.where(near_ref[3, cell] >> 2 == before[col], 1, 0)
            here.append(cell)
            place = row * cols + col
            at = (place // share ^ me) * share + place % share
            pick_ref[pl.ds(at, 1), :] = jnp.where(lane == cell, 1.0, 0.0)
            facts = (
                metric_ref[0, cell],
                metric_ref[1, cell],
                face.astype(jnp.float32),
                flip_y.astype(jnp.float32),
            )
            for kind, fact in enumerate(facts):
                facts_ref[kind, pl.ds(at, 1), :] = jnp.full((1, LANES), fact, jnp.float32)
            if col + 1 < cols:
                step = near_ref[face ^ 1, cell]
                cell = step >> 2
                face = step & 1
        before = here
    for block in range(elems * NODES // LANES):
        at = pl.ds(block * LANES, LANES)
        flat[at, :] = state_ref[:, at].T
    pick = pick_ref[...].astype(jnp.bfloat16)
    for node in range(NODES):
        high, low = split(flat[pl.ds(node, elems, stride=NODES), :])
        moved = mm(pick, jnp.concatenate([high, low], axis=0))
        for step in range(span):
            sends[step][pl.ds(node * share, share), :] = moved[step * share : (step + 1) * share]


def sides_of(value, flip_x, flip_y):
    near_x = [jnp.where(flip_x, value(5, t), value(0, t)) for t in range(SIDE)]
    far_x = [jnp.where(flip_x, value(0, t), value(5, t)) for t in range(SIDE)]
    near_y = [jnp.where(flip_y, value(t, 5), value(t, 0)) for t in range(SIDE)]
    far_y = [jnp.where(flip_y, value(t, 0), value(t, 5)) for t in range(SIDE)]

    def along(trace, flip):
        return [jnp.where(flip, trace[SIDE - 1 - t], trace[t]) for t in range(SIDE)]

    return along(near_x, flip_y), along(far_x, flip_y), along(near_y, flip_x), along(far_y, flip_x)


def sign(value):
    return jnp.where(value < 0.0, -1.0, 1.0)


def planes_kernel(dims, where_ref, facts_ref, high_ref, low_ref, *refs):
    cols, share, span, num_vars, modes = dims
    takes = refs[:span]
    phys_ref, up_ref, down_ref, next_ref, prev_ref = refs[span:]
    me = where_ref[0]
    lane = lax.broadcasted_iota(jnp.int32, (1, LANES), 1)
    tables = []
    for ref in (high_ref, low_ref):
        tables.append(
            jnp.concatenate([ref[pl.ds((me ^ k) * modes, modes), :] for k in range(span)], axis=0)
        )
    pieces = []
    for group in range(span // 4):
        pieces.append(regroup([takes[4 * group + q][...] for q in range(4)], lane))
    count = span * modes
    for var in range(num_vars):
        high, low = split(jnp.concatenate([piece[var] for piece in pieces], axis=1))
        planes = mm(high, tables[0]) + mm(low, tables[0]) + mm(high, tables[1])
        for tile in range(count // LANES):
            phys_ref[tile, var] = planes[:, tile * LANES : (tile + 1) * LANES]
    flip_x = facts_ref[2] > 0.5
    flip_y = facts_ref[3] > 0.5
    turn_x = sign(facts_ref[0]) * (1.0 - 2.0 * facts_ref[2])
    turn_y = sign(facts_ref[1]) * (1.0 - 2.0 * facts_ref[3])

    def reader(tile, var):
        return lambda i, j: phys_ref[tile, var, pl.ds((SIDE * i + j) * SUB, SUB), :]

    for tile in range(count // LANES):
        speed_x = sides_of(reader(tile, 0), flip_x, flip_y)
        speed_y = sides_of(reader(tile, 1), flip_x, flip_y)
        for var in range(num_vars):
            trace = sides_of(reader(tile, var), flip_x, flip_y)
            for t in range(SIDE):
                low_x = (1.0 - turn_x * speed_x[0][t]) * trace[0][t]
                high_x = (1.0 + turn_x * speed_x[1][t]) * trace[1][t]
                low_y = (1.0 - turn_y * speed_y[2][t]) * trace[2][t]
                high_y = (1.0 + turn_y * speed_y[3][t]) * trace[3][t]
                lines = share // cols
                for line in range(lines):
                    at = pl.ds(t * lines + line, 1)
                    up_ref[tile, var, at, :] = high_x[(line + 1) * cols - 1 : (line + 1) * cols]
                    down_ref[tile, var, at, :] = low_x[line * cols : line * cols + 1]
                at = pl.ds(t * cols, cols)
                next_ref[tile, var, at, :] = high_y[share - cols :]
                prev_ref[tile, var, at, :] = low_y[:cols]


def rates_kernel(
    dims, where_ref, facts_ref, high_ref, low_ref, phys_ref, lower_ref, upper_ref, prev_ref,
    next_ref, *refs
):
    cols, share, span, num_vars, modes = dims
    outs = refs[:span]
    rate_ref = refs[span]
    me = where_ref[0]
    count = span * modes
    tiles = count // LANES
    lines = share // cols
    deriv = np.asarray(gll_matrix(), np.float32)
    lane = lax.broadcasted_iota(jnp.int32, (1, LANES), 1)
    slot = lax.broadcasted_iota(jnp.int32, (SUB, LANES), 0)
    flip_x = facts_ref[2] > 0.5
    flip_y = facts_ref[3] > 0.5
    scale_x = facts_ref[0]
    scale_y = facts_ref[1]
    turn_x = sign(scale_x) * (1.0 - 2.0 * facts_ref[2])
    turn_y = sign(scale_y) * (1.0 - 2.0 * facts_ref[3])
    weight_x = 7.5 * jnp.abs(scale_x)
    weight_y = 7.5 * jnp.abs(scale_y)
    first_col = slot % cols == 0
    last_col = slot % cols == cols - 1
    first_line = slot < cols
    last_line = slot >= share - cols
    at_floor = me == 0
    at_roof = me == span - 1

    for tile in range(tiles):

        def reader(var, tile=tile):
            return lambda i, j: phys_ref[tile, var, pl.ds((SIDE * i + j) * SUB, SUB), :]

        speed_x = sides_of(reader(0), flip_x, flip_y)
        speed_y = sides_of(reader(1), flip_x, flip_y)
        for var in range(num_vars):
            q = reader(var)
            mirror = 1.0 if var == num_vars - 1 else -1.0
            total = {}
            for j in range(SIDE):
                flux = [q(i, j) * reader(0)(i, j) for i in range(SIDE)]
                for i in range(SIDE):
                    acc = None
                    for s in range(SIDE):
                        if abs(deriv[i, s]) > 1e-6:
                            term = flux[s] * float(deriv[i, s])
                            acc = term if acc is None else acc + term
                    total[i, j] = -scale_x * acc
            for i in range(SIDE):
                flux = [q(i, j) * reader(1)(i, j) for j in range(SIDE)]
                for j in range(SIDE):
                    acc = None
                    for s in range(SIDE):
                        if abs(deriv[j, s]) > 1e-6:
                            term = flux[s] * float(deriv[j, s])
                            acc = term if acc is None else acc + term
                    total[i, j] = total[i, j] - scale_y * acc
            trace = sides_of(q, flip_x, flip_y)
            jump = {0: [], 1: [], 2: [], 3: []}
            for t in range(SIDE):
                pace = turn_x * speed_x[0][t]
                own_low, give_low = -(pace + 1.0) * trace[0][t], (1.0 - pace) * trace[0][t]
                pace = turn_x * speed_x[1][t]
                own_high, give_high = (pace - 1.0) * trace[1][t], (1.0 + pace) * trace[1][t]
                from_low = pltpu.roll(give_high, 1, 0)
                from_high = pltpu.roll(give_low, SUB - 1, 0)
                for line in range(lines):
                    at = pl.ds(t * lines + line, 1)
                    from_low = jnp.where(
                        slot == line * cols, lower_ref[tile, var, at, :], from_low
                    )
                    from_high = jnp.where(
                        slot == (line + 1) * cols - 1, upper_ref[tile, var, at, :], from_high
                    )
                jump[0].append(weight_x * (own_low + from_low))
                jump[1].append(weight_x * (own_high + from_high))
                pace = turn_y * speed_y[2][t]
                own_low, give_low = -(pace + 1.0) * trace[2][t], (1.0 - pace) * trace[2][t]
                pace = turn_y * speed_y[3][t]
                own_high, give_high = (pace - 1.0) * trace[3][t], (1.0 + pace) * trace[3][t]
                from_low = pltpu.roll(give_high, cols, 0)
                from_high = pltpu.roll(give_low, SUB - cols, 0)
                at = pl.ds(t * cols, cols)
                below = jnp.concatenate([prev_ref[tile, var, at, :]] * lines, axis=0)
                above = jnp.concatenate([next_ref[tile, var, at, :]] * lines, axis=0)
                below = jnp.where(at_floor, mirror * give_low, below)
                above = jnp.where(at_roof, mirror * give_high, above)
                from_low = jnp.where(first_line, below, from_low)
                from_high = jnp.where(last_line, above, from_high)
                jump[2].append(weight_y * (own_low + from_low))
                jump[3].append(weight_y * (own_high + from_high))

            def back(one, two, flip, flip_along):
                mixed = [jnp.where(flip, two[t], one[t]) for t in range(SIDE)]
                return [
                    jnp.where(flip_along, mixed[SIDE - 1 - t], mixed[t]) for t in range(SIDE)
                ]

            side = back(jump[0], jump[1], flip_x, flip_y)
            for t in range(SIDE):
                total[0, t] = total[0, t] + side[t]
            side = back(jump[1], jump[0], flip_x, flip_y)
            for t in range(SIDE):
                total[5, t] = total[5, t] + side[t]
            side = back(jump[2], jump[3], flip_y, flip_x)
            for t in range(SIDE):
                total[t, 0] = total[t, 0] + side[t]
            side = back(jump[3], jump[2], flip_y, flip_x)
            for t in range(SIDE):
                total[t, 5] = total[t, 5] + side[t]
            for i in range(SIDE):
                for j in range(SIDE):
                    at = pl.ds((SIDE * i + j) * SUB, SUB)
                    rate_ref[var, at, pl.ds(tile * LANES, LANES)] = total[i, j]
                    rate_ref[var, at, pl.ds(count + tile * LANES, LANES)] = q(i, j) * reader(2)(
                        i, j
                    )

    tables = []
    for ref in (high_ref, low_ref):
        tables.append(
            jnp.concatenate([ref[pl.ds((me ^ k) * modes, modes), :] for k in range(span)], axis=0)
        )
    gains = []
    for var in range(num_vars):
        high, low = split(rate_ref[var])
        gains.append(mm_nt(high, tables[0]) + mm_nt(low, tables[0]) + mm_nt(high, tables[1]))
    for group in range(span // 4):
        at = slice(group * LANES, (group + 1) * LANES)
        for q, part in enumerate(regroup([gain[:, at] for gain in gains], lane)):
            outs[4 * group + q][...] = part


def gather_kernel(dims, where_ref, pick_ref, state_ref, *refs):
    rows, cols, share, span, modes = dims
    takes = refs[:span]
    out_ref, flat = refs[span:]
    elems = rows * cols
    count = span * modes
    turned = pick_ref[...].T[:elems]
    pick = jnp.concatenate([turned] * (LANES // elems), axis=1).astype(jnp.bfloat16)
    for node in range(NODES):
        part = jnp.concatenate([take[pl.ds(node * share, share), :] for take in takes], axis=0)
        high, low = split(part)
        flat[pl.ds(node, elems, stride=NODES), :] = mm(pick, jnp.concatenate([high, low], axis=0))
    index = where_ref[0] * modes + lax.broadcasted_iota(jnp.int32, (LANES, 1), 0) % modes
    wave = jnp.where(index == 1, count // 2, index // 2).astype(jnp.float32)
    damping = 1.0 / (1.0 + TIME_STEP * VISCOSITY * wave * wave)
    for block in range(elems * NODES // LANES):
        at = pl.ds(block * LANES, LANES)
        out_ref[:, at] = state_ref[:, at] * damping + flat[at, :].T


def smem():
    return pl.BlockSpec(memory_space=pltpu.SMEM)


def vmem(count):
    return [pl.BlockSpec(memory_space=pltpu.VMEM)] * count


PARAMS = pltpu.CompilerParams(vmem_limit_bytes=24 * 1024 * 1024)


def exchange(blocks, span):
    order = sorted(range(1, span), key=lambda k: -bin(k).count("1"))
    taken = {0: blocks[0]}
    for k in order:
        taken[k] = lax.ppermute(blocks[k], "span", [(s, s ^ k) for s in range(span)])
    return [taken[k] for k in range(span)]


def ordered_body(state, metric, neighbour, orient, wall, rim):
    num_vars, modes, flat_size = state.shape
    elems = flat_size // NODES
    span = lax.axis_size("span")
    groups = lax.axis_size("elem")
    share = elems // span
    rows = rim.shape[1]
    cols = elems // rows
    count = modes * span
    tiles = count // LANES
    lines = share // cols
    me = lax.axis_index("span").reshape(1)
    flat_state = state.reshape(num_vars * modes, flat_size)
    f32 = jnp.float32
    block = jax.ShapeDtypeStruct((NODES * share, LANES), f32)

    first = pl.pallas_call(
        functools.partial(spread_kernel, (rows, cols, share, span)),
        out_shape=[block] * span
        + [
            jax.ShapeDtypeStruct((elems, LANES), f32),
            jax.ShapeDtypeStruct((4, elems, LANES), f32),
        ],
        in_specs=[smem()] * 5 + vmem(1),
        out_specs=vmem(span + 2),
        scratch_shapes=[pltpu.VMEM((flat_size, LANES), f32)],
        compiler_params=PARAMS,
        name="spread",
    )(me, neighbour.T, wall.T, rim, metric, flat_state)
    takes = exchange(first[:span], span)
    pick, facts = first[span:]
    facts = facts[:, :share]

    dims = (cols, share, span, num_vars, modes)
    line_shape = jax.ShapeDtypeStruct((tiles, num_vars, SIDE * lines, LANES), f32)
    row_shape = jax.ShapeDtypeStruct((tiles, num_vars, SIDE * cols, LANES), f32)
    phys, up, down, ahead, behind = pl.pallas_call(
        functools.partial(planes_kernel, dims),
        out_shape=[
            jax.ShapeDtypeStruct((tiles, num_vars, NODES * share, LANES), f32),
            line_shape,
            line_shape,
            row_shape,
            row_shape,
        ],
        in_specs=[smem()] + vmem(3 + span),
        out_specs=vmem(5),
        compiler_params=PARAMS,
        name="planes",
    )(me, facts, *[jnp.asarray(t) for t in forward_tables(count)], *takes)
    lower = lax.ppermute(up, "elem", [(g, (g + 1) % groups) for g in range(groups)])
    upper = lax.ppermute(down, "elem", [(g, (g - 1) % groups) for g in range(groups)])
    prev = lax.ppermute(ahead, "span", [(s, s + 1) for s in range(span - 1)])
    after = lax.ppermute(behind, "span", [(s + 1, s) for s in range(span - 1)])

    gains = pl.pallas_call(
        functools.partial(rates_kernel, dims),
        out_shape=[block] * span,
        in_specs=[smem()] + vmem(8),
        out_specs=vmem(span),
        scratch_shapes=[pltpu.VMEM((num_vars, NODES * share, 2 * count), f32)],
        compiler_params=PARAMS,
        name="rates",
    )(
        me, facts, *[jnp.asarray(t) for t in backward_tables(count)], phys, lower, upper, prev,
        after,
    )
    takes = exchange(gains, span)

    out = pl.pallas_call(
        functools.partial(gather_kernel, (rows, cols, share, span, modes)),
        out_shape=jax.ShapeDtypeStruct((num_vars * modes, flat_size), f32),
        in_specs=[smem()] + vmem(2 + span),
        out_specs=pl.BlockSpec(memory_space=pltpu.VMEM),
        scratch_shapes=[pltpu.VMEM((flat_size, LANES), f32)],
        compiler_params=PARAMS,
        name="collect",
    )(me, pick, flat_state, *takes)
    return out.reshape(state.shape)


def from_behind(value, axis, steps):
    count = lax.axis_size(axis)
    pairs = [(source, (source + steps) % count) for source in range(count)]
    return lax.ppermute(value, axis, pairs)


def gll_tables():
    near_point = math.sqrt(1.0 / 3.0 - 2.0 * math.sqrt(7.0) / 21.0)
    far_point = math.sqrt(1.0 / 3.0 + 2.0 * math.sqrt(7.0) / 21.0)
    points = np.array([-1.0, -far_point, -near_point, near_point, far_point, 1.0])
    weights = np.array(
        [
            1.0
            / np.prod([points[column] - points[second] for second in range(6) if second != column])
            for column in range(6)
        ]
    )
    deriv = np.zeros((6, 6))
    for target in range(6):
        for source in range(6):
            if source != target:
                deriv[target, source] = (
                    weights[source] / weights[target] / (points[target] - points[source])
                )
        deriv[target, target] = -np.sum(deriv[target])
    identity = np.eye(6)
    along_x = np.kron(deriv, identity)
    along_y = np.kron(identity, deriv)
    edge_nodes = np.array(
        [
            [offset for offset in range(6)],
            [30 + offset for offset in range(6)],
            [6 * offset for offset in range(6)],
            [6 * offset + 5 for offset in range(6)],
        ]
    ).reshape(-1)
    lifting = np.zeros((36, 24))
    lifting[edge_nodes, np.arange(24)] = 1.0
    return (
        jnp.asarray(along_x, jnp.float32),
        jnp.asarray(along_y, jnp.float32),
        edge_nodes,
        jnp.asarray(lifting, jnp.float32),
    )


def spanwise_basis(count):
    mode_index = jnp.arange(count, dtype=jnp.int32)
    planes = jnp.arange(count, dtype=jnp.int32)
    phase = mode_index[:, None] // 2 * planes[None, :] % count
    phase_angle = phase.astype(jnp.float32) * (2.0 * math.pi / count)
    odd_rows = (mode_index % 2 == 1)[:, None]
    basis_table = jnp.where(odd_rows, jnp.sin(phase_angle), jnp.cos(phase_angle)) * math.sqrt(
        2.0 / count
    )
    alternate = (1 - 2 * (planes % 2)).astype(jnp.float32) / math.sqrt(count)
    constant = jnp.ones((count,), jnp.float32) / math.sqrt(count)
    basis_table = jnp.where(mode_index[:, None] == 0, constant[None, :], basis_table)
    basis_table = jnp.where(mode_index[:, None] == 1, alternate[None, :], basis_table)
    return basis_table


def spanwise_derivative(modal):
    shape_in = modal.shape
    paired = modal.reshape(shape_in[0], shape_in[1] // 2, 2, shape_in[2])
    wavenumber = jnp.arange(shape_in[1] // 2, dtype=jnp.int32).astype(jnp.float32)[None, :, None]
    return jnp.stack([wavenumber * paired[:, :, 1], -wavenumber * paired[:, :, 0]], axis=2).reshape(
        shape_in
    )


def planar_terms(flux_x, flux_y, metric_part):
    along_x, along_y, edge_nodes, lifting = gll_tables()
    scale_x = metric_part[0][:, None]
    scale_y = metric_part[1][:, None]
    grad_x = jnp.einsum("pq,vmeq->vmep", along_x, flux_x, precision=HIGHEST)
    grad_y = jnp.einsum("pq,vmeq->vmep", along_y, flux_y, precision=HIGHEST)
    planar = scale_x * grad_x + scale_y * grad_y
    sign_x = jnp.sign(scale_x)
    sign_y = jnp.sign(scale_y)
    edge_flux = jnp.concatenate(
        [
            -sign_x * flux_x[:, :, :, edge_nodes[0:6]],
            sign_x * flux_x[:, :, :, edge_nodes[6:12]],
            -sign_y * flux_y[:, :, :, edge_nodes[12:18]],
            sign_y * flux_y[:, :, :, edge_nodes[18:24]],
        ],
        axis=3,
    )
    return (planar, edge_flux)


def node_major(flat, num_vars, local_modes, nodes, local_elems):
    return jnp.transpose(flat.reshape(num_vars, local_modes, local_elems, nodes), (0, 1, 3, 2))


def trace_pool(traces):
    shape_in = traces.shape
    return (
        traces.reshape(shape_in[0], shape_in[1], 4, 6, shape_in[3])
        .transpose(0, 1, 3, 4, 2)
        .reshape(shape_in[0], shape_in[1], 6, 4 * shape_in[3])
    )


def own_pools(state_local, normal_flux):
    edge_nodes = gll_tables()[2]
    return (trace_pool(state_local[:, :, edge_nodes, :]), trace_pool(normal_flux))


def update(
    state_local,
    divergence,
    own_q,
    own_flux,
    from_lower,
    from_upper,
    neighbour,
    orient,
    wall,
    metric_local,
    first_mode,
    total_modes,
):
    lifting = gll_tables()[3]
    num_vars, modes_here, num_nodes, count = state_local.shape
    pool_q = jnp.concatenate([own_q, from_lower[0], from_upper[0]], axis=3)
    pool_flux = jnp.concatenate([own_flux, from_lower[1], from_upper[1]], axis=3)
    flat_index = neighbour.reshape(-1)
    other_q = jnp.take(pool_q, flat_index, axis=3)
    other_flux = jnp.take(pool_flux, flat_index, axis=3)
    flipped = orient.reshape(-1) == 1
    other_q = jnp.where(flipped, other_q[:, :, ::-1, :], other_q)
    other_flux = jnp.where(flipped, other_flux[:, :, ::-1, :], other_flux)
    mirror = jnp.array([-1.0, -1.0, -1.0, 1.0], jnp.float32).reshape(4, 1, 1, 1)
    walled = wall.reshape(-1) == 1
    other_q = jnp.where(walled, mirror * own_q, other_q)
    other_flux = jnp.where(walled, mirror * own_flux, other_flux)
    magnitude = (
        jnp.abs(
            jnp.stack([metric_local[0], metric_local[0], metric_local[1], metric_local[1]], axis=1)
        ).reshape(-1)
        * 15.0
    )
    surface_jump = magnitude * (0.5 * (own_flux + other_flux) - 0.5 * PENALTY * (own_q - other_q))
    unpooled = (
        surface_jump.reshape(num_vars, modes_here, 6, count, 4)
        .transpose(0, 1, 4, 2, 3)
        .reshape(num_vars, modes_here, 24, count)
    )
    surface = jnp.einsum("pq,vmqe->vmpe", lifting, unpooled, precision=HIGHEST)
    mode_index = first_mode + jnp.arange(modes_here, dtype=jnp.int32)
    wavenumber = jnp.where(mode_index == 1, total_modes // 2, mode_index // 2).astype(jnp.float32)
    damping = 1.0 + TIME_STEP * VISCOSITY * wavenumber * wavenumber
    return (state_local + TIME_STEP * (surface - divergence)) / damping[None, :, None, None]


def plain_body(state, metric, neighbour, orient, wall, rim):
    num_vars, local_modes, flat_size = state.shape
    num_nodes = 36
    local_elems = flat_size // num_nodes
    span_size = lax.axis_size("span")
    total_modes = local_modes * span_size
    share = local_elems // span_size
    state_nodes = node_major(state, num_vars, local_modes, num_nodes, local_elems)
    planes_in = lax.all_to_all(state, "span", split_axis=2, concat_axis=1, tiled=True)
    basis_table = spanwise_basis(total_modes)
    physical = jnp.einsum("mn,vmk->vnk", basis_table, planes_in, precision=HIGHEST)
    metric_part = lax.dynamic_slice_in_dim(metric, lax.axis_index("span") * share, share, axis=1)
    shape_here = (num_vars, total_modes, share, num_nodes)
    planar_div, edge_flux = planar_terms(
        (physical[0:1] * physical).reshape(shape_here),
        (physical[1:2] * physical).reshape(shape_here),
        metric_part,
    )
    volume_fields = jnp.concatenate(
        [planar_div.reshape(num_vars, total_modes, share * num_nodes), physical[2:3] * physical],
        axis=0,
    )
    volume_modal = jnp.einsum("mn,vnk->vmk", basis_table, volume_fields, precision=HIGHEST)
    edge_modal = jnp.einsum(
        "mn,vnk->vmk",
        basis_table,
        edge_flux.reshape(num_vars, total_modes, share * 24),
        precision=HIGHEST,
    )
    combined = volume_modal[0:4] + spanwise_derivative(volume_modal[4:8])
    div_flat, flux_flat = (
        lax.all_to_all(combined, "span", split_axis=1, concat_axis=2, tiled=True),
        lax.all_to_all(edge_modal, "span", split_axis=1, concat_axis=2, tiled=True),
    )
    divergence = node_major(div_flat, num_vars, local_modes, num_nodes, local_elems)
    normal_flux = node_major(flux_flat, num_vars, local_modes, 24, local_elems)
    own_q, own_flux = own_pools(state_nodes, normal_flux)
    upper_rim = jnp.stack([jnp.take(own_q, rim[1], axis=3), jnp.take(own_flux, rim[1], axis=3)])
    lower_rim = jnp.stack([jnp.take(own_q, rim[0], axis=3), jnp.take(own_flux, rim[0], axis=3)])
    from_lower = from_behind(upper_rim, "elem", 1)
    from_upper = from_behind(lower_rim, "elem", -1)
    first_mode = lax.axis_index("span") * local_modes
    result = update(
        state_nodes,
        divergence,
        own_q,
        own_flux,
        from_lower,
        from_upper,
        neighbour,
        orient,
        wall,
        metric,
        first_mode,
        total_modes,
    )
    return jnp.transpose(result, (0, 1, 3, 2)).reshape(num_vars, local_modes, flat_size)


def body(state, metric, neighbour, orient, wall, rim):
    num_vars, modes, flat_size = state.shape
    span = lax.axis_size("span")
    elems = flat_size // NODES
    rows = rim.shape[1]
    fits = (
        num_vars * modes == LANES
        and modes * 4 == LANES
        and span % 4 == 0
        and span & (span - 1) == 0
        and LANES % elems == 0
        and elems == SUB * span
        and elems % rows == 0
        and SUB % (elems // rows) == 0
    )
    chosen = ordered_body if fits else plain_body
    return chosen(state, metric, neighbour, orient, wall, rim)


def solution(mesh):
    placed = (
        P(None, "span", "elem"),
        P(None, "elem"),
        P("elem", None),
        P("elem", None),
        P("elem", None),
        P(None, "elem"),
    )
    return jax.shard_map(
        body, mesh=mesh, in_specs=placed, out_specs=P(None, "span", "elem"), check_vma=False
    )
```

```python
import functools
import math

import jax
import jax.numpy as jnp
import numpy as np
from jax import lax
from jax.experimental import pallas as pl
from jax.experimental.pallas import tpu as pltpu
from jax.sharding import PartitionSpec as P


TIME_STEP = 0.001
VISCOSITY = 0.02
PENALTY = 1.0
HIGHEST = lax.Precision.HIGHEST
SIDE = 6
NODES = SIDE * SIDE
LANES = 128
SUB = 8
CHUNK = 3 * LANES
RIM_NODES = [p for p in range(NODES) if p // SIDE in (0, 5) or p % SIDE in (0, 5)]
CORE_NODES = [p for p in range(NODES) if p not in RIM_NODES]
PARTS = (RIM_NODES, CORE_NODES)


def gll_matrix():
    near_point = math.sqrt(1.0 / 3.0 - 2.0 * math.sqrt(7.0) / 21.0)
    far_point = math.sqrt(1.0 / 3.0 + 2.0 * math.sqrt(7.0) / 21.0)
    points = np.array([-1.0, -far_point, -near_point, near_point, far_point, 1.0])
    weights = np.array(
        [
            1.0
            / np.prod([points[column] - points[second] for second in range(6) if second != column])
            for column in range(6)
        ]
    )
    deriv = np.zeros((6, 6))
    for target in range(6):
        for source in range(6):
            if source != target:
                deriv[target, source] = (
                    weights[source] / weights[target] / (points[target] - points[source])
                )
        deriv[target, target] = -np.sum(deriv[target])
    return deriv


def basis_matrix(count):
    mode = np.arange(count)[:, None]
    plane = np.arange(count)[None, :]
    angle = (mode // 2 * plane % count) * (2.0 * math.pi / count)
    table = np.where(mode % 2 == 1, np.sin(angle), np.cos(angle)) * math.sqrt(2.0 / count)
    table = np.where(mode == 0, 1.0 / math.sqrt(count), table)
    return np.where(mode == 1, (1.0 - 2.0 * (plane % 2)) / math.sqrt(count), table)


def halves(table):
    table = np.asarray(table, np.float32)
    high = table.astype(jnp.bfloat16)
    low = (table - high.astype(np.float32)).astype(jnp.bfloat16)
    return high, low


def forward_tables(count):
    return halves(basis_matrix(count))


def backward_tables(count):
    basis = basis_matrix(count)
    wave = np.arange(count) // 2
    swapped = np.empty_like(basis)
    swapped[0::2] = wave[0::2, None] * basis[1::2]
    swapped[1::2] = -wave[1::2, None] * basis[0::2]
    damp_wave = np.where(np.arange(count) == 1, count // 2, wave).astype(np.float64)
    factor = TIME_STEP / (1.0 + TIME_STEP * VISCOSITY * damp_wave * damp_wave)
    return halves(factor[:, None] * np.concatenate([basis, -swapped], axis=1))


def split(value):
    high = value.astype(jnp.bfloat16)
    low = (value - high.astype(jnp.float32)).astype(jnp.bfloat16)
    return high, low


def mm(a, b):
    return lax.dot_general(a, b, (((1,), (0,)), ((), ())), preferred_element_type=jnp.float32)


def mm_nt(a, b):
    return lax.dot_general(a, b, (((1,), (1,)), ((), ())), preferred_element_type=jnp.float32)


def regroup(parts, lane):
    quarter = LANES // 4
    low_half = lane < 2 * quarter
    rolled = [pltpu.roll(part, 2 * quarter, 1) for part in parts]
    first = [
        jnp.where(low_half, parts[0], rolled[2]),
        jnp.where(low_half, parts[1], rolled[3]),
        jnp.where(low_half, rolled[0], parts[2]),
        jnp.where(low_half, rolled[1], parts[3]),
    ]
    even = lane // quarter % 2 == 0
    out = []
    for pair in (0, 2):
        a, b = first[pair], first[pair + 1]
        out.append(jnp.where(even, a, pltpu.roll(b, quarter, 1)))
        out.append(jnp.where(even, pltpu.roll(a, LANES - quarter, 1), b))
    return out


def spread_kernel(dims, where_ref, near_any, wall_any, rim_any, metric_any, state_any, *refs):
    rows, cols, share, span = dims
    sends = [refs[:span], refs[span : 2 * span]]
    pick_ref, facts_ref = refs[2 * span : 2 * span + 2]
    halo_ref, bends_ref, near_ref, wall_ref, rim_ref, metric_ref, state_ref, flat, sems = refs[2 * span + 2 :]
    me = where_ref[0]
    elems = rows * cols
    width = elems * NODES
    small = [
        pltpu.make_async_copy(source, target, sems.at[at])
        for at, (source, target) in enumerate(
            (
                (near_any, near_ref),
                (wall_any, wall_ref),
                (rim_any, rim_ref),
                (metric_any, metric_ref),
            )
        )
    ]
    large = [
        pltpu.make_async_copy(
            state_any.at[:, pl.ds(at, CHUNK)],
            state_ref.at[:, pl.ds(at, CHUNK)],
            sems.at[len(small) + at // CHUNK],
        )
        for at in range(0, width, CHUNK)
    ]
    for copy in small + large:
        copy.start()
    for copy in small:
        copy.wait()
    lane = lax.broadcasted_iota(jnp.int32, (1, LANES), 1) % elems
    lines = share // cols
    halo_ref[...] = jnp.zeros_like(halo_ref)
    bends_ref[...] = jnp.zeros_like(bends_ref)
    before = None
    for row in range(rows):
        cell = rim_ref[0, row] >> 2
        face = rim_ref[0, row] & 1
        here = []
        for col in range(cols):
            if row == 0:
                flip_y = wall_ref[3, cell]
            else:
                flip_y = jnp.where(near_ref[3, cell] >> 2 == before[col], 1, 0)
            here.append(cell)
            place = row * cols + col
            at = (place // share ^ me) * share + place % share
            chosen = jnp.where(lane == cell, 1.0, 0.0)
            pick_ref[pl.ds(at, 1), :] = chosen
            if row % lines == lines - 1 and row + 1 < rows:
                under = ((row // lines + 1) ^ me) * share + col
                halo_ref[pl.ds(under, 1), :] = chosen
                for kind, bend in enumerate((face, 1 - flip_y)):
                    bends_ref[kind, pl.ds(under, 1), :] = jnp.full((1, LANES), bend, jnp.int32)
            if row % lines == 0 and row > 0:
                over = ((row // lines - 1) ^ me) * share + cols + col
                halo_ref[pl.ds(over, 1), :] = chosen
                for kind, bend in enumerate((face, flip_y)):
                    bends_ref[kind, pl.ds(over, 1), :] = jnp.full((1, LANES), bend, jnp.int32)
            facts = (
                metric_ref[0, cell],
                metric_ref[1, cell],
                face.astype(jnp.float32),
                flip_y.astype(jnp.float32),
            )

            @pl.when(at < share)
            def _(at=at, facts=facts):
                for kind, fact in enumerate(facts):
                    facts_ref[kind, pl.ds(at, 1), :] = jnp.full((1, LANES), fact, jnp.float32)

            if col + 1 < cols:
                step = near_ref[face ^ 1, cell]
                cell = step >> 2
                face = step & 1
        before = here
    for at in range(0, width, LANES):
        if at % CHUNK == 0:
            large[at // CHUNK].wait()
        flat[pl.ds(at, LANES), :] = state_ref[:, pl.ds(at, LANES)].T
    pick = pick_ref[...].astype(jnp.bfloat16)
    both = jnp.concatenate([pick, halo_ref[...].astype(jnp.bfloat16)], axis=0)
    edge = {}
    for nodes, outs in zip(PARTS, sends):
        for at, node in enumerate(nodes):
            high, low = split(flat[pl.ds(node, elems, stride=NODES), :])
            wanted = node % SIDE in (0, 5)
            moved = mm(both if wanted else pick, jnp.concatenate([high, low], axis=0))
            if wanted:
                edge[divmod(node, SIDE)] = moved[elems:]
            for step in range(span):
                outs[step][pl.ds(at * share, share), :] = moved[step * share : (step + 1) * share]
    bend_x = bends_ref[0] == 1
    bend_y = bends_ref[1] == 1
    trace = [jnp.where(bend_y, edge[t, 5], edge[t, 0]) for t in range(SIDE)]
    for t in range(SIDE):
        moved = jnp.where(bend_x, trace[SIDE - 1 - t], trace[t])
        at = pl.ds((len(RIM_NODES) + t) * share, share)
        for step in range(span):
            sends[0][step][at, :] = moved[step * share : (step + 1) * share]


def along(trace, flip):
    return [jnp.where(flip, trace[SIDE - 1 - t], trace[t]) for t in range(SIDE)]


def sides_x(value, flip_x, flip_y):
    low = [jnp.where(flip_x, value(5, t), value(0, t)) for t in range(SIDE)]
    high = [jnp.where(flip_x, value(0, t), value(5, t)) for t in range(SIDE)]
    return along(low, flip_y), along(high, flip_y)


def sides_y(value, flip_x, flip_y):
    low = [jnp.where(flip_y, value(t, 5), value(t, 0)) for t in range(SIDE)]
    high = [jnp.where(flip_y, value(t, 0), value(t, 5)) for t in range(SIDE)]
    return along(low, flip_x), along(high, flip_x)


def rim_reader(ref, tile, var):
    return lambda i, j: ref[tile, var, pl.ds(RIM_NODES.index(SIDE * i + j) * SUB, SUB), :]


def back(one, two, flip, flip_along):
    return along([jnp.where(flip, two[t], one[t]) for t in range(SIDE)], flip_along)


def sign(value):
    return jnp.where(value < 0.0, -1.0, 1.0)


def to_planes(dims, me, high_ref, low_ref, takes, phys_ref):
    _, _, span, num_vars, modes = dims
    lane = lax.broadcasted_iota(jnp.int32, (1, LANES), 1)
    tables = []
    for ref in (high_ref, low_ref):
        tables.append(
            jnp.concatenate([ref[pl.ds((me ^ k) * modes, modes), :] for k in range(span)], axis=0)
        )
    pieces = []
    for group in range(span // 4):
        pieces.append(regroup([takes[4 * group + q][...] for q in range(4)], lane))
    for var in range(num_vars):
        high, low = split(jnp.concatenate([piece[var] for piece in pieces], axis=1))
        planes = mm(high, tables[0]) + mm(low, tables[0]) + mm(high, tables[1])
        for tile in range(span * modes // LANES):
            phys_ref[tile, var] = planes[:, tile * LANES : (tile + 1) * LANES]


def planes_kernel(dims, where_ref, facts_ref, high_ref, low_ref, *refs):
    cols, share, span, num_vars, modes = dims
    takes = refs[:span]
    phys_ref, one_ref, two_ref = refs[span:]
    to_planes(dims, where_ref[0], high_ref, low_ref, takes, phys_ref)
    odd = where_ref[1] == 1
    lines = share // cols
    flip_x = facts_ref[2] > 0.5
    flip_y = facts_ref[3] > 0.5
    turn_x = sign(facts_ref[0]) * (1.0 - 2.0 * facts_ref[2])
    for tile in range(span * modes // LANES):
        speed = sides_x(rim_reader(phys_ref, tile, 0), flip_x, flip_y)
        for var in range(num_vars):
            trace = sides_x(rim_reader(phys_ref, tile, var), flip_x, flip_y)
            for t in range(SIDE):
                low_x = (1.0 - turn_x * speed[0][t]) * trace[0][t]
                high_x = (1.0 + turn_x * speed[1][t]) * trace[1][t]
                for line in range(lines):
                    at = pl.ds(t * lines + line, 1)
                    up = high_x[(line + 1) * cols - 1 : (line + 1) * cols]
                    down = low_x[line * cols : line * cols + 1]
                    one_ref[tile, var, at, :] = jnp.where(odd, down, up)
                    two_ref[tile, var, at, :] = jnp.where(odd, up, down)


def to_modes(dims, me, high_ref, low_ref, rates):
    _, _, span, _, modes = dims
    lane = lax.broadcasted_iota(jnp.int32, (1, LANES), 1)
    tables = []
    for ref in (high_ref, low_ref):
        tables.append(
            jnp.concatenate([ref[pl.ds((me ^ k) * modes, modes), :] for k in range(span)], axis=0)
        )
    gains = []
    for rate in rates:
        high, low = split(rate)
        gains.append(mm_nt(high, tables[0]) + mm_nt(low, tables[0]) + mm_nt(high, tables[1]))
    out = []
    for group in range(span // 4):
        at = slice(group * LANES, (group + 1) * LANES)
        out += regroup([gain[:, at] for gain in gains], lane)
    return out


def rates_kernel(
    dims, where_ref, facts_ref, there_high, there_low, high_ref, low_ref, phys_ref, *refs
):
    cols, _, span, num_vars, modes = dims
    mid_ref, edge_ref, core_ref, rate_ref = refs[span:]
    me = where_ref[0]
    to_planes(dims, me, there_high, there_low, refs[:span], core_ref)
    count = span * modes
    deriv = np.asarray(gll_matrix(), np.float32)
    slot = lax.broadcasted_iota(jnp.int32, (SUB, LANES), 0)
    flip_x = facts_ref[2] > 0.5
    flip_y = facts_ref[3] > 0.5
    scale_x = facts_ref[0]
    scale_y = facts_ref[1]
    turn_x = sign(scale_x) * (1.0 - 2.0 * facts_ref[2])
    turn_y = sign(scale_y) * (1.0 - 2.0 * facts_ref[3])
    weight_x = 7.5 * jnp.abs(scale_x)
    weight_y = 7.5 * jnp.abs(scale_y)
    first_col = slot % cols == 0
    last_col = slot % cols == cols - 1
    first_line = slot < cols
    turn_halo = jnp.where(first_line, turn_y, -turn_y)
    floor = jnp.logical_and(first_line, me == 0)
    roof = jnp.logical_and(jnp.logical_not(first_line), me == span - 1)

    for tile in range(count // LANES):

        def reader(var, tile=tile):
            def read(i, j):
                node = SIDE * i + j
                ref = phys_ref if node in RIM_NODES else core_ref
                nodes = RIM_NODES if node in RIM_NODES else CORE_NODES
                return ref[tile, var, pl.ds(nodes.index(node) * SUB, SUB), :]

            return read

        def halo(var, t, tile=tile):
            return phys_ref[tile, var, pl.ds((len(RIM_NODES) + t) * SUB, SUB), :]

        speed_x = sides_x(reader(0), flip_x, flip_y)
        speed_y = sides_y(reader(1), flip_x, flip_y)
        pace_x = [[turn_x * speed for speed in side] for side in speed_x]
        pace_y = [[turn_y * speed for speed in side] for side in speed_y]
        for var in range(num_vars):
            q = reader(var)
            mirror = 1.0 if var == num_vars - 1 else -1.0
            total = {}
            for j in range(SIDE):
                flux = [q(i, j) * reader(0)(i, j) for i in range(SIDE)]
                for i in range(SIDE):
                    acc = None
                    for s in range(SIDE):
                        if abs(deriv[i, s]) > 1e-6:
                            term = flux[s] * float(deriv[i, s])
                            acc = term if acc is None else acc + term
                    total[i, j] = -scale_x * acc
            for i in range(SIDE):
                flux = [q(i, j) * reader(1)(i, j) for j in range(SIDE)]
                for j in range(SIDE):
                    acc = None
                    for s in range(SIDE):
                        if abs(deriv[j, s]) > 1e-6:
                            term = flux[s] * float(deriv[j, s])
                            acc = term if acc is None else acc + term
                    total[i, j] = total[i, j] - scale_y * acc
            trace = sides_x(q, flip_x, flip_y)
            low, high = [], []
            for t in range(SIDE):
                pace, value = pace_x[0][t], trace[0][t]
                own_low, give_low = -(pace + 1.0) * value, (1.0 - pace) * value
                pace, value = pace_x[1][t], trace[1][t]
                own_high, give_high = (pace - 1.0) * value, (1.0 + pace) * value
                from_low = jnp.where(first_col, 0.0, pltpu.roll(give_high, 1, 0))
                from_high = jnp.where(last_col, 0.0, pltpu.roll(give_low, SUB - 1, 0))
                low.append(weight_x * (own_low + from_low))
                high.append(weight_x * (own_high + from_high))
            for i, side in (
                (0, back(low, high, flip_x, flip_y)),
                (5, back(high, low, flip_x, flip_y)),
            ):
                for t in range(SIDE):
                    total[i, t] = total[i, t] + side[t]
            trace = sides_y(q, flip_x, flip_y)
            low, high = [], []
            for t in range(SIDE):
                pace, value = pace_y[0][t], trace[0][t]
                own_low, give_low = -(pace + 1.0) * value, (1.0 - pace) * value
                pace, value = pace_y[1][t], trace[1][t]
                own_high, give_high = (pace - 1.0) * value, (1.0 + pace) * value
                outside = (1.0 + turn_halo * halo(1, t)) * halo(var, t)
                outside = jnp.where(floor, mirror * give_low, outside)
                outside = jnp.where(roof, mirror * give_high, outside)
                from_low = jnp.where(first_line, outside, pltpu.roll(give_high, cols, 0))
                from_high = jnp.where(first_line, pltpu.roll(give_low, SUB - cols, 0), outside)
                low.append(weight_y * (own_low + from_low))
                high.append(weight_y * (own_high + from_high))
            for j, side in (
                (0, back(low, high, flip_y, flip_x)),
                (5, back(high, low, flip_y, flip_x)),
            ):
                for t in range(SIDE):
                    total[t, j] = total[t, j] + side[t]
            for i in range(SIDE):
                for j in range(SIDE):
                    if i in (0, 5):
                        ref, node = edge_ref, i // 5 * SIDE + j
                    else:
                        ref, node = rate_ref, SIDE * (i - 1) + j
                    at = pl.ds(node * SUB, SUB)
                    ref[var, at, pl.ds(tile * LANES, LANES)] = total[i, j]
                    ref[var, at, pl.ds(count + tile * LANES, LANES)] = q(i, j) * reader(2)(i, j)
    parts = to_modes(dims, me, high_ref, low_ref, [rate_ref[var] for var in range(num_vars)])
    for k in range(span):
        mid_ref[k] = parts[k]


def edges_kernel(
    dims, where_ref, facts_ref, high_ref, low_ref, mid_ref, edge_ref, one_ref, two_ref, *refs
):
    cols, share, span, num_vars, modes = dims
    outs = refs[:span]
    rate_ref = refs[span]
    count = span * modes
    lines = share // cols
    odd = where_ref[1] == 1
    slot = lax.broadcasted_iota(jnp.int32, (SUB, LANES), 0)
    flip_x = facts_ref[2] > 0.5
    flip_y = facts_ref[3] > 0.5
    weight = 7.5 * jnp.abs(facts_ref[0])
    for tile in range(count // LANES):
        for var in range(num_vars):
            low, high = [], []
            for t in range(SIDE):
                below, above = jnp.zeros((SUB, LANES)), jnp.zeros((SUB, LANES))
                for line in range(lines):
                    at = pl.ds(t * lines + line, 1)
                    one, two = one_ref[tile, var, at, :], two_ref[tile, var, at, :]
                    below = jnp.where(slot == line * cols, jnp.where(odd, one, two), below)
                    above = jnp.where(
                        slot == (line + 1) * cols - 1, jnp.where(odd, two, one), above
                    )
                low.append(weight * below)
                high.append(weight * above)
            for i, side in enumerate(
                (back(low, high, flip_x, flip_y), back(high, low, flip_x, flip_y))
            ):
                for t in range(SIDE):
                    at = (pl.ds((i * SIDE + t) * SUB, SUB), pl.ds(tile * LANES, LANES))
                    rate_ref[var, at[0], at[1]] = edge_ref[var, at[0], at[1]] + side[t]
    rates = [
        jnp.concatenate([rate_ref[var], edge_ref[var, :, count:]], axis=1)
        for var in range(num_vars)
    ]
    parts = to_modes(dims, where_ref[0], high_ref, low_ref, rates)
    half = SIDE * share
    for k in range(span):
        outs[k][:half] = parts[k][:half]
        outs[k][half : (NODES - SIDE) * share] = mid_ref[k]
        outs[k][(NODES - SIDE) * share :] = parts[k][half:]


def gather_kernel(dims, where_ref, pick_ref, state_ref, *refs):
    rows, cols, share, span, modes = dims
    takes = refs[:span]
    out_any, flat, out_ref, sems = refs[span:]
    elems = rows * cols
    count = span * modes
    turned = pick_ref[...].T[:elems]
    pick = jnp.concatenate([turned] * (LANES // elems), axis=1).astype(jnp.bfloat16)
    for node in range(NODES):
        part = jnp.concatenate([take[pl.ds(node * share, share), :] for take in takes], axis=0)
        high, low = split(part)
        flat[pl.ds(node, elems, stride=NODES), :] = mm(pick, jnp.concatenate([high, low], axis=0))
    index = where_ref[0] * modes + lax.broadcasted_iota(jnp.int32, (LANES, 1), 0) % modes
    wave = jnp.where(index == 1, count // 2, index // 2).astype(jnp.float32)
    damping = 1.0 / (1.0 + TIME_STEP * VISCOSITY * wave * wave)
    copies = []
    for start in range(0, elems * NODES, CHUNK):
        for block in range(start, start + CHUNK, LANES):
            at = pl.ds(block, LANES)
            out_ref[:, at] = state_ref[:, at] * damping + flat[at, :].T
        at = pl.ds(start, CHUNK)
        copies.append(
            pltpu.make_async_copy(out_ref.at[:, at], out_any.at[:, at], sems.at[start // CHUNK])
        )
        copies[-1].start()
    for copy in copies:
        copy.wait()


def smem():
    return pl.BlockSpec(memory_space=pltpu.SMEM)


def in_hbm(array):
    return pltpu.with_memory_space_constraint(array, pltpu.HBM)


def anywhere(count):
    return [pl.BlockSpec(memory_space=pltpu.HBM)] * count


def vmem(count):
    return [pl.BlockSpec(memory_space=pltpu.VMEM)] * count


PARAMS = pltpu.CompilerParams(vmem_limit_bytes=24 * 1024 * 1024)


def exchange(blocks, span):
    taken = {0: blocks[0]}
    for k in range(1, span):
        taken[k] = lax.ppermute(blocks[k], "span", [(s, s ^ k) for s in range(span)])
    return [taken[k] for k in range(span)]


def ordered_body(state, metric, neighbour, wall, rim):
    num_vars, modes, flat_size = state.shape
    elems = flat_size // NODES
    span = lax.axis_size("span")
    groups = lax.axis_size("elem")
    share = elems // span
    rows = rim.shape[1]
    cols = elems // rows
    count = modes * span
    tiles = count // LANES
    lines = share // cols
    me = jnp.stack([lax.axis_index("span"), lax.axis_index("elem") % 2])
    flat_state = state.reshape(num_vars * modes, flat_size)
    f32 = jnp.float32
    whole, rim_part, core_part = (
        jax.ShapeDtypeStruct((nodes * share, LANES), f32)
        for nodes in (NODES, len(RIM_NODES) + SIDE, len(CORE_NODES))
    )
    chunks = flat_size // CHUNK
    first = pl.pallas_call(
        functools.partial(spread_kernel, (rows, cols, share, span)),
        out_shape=[rim_part] * span
        + [core_part] * span
        + [
            jax.ShapeDtypeStruct((elems, LANES), f32),
            jax.ShapeDtypeStruct((4, share, LANES), f32),
        ],
        in_specs=[smem()] + anywhere(5),
        out_specs=vmem(2 * span + 2),
        scratch_shapes=[
            pltpu.VMEM((elems, LANES), f32),
            pltpu.VMEM((2, elems, LANES), jnp.int32),
            pltpu.SMEM(neighbour.T.shape, jnp.int32),
            pltpu.SMEM(wall.T.shape, jnp.int32),
            pltpu.SMEM(rim.shape, jnp.int32),
            pltpu.SMEM(metric.shape, f32),
            pltpu.VMEM(flat_state.shape, f32),
            pltpu.VMEM((flat_size, LANES), f32),
            pltpu.SemaphoreType.DMA((4 + chunks,)),
        ],
        compiler_params=PARAMS,
        name="spread",
    )(me, *[in_hbm(x) for x in (neighbour.T, wall.T, rim, metric, flat_state)])
    rim_takes = exchange(first[:span], span)
    core_takes = exchange(first[span : 2 * span], span)
    pick, facts = first[2 * span :]

    dims = (cols, share, span, num_vars, modes)
    forward = [jnp.asarray(t) for t in forward_tables(count)]
    backward = [jnp.asarray(t) for t in backward_tables(count)]
    line_shape = jax.ShapeDtypeStruct((tiles, num_vars, SIDE * lines, LANES), f32)
    planes = pl.pallas_call(
        functools.partial(planes_kernel, dims),
        out_shape=[
            jax.ShapeDtypeStruct((tiles, num_vars, (len(RIM_NODES) + SIDE) * share, LANES), f32),
            line_shape,
            line_shape,
        ],
        in_specs=[smem()] + vmem(3 + span),
        out_specs=vmem(3),
        compiler_params=PARAMS,
        name="planes",
    )
    phys, one, two = planes(me, facts, *forward, *rim_takes)
    one = lax.ppermute(one, "elem", [(g, g ^ 1) for g in range(groups)])
    two = lax.ppermute(
        two, "elem", [(g, (g - 1 if g % 2 == 0 else g + 1) % groups) for g in range(groups)]
    )

    middle = NODES - 2 * SIDE
    rates = pl.pallas_call(
        functools.partial(rates_kernel, dims),
        out_shape=[
            jax.ShapeDtypeStruct((span, middle * share, LANES), f32),
            jax.ShapeDtypeStruct((num_vars, 2 * SIDE * share, 2 * count), f32),
        ],
        in_specs=[smem()] + vmem(6 + span),
        out_specs=vmem(2),
        scratch_shapes=[
            pltpu.VMEM((tiles, num_vars, len(CORE_NODES) * share, LANES), f32),
            pltpu.VMEM((num_vars, middle * share, 2 * count), f32),
        ],
        compiler_params=PARAMS,
        name="rates",
    )
    mid, edge = rates(me, facts, *forward, *backward, phys, *core_takes)
    gains = pl.pallas_call(
        functools.partial(edges_kernel, dims),
        out_shape=[whole] * span,
        in_specs=[smem()] + vmem(7),
        out_specs=vmem(span),
        scratch_shapes=[pltpu.VMEM((num_vars, 2 * SIDE * share, count), f32)],
        compiler_params=PARAMS,
        name="edges",
    )(me, facts, *backward, mid, edge, one, two)
    takes = exchange(gains, span)

    out = pl.pallas_call(
        functools.partial(gather_kernel, (rows, cols, share, span, modes)),
        out_shape=jax.ShapeDtypeStruct((num_vars * modes, flat_size), f32),
        in_specs=[smem()] + vmem(2 + span),
        out_specs=pl.BlockSpec(memory_space=pltpu.HBM),
        scratch_shapes=[
            pltpu.VMEM((flat_size, LANES), f32),
            pltpu.VMEM(flat_state.shape, f32),
            pltpu.SemaphoreType.DMA((chunks,)),
        ],
        compiler_params=PARAMS,
        name="collect",
    )(me, pick, flat_state, *takes)
    return out.reshape(state.shape)


def from_behind(value, axis, steps):
    count = lax.axis_size(axis)
    pairs = [(source, (source + steps) % count) for source in range(count)]
    return lax.ppermute(value, axis, pairs)


def gll_tables():
    near_point = math.sqrt(1.0 / 3.0 - 2.0 * math.sqrt(7.0) / 21.0)
    far_point = math.sqrt(1.0 / 3.0 + 2.0 * math.sqrt(7.0) / 21.0)
    points = np.array([-1.0, -far_point, -near_point, near_point, far_point, 1.0])
    weights = np.array(
        [
            1.0
            / np.prod([points[column] - points[second] for second in range(6) if second != column])
            for column in range(6)
        ]
    )
    deriv = np.zeros((6, 6))
    for target in range(6):
        for source in range(6):
            if source != target:
                deriv[target, source] = (
                    weights[source] / weights[target] / (points[target] - points[source])
                )
        deriv[target, target] = -np.sum(deriv[target])
    identity = np.eye(6)
    along_x = np.kron(deriv, identity)
    along_y = np.kron(identity, deriv)
    edge_nodes = np.array(
        [
            [offset for offset in range(6)],
            [30 + offset for offset in range(6)],
            [6 * offset for offset in range(6)],
            [6 * offset + 5 for offset in range(6)],
        ]
    ).reshape(-1)
    lifting = np.zeros((36, 24))
    lifting[edge_nodes, np.arange(24)] = 1.0
    return (
        jnp.asarray(along_x, jnp.float32),
        jnp.asarray(along_y, jnp.float32),
        edge_nodes,
        jnp.asarray(lifting, jnp.float32),
    )


def spanwise_basis(count):
    mode_index = jnp.arange(count, dtype=jnp.int32)
    planes = jnp.arange(count, dtype=jnp.int32)
    phase = mode_index[:, None] // 2 * planes[None, :] % count
    phase_angle = phase.astype(jnp.float32) * (2.0 * math.pi / count)
    odd_rows = (mode_index % 2 == 1)[:, None]
    basis_table = jnp.where(odd_rows, jnp.sin(phase_angle), jnp.cos(phase_angle)) * math.sqrt(
        2.0 / count
    )
    alternate = (1 - 2 * (planes % 2)).astype(jnp.float32) / math.sqrt(count)
    constant = jnp.ones((count,), jnp.float32) / math.sqrt(count)
    basis_table = jnp.where(mode_index[:, None] == 0, constant[None, :], basis_table)
    basis_table = jnp.where(mode_index[:, None] == 1, alternate[None, :], basis_table)
    return basis_table


def spanwise_derivative(modal):
    shape_in = modal.shape
    paired = modal.reshape(shape_in[0], shape_in[1] // 2, 2, shape_in[2])
    wavenumber = jnp.arange(shape_in[1] // 2, dtype=jnp.int32).astype(jnp.float32)[None, :, None]
    return jnp.stack([wavenumber * paired[:, :, 1], -wavenumber * paired[:, :, 0]], axis=2).reshape(
        shape_in
    )


def planar_terms(flux_x, flux_y, metric_part):
    along_x, along_y, edge_nodes, _ = gll_tables()
    scale_x = metric_part[0][:, None]
    scale_y = metric_part[1][:, None]
    grad_x = jnp.einsum("pq,vmeq->vmep", along_x, flux_x, precision=HIGHEST)
    grad_y = jnp.einsum("pq,vmeq->vmep", along_y, flux_y, precision=HIGHEST)
    planar = scale_x * grad_x + scale_y * grad_y
    sign_x = jnp.sign(scale_x)
    sign_y = jnp.sign(scale_y)
    edge_flux = jnp.concatenate(
        [
            -sign_x * flux_x[:, :, :, edge_nodes[0:6]],
            sign_x * flux_x[:, :, :, edge_nodes[6:12]],
            -sign_y * flux_y[:, :, :, edge_nodes[12:18]],
            sign_y * flux_y[:, :, :, edge_nodes[18:24]],
        ],
        axis=3,
    )
    return (planar, edge_flux)


def node_major(flat, num_vars, local_modes, nodes, local_elems):
    return jnp.transpose(flat.reshape(num_vars, local_modes, local_elems, nodes), (0, 1, 3, 2))


def trace_pool(traces):
    shape_in = traces.shape
    return (
        traces.reshape(shape_in[0], shape_in[1], 4, 6, shape_in[3])
        .transpose(0, 1, 3, 4, 2)
        .reshape(shape_in[0], shape_in[1], 6, 4 * shape_in[3])
    )


def own_pools(state_local, normal_flux):
    edge_nodes = gll_tables()[2]
    return (trace_pool(state_local[:, :, edge_nodes, :]), trace_pool(normal_flux))


def update(
    state_local,
    divergence,
    own_q,
    own_flux,
    from_lower,
    from_upper,
    neighbour,
    orient,
    wall,
    metric_local,
    first_mode,
    total_modes,
):
    lifting = gll_tables()[3]
    num_vars, modes_here, _, count = state_local.shape
    pool_q = jnp.concatenate([own_q, from_lower[0], from_upper[0]], axis=3)
    pool_flux = jnp.concatenate([own_flux, from_lower[1], from_upper[1]], axis=3)
    flat_index = neighbour.reshape(-1)
    other_q = jnp.take(pool_q, flat_index, axis=3)
    other_flux = jnp.take(pool_flux, flat_index, axis=3)
    flipped = orient.reshape(-1) == 1
    other_q = jnp.where(flipped, other_q[:, :, ::-1, :], other_q)
    other_flux = jnp.where(flipped, other_flux[:, :, ::-1, :], other_flux)
    mirror = jnp.array([-1.0, -1.0, -1.0, 1.0], jnp.float32).reshape(4, 1, 1, 1)
    walled = wall.reshape(-1) == 1
    other_q = jnp.where(walled, mirror * own_q, other_q)
    other_flux = jnp.where(walled, mirror * own_flux, other_flux)
    magnitude = (
        jnp.abs(
            jnp.stack([metric_local[0], metric_local[0], metric_local[1], metric_local[1]], axis=1)
        ).reshape(-1)
        * 15.0
    )
    surface_jump = magnitude * (0.5 * (own_flux + other_flux) - 0.5 * PENALTY * (own_q - other_q))
    unpooled = (
        surface_jump.reshape(num_vars, modes_here, 6, count, 4)
        .transpose(0, 1, 4, 2, 3)
        .reshape(num_vars, modes_here, 24, count)
    )
    surface = jnp.einsum("pq,vmqe->vmpe", lifting, unpooled, precision=HIGHEST)
    mode_index = first_mode + jnp.arange(modes_here, dtype=jnp.int32)
    wavenumber = jnp.where(mode_index == 1, total_modes // 2, mode_index // 2).astype(jnp.float32)
    damping = 1.0 + TIME_STEP * VISCOSITY * wavenumber * wavenumber
    return (state_local + TIME_STEP * (surface - divergence)) / damping[None, :, None, None]


def plain_body(state, metric, neighbour, orient, wall, rim):
    num_vars, local_modes, flat_size = state.shape
    num_nodes = 36
    local_elems = flat_size // num_nodes
    span_size = lax.axis_size("span")
    total_modes = local_modes * span_size
    share = local_elems // span_size
    state_nodes = node_major(state, num_vars, local_modes, num_nodes, local_elems)
    planes_in = lax.all_to_all(state, "span", split_axis=2, concat_axis=1, tiled=True)
    basis_table = spanwise_basis(total_modes)
    physical = jnp.einsum("mn,vmk->vnk", basis_table, planes_in, precision=HIGHEST)
    metric_part = lax.dynamic_slice_in_dim(metric, lax.axis_index("span") * share, share, axis=1)
    shape_here = (num_vars, total_modes, share, num_nodes)
    planar_div, edge_flux = planar_terms(
        (physical[0:1] * physical).reshape(shape_here),
        (physical[1:2] * physical).reshape(shape_here),
        metric_part,
    )
    volume_fields = jnp.concatenate(
        [planar_div.reshape(num_vars, total_modes, share * num_nodes), physical[2:3] * physical],
        axis=0,
    )
    volume_modal = jnp.einsum("mn,vnk->vmk", basis_table, volume_fields, precision=HIGHEST)
    edge_modal = jnp.einsum(
        "mn,vnk->vmk",
        basis_table,
        edge_flux.reshape(num_vars, total_modes, share * 24),
        precision=HIGHEST,
    )
    combined = volume_modal[0:4] + spanwise_derivative(volume_modal[4:8])
    div_flat, flux_flat = (
        lax.all_to_all(combined, "span", split_axis=1, concat_axis=2, tiled=True),
        lax.all_to_all(edge_modal, "span", split_axis=1, concat_axis=2, tiled=True),
    )
    divergence = node_major(div_flat, num_vars, local_modes, num_nodes, local_elems)
    normal_flux = node_major(flux_flat, num_vars, local_modes, 24, local_elems)
    own_q, own_flux = own_pools(state_nodes, normal_flux)
    upper_rim = jnp.stack([jnp.take(own_q, rim[1], axis=3), jnp.take(own_flux, rim[1], axis=3)])
    lower_rim = jnp.stack([jnp.take(own_q, rim[0], axis=3), jnp.take(own_flux, rim[0], axis=3)])
    from_lower = from_behind(upper_rim, "elem", 1)
    from_upper = from_behind(lower_rim, "elem", -1)
    first_mode = lax.axis_index("span") * local_modes
    result = update(
        state_nodes,
        divergence,
        own_q,
        own_flux,
        from_lower,
        from_upper,
        neighbour,
        orient,
        wall,
        metric,
        first_mode,
        total_modes,
    )
    return jnp.transpose(result, (0, 1, 3, 2)).reshape(num_vars, local_modes, flat_size)


def body(state, metric, neighbour, orient, wall, rim):
    num_vars, modes, flat_size = state.shape
    span = lax.axis_size("span")
    groups = lax.axis_size("elem")
    elems = flat_size // NODES
    rows = rim.shape[1]
    fits = (
        groups % 2 == 0
        and rows % span == 0
        and SUB == 2 * (elems // rows)
        and num_vars * modes == LANES
        and modes * 4 == LANES
        and span % 4 == 0
        and span & (span - 1) == 0
        and LANES % elems == 0
        and elems == SUB * span
        and elems % rows == 0
        and SUB % (elems // rows) == 0
        and flat_size % CHUNK == 0
    )
    if not fits:
        return plain_body(state, metric, neighbour, orient, wall, rim)
    return ordered_body(state, metric, neighbour, wall, rim)


def solution(mesh):
    placed = (
        P(None, "span", "elem"),
        P(None, "elem"),
        P("elem", None),
        P("elem", None),
        P("elem", None),
        P(None, "elem"),
    )
    return jax.shard_map(
        body, mesh=mesh, in_specs=placed, out_specs=P(None, "span", "elem"), check_vma=False
    )
```

```python
import functools
import math

import jax
import jax.numpy as jnp
import numpy as np
from jax import lax
from jax.experimental import pallas as pl
from jax.experimental.pallas import tpu as pltpu
from jax.sharding import PartitionSpec as P


TIME_STEP = 0.001
VISCOSITY = 0.02
PENALTY = 1.0
HIGHEST = lax.Precision.HIGHEST
SIDE = 6
NODES = SIDE * SIDE
LANES = 128
SUB = 8
CHUNK = 3 * LANES
RIM_NODES = [p for p in range(NODES) if p // SIDE in (0, 5) or p % SIDE in (0, 5)]
CORE_NODES = [p for p in range(NODES) if p not in RIM_NODES]
MID_NODES = [p for p in range(NODES) if p // SIDE not in (0, 5)]
END_NODES = [p for p in range(NODES) if p // SIDE in (0, 5)]


def gll_matrix():
    near_point = math.sqrt(1.0 / 3.0 - 2.0 * math.sqrt(7.0) / 21.0)
    far_point = math.sqrt(1.0 / 3.0 + 2.0 * math.sqrt(7.0) / 21.0)
    points = np.array([-1.0, -far_point, -near_point, near_point, far_point, 1.0])
    weights = np.array(
        [
            1.0
            / np.prod([points[column] - points[second] for second in range(6) if second != column])
            for column in range(6)
        ]
    )
    deriv = np.zeros((6, 6))
    for target in range(6):
        for source in range(6):
            if source != target:
                deriv[target, source] = (
                    weights[source] / weights[target] / (points[target] - points[source])
                )
        deriv[target, target] = -np.sum(deriv[target])
    return deriv


def basis_matrix(count):
    mode = np.arange(count)[:, None]
    plane = np.arange(count)[None, :]
    angle = (mode // 2 * plane % count) * (2.0 * math.pi / count)
    table = np.where(mode % 2 == 1, np.sin(angle), np.cos(angle)) * math.sqrt(2.0 / count)
    table = np.where(mode == 0, 1.0 / math.sqrt(count), table)
    return np.where(mode == 1, (1.0 - 2.0 * (plane % 2)) / math.sqrt(count), table)


def halves(table):
    table = np.asarray(table, np.float32)
    high = table.astype(jnp.bfloat16)
    low = (table - high.astype(np.float32)).astype(jnp.bfloat16)
    return high, low


def forward_tables(count):
    return halves(basis_matrix(count))


def backward_tables(count):
    basis = basis_matrix(count)
    wave = np.arange(count) // 2
    swapped = np.empty_like(basis)
    swapped[0::2] = wave[0::2, None] * basis[1::2]
    swapped[1::2] = -wave[1::2, None] * basis[0::2]
    damp_wave = np.where(np.arange(count) == 1, count // 2, wave).astype(np.float64)
    factor = TIME_STEP / (1.0 + TIME_STEP * VISCOSITY * damp_wave * damp_wave)
    return halves(factor[:, None] * np.concatenate([basis, -swapped], axis=1))


def split(value):
    high = value.astype(jnp.bfloat16)
    low = (value - high.astype(jnp.float32)).astype(jnp.bfloat16)
    return high, low


def mm(a, b):
    return lax.dot_general(a, b, (((1,), (0,)), ((), ())), preferred_element_type=jnp.float32)


def mm_nt(a, b):
    return lax.dot_general(a, b, (((1,), (1,)), ((), ())), preferred_element_type=jnp.float32)


def regroup(parts, lane):
    quarter = LANES // 4
    low_half = lane < 2 * quarter
    rolled = [pltpu.roll(part, 2 * quarter, 1) for part in parts]
    first = [
        jnp.where(low_half, parts[0], rolled[2]),
        jnp.where(low_half, parts[1], rolled[3]),
        jnp.where(low_half, rolled[0], parts[2]),
        jnp.where(low_half, rolled[1], parts[3]),
    ]
    even = lane // quarter % 2 == 0
    out = []
    for pair in (0, 2):
        a, b = first[pair], first[pair + 1]
        out.append(jnp.where(even, a, pltpu.roll(b, quarter, 1)))
        out.append(jnp.where(even, pltpu.roll(a, LANES - quarter, 1), b))
    return out


def move_nodes(nodes, elems, flat, pick, pick_sides, put):
    for at in range(0, len(nodes), 2):
        pair = nodes[at : at + 2]
        columns = [
            jnp.concatenate(split(flat[pl.ds(node, elems, stride=NODES), :]), axis=0)
            for node in pair
        ]
        chosen = pick_sides if any(node % SIDE in (0, 5) for node in pair) else pick
        moved = mm(chosen, jnp.concatenate(columns, axis=1))
        for half, node in enumerate(pair):
            put(at + half, node, moved[:, half * LANES : (half + 1) * LANES])


def spread_kernel(dims, near_any, wall_any, rim_any, metric_any, state_any, *refs):
    rows, cols, share, span = dims
    sends = refs[:span]
    pick_ref, facts_ref, flat, all_ref = refs[span : span + 4]
    halo_ref, bends_ref, near_ref, wall_ref, rim_ref, metric_ref, state_ref, sems = refs[span + 4 :]
    me = lax.axis_index("span")
    elems = rows * cols
    width = elems * NODES
    small = [
        pltpu.make_async_copy(source, target, sems.at[at])
        for at, (source, target) in enumerate(
            (
                (near_any, near_ref),
                (wall_any, wall_ref),
                (rim_any, rim_ref),
                (metric_any, metric_ref),
            )
        )
    ]
    large = [
        pltpu.make_async_copy(
            state_any.at[:, pl.ds(at, CHUNK)],
            state_ref.at[:, pl.ds(at, CHUNK)],
            sems.at[len(small) + at // CHUNK],
        )
        for at in range(0, width, CHUNK)
    ]
    for copy in small + large:
        copy.start()
    for copy in small:
        copy.wait()
    lane = lax.broadcasted_iota(jnp.int32, (1, LANES), 1) % elems
    lines = share // cols
    halo_ref[...] = jnp.zeros_like(halo_ref)
    bends_ref[...] = jnp.zeros_like(bends_ref)
    before = None
    for row in range(rows):
        cell = rim_ref[0, row] >> 2
        face = rim_ref[0, row] & 1
        here = []
        for col in range(cols):
            if row == 0:
                flip_y = wall_ref[3, cell]
            else:
                flip_y = jnp.where(near_ref[3, cell] >> 2 == before[col], 1, 0)
            here.append(cell)
            place = row * cols + col
            at = (place // share ^ me) * share + place % share
            chosen = jnp.where(lane == cell, 1.0, 0.0)
            pick_ref[pl.ds(at, 1), :] = chosen
            if row % lines == lines - 1 and row + 1 < rows:
                under = ((row // lines + 1) ^ me) * share + col
                halo_ref[pl.ds(under, 1), :] = chosen
                for kind, bend in enumerate((face, 1 - flip_y)):
                    bends_ref[kind, pl.ds(under, 1), :] = jnp.full((1, LANES), bend, jnp.int32)
            if row % lines == 0 and row > 0:
                over = ((row // lines - 1) ^ me) * share + cols + col
                halo_ref[pl.ds(over, 1), :] = chosen
                for kind, bend in enumerate((face, flip_y)):
                    bends_ref[kind, pl.ds(over, 1), :] = jnp.full((1, LANES), bend, jnp.int32)
            facts = (
                metric_ref[0, cell],
                metric_ref[1, cell],
                face.astype(jnp.float32),
                flip_y.astype(jnp.float32),
            )
            for kind, fact in enumerate(facts):
                all_ref[kind, pl.ds(at, 1), :] = jnp.full((1, LANES), fact, jnp.float32)
            if col + 1 < cols:
                step = near_ref[face ^ 1, cell]
                cell = step >> 2
                face = step & 1
        before = here
    for at in range(0, width, LANES):
        if at % CHUNK == 0:
            large[at // CHUNK].wait()
        flat[pl.ds(at, LANES), :] = state_ref[:, pl.ds(at, LANES)].T
    facts_ref[...] = all_ref[:, :share]
    pick = pick_ref[...].astype(jnp.bfloat16)
    both = jnp.concatenate([pick, halo_ref[...].astype(jnp.bfloat16)], axis=0)
    edge = {}

    def put(at, node, mine):
        if node % SIDE in (0, 5):
            edge[divmod(node, SIDE)] = mine[elems:]
        for step in range(span):
            sends[step][pl.ds(at * share, share), :] = mine[step * share : (step + 1) * share]

    move_nodes(RIM_NODES, elems, flat, pick, both, put)
    bend_x = bends_ref[0] == 1
    bend_y = bends_ref[1] == 1
    trace = [jnp.where(bend_y, edge[t, 5], edge[t, 0]) for t in range(SIDE)]
    for t in range(SIDE):
        moved = jnp.where(bend_x, trace[SIDE - 1 - t], trace[t])
        at = pl.ds((len(RIM_NODES) + t) * share, share)
        for step in range(span):
            sends[step][at, :] = moved[step * share : (step + 1) * share]


def spread_core_kernel(share, span, pick_ref, flat, odd_ref, *evens):
    pick = pick_ref[...].astype(jnp.bfloat16)
    size = len(CORE_NODES) * share

    def put(at, node, mine):
        for step in range(span):
            value = mine[step * share : (step + 1) * share]
            if step % 2:
                odd_ref[pl.ds(step // 2 * size + at * share, share), :] = value
            else:
                evens[step // 2][pl.ds(at * share, share), :] = value

    move_nodes(CORE_NODES, pick.shape[0], flat, pick, pick, put)


def along(trace, flip):
    return {t: jnp.where(flip, trace[SIDE - 1 - t], trace[t]) for t in trace}


def sides_x(value, flip_x, flip_y):
    low = {t: jnp.where(flip_x, value(5, t), value(0, t)) for t in range(SIDE)}
    high = {t: jnp.where(flip_x, value(0, t), value(5, t)) for t in range(SIDE)}
    return along(low, flip_y), along(high, flip_y)


def sides_y(value, flip_x, flip_y, wanted):
    low = {t: jnp.where(flip_y, value(t, 5), value(t, 0)) for t in wanted}
    high = {t: jnp.where(flip_y, value(t, 0), value(t, 5)) for t in wanted}
    return along(low, flip_x), along(high, flip_x)


def rim_reader(ref, tile, var):
    return lambda i, j: ref[tile, var, pl.ds(RIM_NODES.index(SIDE * i + j) * SUB, SUB), :]


def back(one, two, flip, flip_along):
    return along({t: jnp.where(flip, two[t], one[t]) for t in one}, flip_along)


def sign(value):
    return jnp.where(value < 0.0, -1.0, 1.0)


def to_planes(dims, me, high_ref, low_ref, takes, phys_ref):
    _, _, span, num_vars, modes = dims
    lane = lax.broadcasted_iota(jnp.int32, (1, LANES), 1)
    tables = []
    for ref in (high_ref, low_ref):
        tables.append(
            jnp.concatenate([ref[pl.ds((me ^ k) * modes, modes), :] for k in range(span)], axis=0)
        )
    pieces = []
    for group in range(span // 4):
        pieces.append(regroup([takes[4 * group + q][...] for q in range(4)], lane))
    stack = [jnp.concatenate([piece[var] for piece in pieces], axis=1) for var in range(num_vars)]
    high, low = split(jnp.concatenate(stack, axis=0))
    planes = mm(high, tables[0]) + mm(low, tables[0]) + mm(high, tables[1])
    size = takes[0].shape[0]
    for var in range(num_vars):
        for tile in range(span * modes // LANES):
            phys_ref[tile, var] = planes[
                var * size : (var + 1) * size, tile * LANES : (tile + 1) * LANES
            ]


def planes_kernel(dims, facts_ref, high_ref, low_ref, *refs):
    cols, share, span, num_vars, modes = dims
    takes = refs[:span]
    phys_ref, one_ref, two_ref = refs[span:]
    to_planes(dims, lax.axis_index("span"), high_ref, low_ref, takes, phys_ref)
    odd = lax.axis_index("elem") % 2 == 1
    lines = share // cols
    flip_x = facts_ref[2] > 0.5
    flip_y = facts_ref[3] > 0.5
    turn_x = sign(facts_ref[0]) * (1.0 - 2.0 * facts_ref[2])
    for tile in range(span * modes // LANES):
        speed = sides_x(rim_reader(phys_ref, tile, 0), flip_x, flip_y)
        for var in range(num_vars):
            trace = sides_x(rim_reader(phys_ref, tile, var), flip_x, flip_y)
            for t in range(SIDE):
                low_x = (1.0 - turn_x * speed[0][t]) * trace[0][t]
                high_x = (1.0 + turn_x * speed[1][t]) * trace[1][t]
                for line in range(lines):
                    at = pl.ds(t * lines + line, 1)
                    up = high_x[(line + 1) * cols - 1 : (line + 1) * cols]
                    down = low_x[line * cols : line * cols + 1]
                    one_ref[tile, var, at, :] = jnp.where(odd, down, up)
                    two_ref[tile, var, at, :] = jnp.where(odd, up, down)


def to_modes(dims, me, high_ref, low_ref, rates):
    _, _, span, num_vars, modes = dims
    lane = lax.broadcasted_iota(jnp.int32, (1, LANES), 1)
    tables = []
    for ref in (high_ref, low_ref):
        tables.append(
            jnp.concatenate([ref[pl.ds((me ^ k) * modes, modes), :] for k in range(span)], axis=0)
        )
    size = rates[0].shape[0]
    high, low = split(jnp.concatenate(rates, axis=0))
    gain = mm_nt(high, tables[0]) + mm_nt(low, tables[0]) + mm_nt(high, tables[1])
    gains = [gain[var * size : (var + 1) * size] for var in range(num_vars)]
    out = []
    for group in range(span // 4):
        at = slice(group * LANES, (group + 1) * LANES)
        out += regroup([gain[:, at] for gain in gains], lane)
    return out


def derivative(values, wanted=tuple(range(SIDE))):
    deriv = gll_matrix()
    last = SIDE - 1
    plus = [values[j] + values[last - j] for j in range(SIDE // 2)]
    minus = [values[j] - values[last - j] for j in range(SIDE // 2)]
    out = [None] * SIDE
    for i in range(SIDE // 2):
        if i not in wanted:
            continue
        even, odd = None, None
        for j in range(SIDE // 2):
            a = minus[j] * float(0.5 * (deriv[i, j] - deriv[i, last - j]))
            b = plus[j] * float(0.5 * (deriv[i, j] + deriv[i, last - j]))
            even = a if even is None else even + a
            odd = b if odd is None else odd + b
        out[i] = even + odd
        out[last - i] = even - odd
    return out


class Faces:
    def __init__(self, dims, facts_ref, phys_ref, core_ref):
        cols, share, span, self.num_vars, modes = dims
        self.cols = cols
        self.phys_ref, self.core_ref = phys_ref, core_ref
        me = lax.axis_index("span")
        slot = lax.broadcasted_iota(jnp.int32, (SUB, LANES), 0)
        self.slot = slot
        self.flip_x = facts_ref[2] > 0.5
        self.flip_y = facts_ref[3] > 0.5
        self.scale_x = -facts_ref[0]
        self.scale_y = facts_ref[1]
        self.turn_x = sign(facts_ref[0]) * (1.0 - 2.0 * facts_ref[2])
        self.turn_y = sign(facts_ref[1]) * (1.0 - 2.0 * facts_ref[3])
        self.weight_x = 7.5 * jnp.abs(facts_ref[0])
        self.weight_y = 7.5 * jnp.abs(facts_ref[1])
        self.first_line = slot < cols
        self.turn_halo = jnp.where(self.first_line, self.turn_y, -self.turn_y)
        self.floor = jnp.logical_and(self.first_line, me == 0)
        self.roof = jnp.logical_and(jnp.logical_not(self.first_line), me == span - 1)

    def reader(self, tile, var):
        def read(i, j):
            node = SIDE * i + j
            ref = self.phys_ref if node in RIM_NODES else self.core_ref
            nodes = RIM_NODES if node in RIM_NODES else CORE_NODES
            return ref[tile, var, pl.ds(nodes.index(node) * SUB, SUB), :]

        return read

    def volume(self, tile, var, wanted):
        q, u, v = (self.reader(tile, at) for at in (var, 0, 1))
        total = {}
        for j in range(SIDE):
            slope = derivative([q(i, j) * u(i, j) for i in range(SIDE)], wanted)
            for i in wanted:
                total[i, j] = self.scale_x * slope[i]
        for i in wanted:
            slope = derivative([q(i, j) * v(i, j) for j in range(SIDE)])
            for j in range(SIDE):
                total[i, j] = total[i, j] - self.scale_y * slope[j]
        return total

    def pace_y(self, tile, wanted):
        speed = sides_y(self.reader(tile, 1), self.flip_x, self.flip_y, wanted)
        return [{t: self.turn_y * side[t] for t in wanted} for side in speed]

    def faces_y(self, tile, var, pace, wanted, total):
        mirror = 1.0 if var == self.num_vars - 1 else -1.0
        trace = sides_y(self.reader(tile, var), self.flip_x, self.flip_y, wanted)
        low, high = {}, {}
        for t in wanted:
            at = pl.ds((len(RIM_NODES) + t) * SUB, SUB)
            speed, value = pace[0][t], trace[0][t]
            own_low, give_low = -(speed + 1.0) * value, (1.0 - speed) * value
            speed, value = pace[1][t], trace[1][t]
            own_high, give_high = (speed - 1.0) * value, (1.0 + speed) * value
            outside = (1.0 + self.turn_halo * self.phys_ref[tile, 1, at, :]) * self.phys_ref[
                tile, var, at, :
            ]
            outside = jnp.where(self.floor, mirror * give_low, outside)
            outside = jnp.where(self.roof, mirror * give_high, outside)
            from_low = jnp.where(self.first_line, outside, pltpu.roll(give_high, self.cols, 0))
            from_high = jnp.where(
                self.first_line, pltpu.roll(give_low, SUB - self.cols, 0), outside
            )
            low[t] = self.weight_y * (own_low + from_low)
            high[t] = self.weight_y * (own_high + from_high)
        for j, one, two in ((0, low, high), (5, high, low)):
            side = back(one, two, self.flip_y, self.flip_x)
            for t in wanted:
                total[t, j] = total[t, j] + side[t]

    def pace_x(self, tile):
        speed = sides_x(self.reader(tile, 0), self.flip_x, self.flip_y)
        return [{t: self.turn_x * side[t] for t in side} for side in speed]

    def faces_x(self, tile, var, pace, total, rim):
        trace = sides_x(self.reader(tile, var), self.flip_x, self.flip_y)
        low, high = {}, {}
        for t in range(SIDE):
            speed, value = pace[0][t], trace[0][t]
            own_low, give_low = -(speed + 1.0) * value, (1.0 - speed) * value
            speed, value = pace[1][t], trace[1][t]
            own_high, give_high = (speed - 1.0) * value, (1.0 + speed) * value
            from_low, from_high = pltpu.roll(give_high, 1, 0), pltpu.roll(give_low, SUB - 1, 0)
            for line, (below, above) in enumerate(rim(t)):
                from_low = jnp.where(self.slot == line * self.cols, below, from_low)
                from_high = jnp.where(self.slot == (line + 1) * self.cols - 1, above, from_high)
            low[t] = self.weight_x * (own_low + from_low)
            high[t] = self.weight_x * (own_high + from_high)
        for i, one, two in ((0, low, high), (5, high, low)):
            side = back(one, two, self.flip_x, self.flip_y)
            for t in range(SIDE):
                total[i, t] = total[i, t] + side[t]


def unpaired(refs, size):
    takes = list(refs[:2])
    for ref in refs[2:]:
        takes += [ref.at[:size], ref.at[size:]]
    return takes


def store_rates(rate_ref, nodes, tile, var, count, total, q, w):
    for place, node in enumerate(nodes):
        i, j = divmod(node, SIDE)
        at = pl.ds(place * SUB, SUB)
        rate_ref[var, at, pl.ds(tile * LANES, LANES)] = total[i, j]
        rate_ref[var, at, pl.ds(count + tile * LANES, LANES)] = q(i, j) * w(i, j)


def rates_kernel(
    dims, facts_ref, there_high, there_low, high_ref, low_ref, phys_ref, *refs
):
    _, share, span, num_vars, modes = dims
    half = span // 2
    outs = refs[half + 1 : half + 1 + span]
    core_ref, rate_ref = refs[half + 1 + span :]
    takes = unpaired(refs[: half + 1], len(CORE_NODES) * share)
    me = lax.axis_index("span")
    to_planes(dims, me, there_high, there_low, takes, core_ref)
    count = span * modes
    faces = Faces(dims, facts_ref, phys_ref, core_ref)
    wanted = tuple(range(1, SIDE - 1))
    for tile in range(count // LANES):
        pace = faces.pace_y(tile, wanted)
        for var in range(num_vars):
            total = faces.volume(tile, var, wanted)
            faces.faces_y(tile, var, pace, wanted, total)
            q, w = faces.reader(tile, var), faces.reader(tile, 2)
            store_rates(rate_ref, MID_NODES, tile, var, count, total, q, w)
    parts = to_modes(dims, me, high_ref, low_ref, [rate_ref[var] for var in range(num_vars)])
    for k in range(span):
        outs[k][...] = parts[k]


def edges_kernel(
    dims, facts_ref, high_ref, low_ref, phys_ref, core_ref, one_ref, two_ref, *refs
):
    cols, share, span, num_vars, modes = dims
    odd_ref, *evens, rate_ref = refs
    count = span * modes
    lines = share // cols
    odd = lax.axis_index("elem") % 2 == 1
    faces = Faces(dims, facts_ref, phys_ref, core_ref)
    wanted = (0, SIDE - 1)
    for tile in range(count // LANES):
        pace_x, pace_y = faces.pace_x(tile), faces.pace_y(tile, wanted)
        for var in range(num_vars):

            def rim(t, tile=tile, var=var):
                found = []
                for line in range(lines):
                    at = pl.ds(t * lines + line, 1)
                    one, two = one_ref[tile, var, at, :], two_ref[tile, var, at, :]
                    found.append((jnp.where(odd, one, two), jnp.where(odd, two, one)))
                return found

            total = faces.volume(tile, var, wanted)
            faces.faces_x(tile, var, pace_x, total, rim)
            faces.faces_y(tile, var, pace_y, wanted, total)
            q, w = faces.reader(tile, var), faces.reader(tile, 2)
            store_rates(rate_ref, END_NODES, tile, var, count, total, q, w)
    me = lax.axis_index("span")
    parts = to_modes(dims, me, high_ref, low_ref, [rate_ref[var] for var in range(num_vars)])
    size = len(END_NODES) * share
    for k in range(span):
        if k % 2:
            odd_ref[pl.ds(k // 2 * size, size), :] = parts[k]
        else:
            evens[k // 2][...] = parts[k]


def put_back(nodes, share, elems, pick_ref, takes, flat):
    turned = pick_ref[...].T[:elems]
    pick = jnp.concatenate([turned] * (LANES // elems), axis=1).astype(jnp.bfloat16)
    for at in range(0, len(nodes), 2):
        columns = []
        for row in (at * share, (at + 1) * share):
            part = jnp.concatenate([take[pl.ds(row, share), :] for take in takes], axis=0)
            columns.append(jnp.concatenate(split(part), axis=0))
        moved = mm(pick, jnp.concatenate(columns, axis=1))
        flat[pl.ds(nodes[at], elems, stride=NODES), :] = moved[:, :LANES]
        flat[pl.ds(nodes[at + 1], elems, stride=NODES), :] = moved[:, LANES:]


def collect_kernel(dims, pick_ref, *refs):
    rows, cols, share, span, _ = dims
    put_back(MID_NODES, share, rows * cols, pick_ref, refs[:span], refs[span])


def finish_kernel(dims, pick_ref, state_ref, flat_in, *refs):
    rows, cols, share, span, modes = dims
    takes = unpaired(refs[: span // 2 + 1], len(END_NODES) * share)
    out_any, flat, out_ref, sems = refs[span // 2 + 1 :]
    elems = rows * cols
    count = span * modes
    put_back(END_NODES, share, elems, pick_ref, takes, flat)
    me = lax.axis_index("span")
    index = me * modes + lax.broadcasted_iota(jnp.int32, (LANES, 1), 0) % modes
    wave = jnp.where(index == 1, count // 2, index // 2).astype(jnp.float32)
    damping = 1.0 / (1.0 + TIME_STEP * VISCOSITY * wave * wave)
    copies = []
    for start in range(0, elems * NODES, CHUNK):
        for block in range(start, start + CHUNK, LANES):
            at = pl.ds(block, LANES)
            out_ref[:, at] = state_ref[:, at] * damping + flat[at, :].T
        at = pl.ds(start, CHUNK)
        copies.append(
            pltpu.make_async_copy(out_ref.at[:, at], out_any.at[:, at], sems.at[start // CHUNK])
        )
        copies[-1].start()
    for copy in copies:
        copy.wait()


def in_hbm(array):
    return pltpu.with_memory_space_constraint(array, pltpu.HBM)


def anywhere(count):
    return [pl.BlockSpec(memory_space=pltpu.HBM)] * count


def vmem(count):
    return [pl.BlockSpec(memory_space=pltpu.VMEM)] * count


PARAMS = pltpu.CompilerParams(vmem_limit_bytes=24 * 1024 * 1024)


def exchange(blocks, span):
    taken = {0: blocks[0]}
    for k in range(1, span):
        taken[k] = lax.ppermute(blocks[k], "span", [(s, s ^ k) for s in range(span)])
    return [taken[k] for k in range(span)]


def relayed(odds, evens, span):
    size = evens[0].shape[0]
    passed = lax.ppermute(odds, "span", [(s, s ^ 1) for s in range(span)])
    taken = [evens[0], passed[:size]]
    for at in range(1, span // 2):
        both = jnp.concatenate([evens[at], passed[at * size : (at + 1) * size]])
        both = lax.ppermute(both, "span", [(s, s ^ (2 * at)) for s in range(span)])
        taken.append(both)
    return taken


def ordered_body(state, metric, neighbour, wall, rim):
    num_vars, modes, flat_size = state.shape
    elems = flat_size // NODES
    span = lax.axis_size("span")
    groups = lax.axis_size("elem")
    share = elems // span
    rows = rim.shape[1]
    cols = elems // rows
    count = modes * span
    tiles = count // LANES
    lines = share // cols
    flat_state = state.reshape(num_vars * modes, flat_size)
    f32 = jnp.float32
    mid_part, end_part, rim_part, core_part = (
        jax.ShapeDtypeStruct((nodes * share, LANES), f32)
        for nodes in (len(MID_NODES), len(END_NODES), len(RIM_NODES) + SIDE, len(CORE_NODES))
    )
    chunks = flat_size // CHUNK
    first = pl.pallas_call(
        functools.partial(spread_kernel, (rows, cols, share, span)),
        out_shape=[rim_part] * span
        + [
            jax.ShapeDtypeStruct((elems, LANES), f32),
            jax.ShapeDtypeStruct((4, share, LANES), f32),
            jax.ShapeDtypeStruct((flat_size, LANES), f32),
        ],
        in_specs=anywhere(5),
        out_specs=vmem(span + 3),
        scratch_shapes=[
            pltpu.VMEM((4, elems, LANES), f32),
            pltpu.VMEM((elems, LANES), f32),
            pltpu.VMEM((2, elems, LANES), jnp.int32),
            pltpu.SMEM(neighbour.T.shape, jnp.int32),
            pltpu.SMEM(wall.T.shape, jnp.int32),
            pltpu.SMEM(rim.shape, jnp.int32),
            pltpu.SMEM(metric.shape, f32),
            pltpu.VMEM(flat_state.shape, f32),
            pltpu.SemaphoreType.DMA((4 + chunks,)),
        ],
        compiler_params=PARAMS,
        name="spread",
    )(*[in_hbm(x) for x in (neighbour.T, wall.T, rim, metric, flat_state)])
    rim_takes = exchange(first[:span], span)
    pick, facts, turned = first[span:]
    spread_core = pl.pallas_call(
        functools.partial(spread_core_kernel, share, span),
        out_shape=[jax.ShapeDtypeStruct((span // 2 * core_part.shape[0], LANES), f32)]
        + [core_part] * (span // 2),
        in_specs=vmem(2),
        out_specs=vmem(1 + span // 2),
        compiler_params=PARAMS,
        name="spread_core",
    )
    odds, *evens = spread_core(pick, turned)
    core_takes = relayed(odds, evens, span)

    dims = (cols, share, span, num_vars, modes)
    forward = [jnp.asarray(t) for t in forward_tables(count)]
    backward = [jnp.asarray(t) for t in backward_tables(count)]
    line_shape = jax.ShapeDtypeStruct((tiles, num_vars, SIDE * lines, LANES), f32)
    planes = pl.pallas_call(
        functools.partial(planes_kernel, dims),
        out_shape=[
            jax.ShapeDtypeStruct((tiles, num_vars, (len(RIM_NODES) + SIDE) * share, LANES), f32),
            line_shape,
            line_shape,
        ],
        in_specs=vmem(3 + span),
        out_specs=vmem(3),
        compiler_params=PARAMS,
        name="planes",
    )
    phys, one, two = planes(facts, *forward, *rim_takes)
    one = lax.ppermute(one, "elem", [(g, g ^ 1) for g in range(groups)])
    two = lax.ppermute(
        two, "elem", [(g, (g - 1 if g % 2 == 0 else g + 1) % groups) for g in range(groups)]
    )

    rates = pl.pallas_call(
        functools.partial(rates_kernel, dims),
        out_shape=[mid_part] * span
        + [jax.ShapeDtypeStruct((tiles, num_vars, len(CORE_NODES) * share, LANES), f32)],
        in_specs=vmem(7 + span // 2),
        out_specs=vmem(span + 1),
        scratch_shapes=[pltpu.VMEM((num_vars, len(MID_NODES) * share, 2 * count), f32)],
        compiler_params=PARAMS,
        name="rates",
    )
    *mids, core = rates(facts, *forward, *backward, phys, *core_takes)
    mid_takes = exchange(mids, span)
    edges = pl.pallas_call(
        functools.partial(edges_kernel, dims),
        out_shape=[jax.ShapeDtypeStruct((span // 2 * end_part.shape[0], LANES), f32)]
        + [end_part] * (span // 2),
        in_specs=vmem(7),
        out_specs=vmem(1 + span // 2),
        scratch_shapes=[pltpu.VMEM((num_vars, len(END_NODES) * share, 2 * count), f32)],
        compiler_params=PARAMS,
        name="edges",
    )
    odds, *evens = edges(facts, *backward, phys, core, one, two)
    end_takes = relayed(odds, evens, span)

    dims = (rows, cols, share, span, modes)
    flat_shape = jax.ShapeDtypeStruct((flat_size, LANES), f32)
    collect = pl.pallas_call(
        functools.partial(collect_kernel, dims),
        out_shape=flat_shape,
        in_specs=vmem(1 + span),
        out_specs=vmem(1)[0],
        compiler_params=PARAMS,
        name="collect",
    )
    flat = collect(pick, *mid_takes)
    out, _ = pl.pallas_call(
        functools.partial(finish_kernel, dims),
        out_shape=[jax.ShapeDtypeStruct(flat_state.shape, f32), flat_shape],
        in_specs=vmem(4 + span // 2),
        out_specs=anywhere(1) + vmem(1),
        scratch_shapes=[
            pltpu.VMEM(flat_state.shape, f32),
            pltpu.SemaphoreType.DMA((chunks,)),
        ],
        input_output_aliases={2: 1},
        compiler_params=PARAMS,
        name="finish",
    )(pick, flat_state, flat, *end_takes)
    return out.reshape(state.shape)


def from_behind(value, axis, steps):
    count = lax.axis_size(axis)
    pairs = [(source, (source + steps) % count) for source in range(count)]
    return lax.ppermute(value, axis, pairs)


def gll_tables():
    near_point = math.sqrt(1.0 / 3.0 - 2.0 * math.sqrt(7.0) / 21.0)
    far_point = math.sqrt(1.0 / 3.0 + 2.0 * math.sqrt(7.0) / 21.0)
    points = np.array([-1.0, -far_point, -near_point, near_point, far_point, 1.0])
    weights = np.array(
        [
            1.0
            / np.prod([points[column] - points[second] for second in range(6) if second != column])
            for column in range(6)
        ]
    )
    deriv = np.zeros((6, 6))
    for target in range(6):
        for source in range(6):
            if source != target:
                deriv[target, source] = (
                    weights[source] / weights[target] / (points[target] - points[source])
                )
        deriv[target, target] = -np.sum(deriv[target])
    identity = np.eye(6)
    along_x = np.kron(deriv, identity)
    along_y = np.kron(identity, deriv)
    edge_nodes = np.array(
        [
            [offset for offset in range(6)],
            [30 + offset for offset in range(6)],
            [6 * offset for offset in range(6)],
            [6 * offset + 5 for offset in range(6)],
        ]
    ).reshape(-1)
    lifting = np.zeros((36, 24))
    lifting[edge_nodes, np.arange(24)] = 1.0
    return (
        jnp.asarray(along_x, jnp.float32),
        jnp.asarray(along_y, jnp.float32),
        edge_nodes,
        jnp.asarray(lifting, jnp.float32),
    )


def spanwise_basis(count):
    mode_index = jnp.arange(count, dtype=jnp.int32)
    planes = jnp.arange(count, dtype=jnp.int32)
    phase = mode_index[:, None] // 2 * planes[None, :] % count
    phase_angle = phase.astype(jnp.float32) * (2.0 * math.pi / count)
    odd_rows = (mode_index % 2 == 1)[:, None]
    basis_table = jnp.where(odd_rows, jnp.sin(phase_angle), jnp.cos(phase_angle)) * math.sqrt(
        2.0 / count
    )
    alternate = (1 - 2 * (planes % 2)).astype(jnp.float32) / math.sqrt(count)
    constant = jnp.ones((count,), jnp.float32) / math.sqrt(count)
    basis_table = jnp.where(mode_index[:, None] == 0, constant[None, :], basis_table)
    basis_table = jnp.where(mode_index[:, None] == 1, alternate[None, :], basis_table)
    return basis_table


def spanwise_derivative(modal):
    shape_in = modal.shape
    paired = modal.reshape(shape_in[0], shape_in[1] // 2, 2, shape_in[2])
    wavenumber = jnp.arange(shape_in[1] // 2, dtype=jnp.int32).astype(jnp.float32)[None, :, None]
    return jnp.stack([wavenumber * paired[:, :, 1], -wavenumber * paired[:, :, 0]], axis=2).reshape(
        shape_in
    )


def planar_terms(flux_x, flux_y, metric_part):
    along_x, along_y, edge_nodes, _ = gll_tables()
    scale_x = metric_part[0][:, None]
    scale_y = metric_part[1][:, None]
    grad_x = jnp.einsum("pq,vmeq->vmep", along_x, flux_x, precision=HIGHEST)
    grad_y = jnp.einsum("pq,vmeq->vmep", along_y, flux_y, precision=HIGHEST)
    planar = scale_x * grad_x + scale_y * grad_y
    sign_x = jnp.sign(scale_x)
    sign_y = jnp.sign(scale_y)
    edge_flux = jnp.concatenate(
        [
            -sign_x * flux_x[:, :, :, edge_nodes[0:6]],
            sign_x * flux_x[:, :, :, edge_nodes[6:12]],
            -sign_y * flux_y[:, :, :, edge_nodes[12:18]],
            sign_y * flux_y[:, :, :, edge_nodes[18:24]],
        ],
        axis=3,
    )
    return (planar, edge_flux)


def node_major(flat, num_vars, local_modes, nodes, local_elems):
    return jnp.transpose(flat.reshape(num_vars, local_modes, local_elems, nodes), (0, 1, 3, 2))


def trace_pool(traces):
    shape_in = traces.shape
    return (
        traces.reshape(shape_in[0], shape_in[1], 4, 6, shape_in[3])
        .transpose(0, 1, 3, 4, 2)
        .reshape(shape_in[0], shape_in[1], 6, 4 * shape_in[3])
    )


def own_pools(state_local, normal_flux):
    edge_nodes = gll_tables()[2]
    return (trace_pool(state_local[:, :, edge_nodes, :]), trace_pool(normal_flux))


def update(
    state_local,
    divergence,
    own_q,
    own_flux,
    from_lower,
    from_upper,
    neighbour,
    orient,
    wall,
    metric_local,
    first_mode,
    total_modes,
):
    lifting = gll_tables()[3]
    num_vars, modes_here, _, count = state_local.shape
    pool_q = jnp.concatenate([own_q, from_lower[0], from_upper[0]], axis=3)
    pool_flux = jnp.concatenate([own_flux, from_lower[1], from_upper[1]], axis=3)
    flat_index = neighbour.reshape(-1)
    other_q = jnp.take(pool_q, flat_index, axis=3)
    other_flux = jnp.take(pool_flux, flat_index, axis=3)
    flipped = orient.reshape(-1) == 1
    other_q = jnp.where(flipped, other_q[:, :, ::-1, :], other_q)
    other_flux = jnp.where(flipped, other_flux[:, :, ::-1, :], other_flux)
    mirror = jnp.array([-1.0, -1.0, -1.0, 1.0], jnp.float32).reshape(4, 1, 1, 1)
    walled = wall.reshape(-1) == 1
    other_q = jnp.where(walled, mirror * own_q, other_q)
    other_flux = jnp.where(walled, mirror * own_flux, other_flux)
    magnitude = (
        jnp.abs(
            jnp.stack([metric_local[0], metric_local[0], metric_local[1], metric_local[1]], axis=1)
        ).reshape(-1)
        * 15.0
    )
    surface_jump = magnitude * (0.5 * (own_flux + other_flux) - 0.5 * PENALTY * (own_q - other_q))
    unpooled = (
        surface_jump.reshape(num_vars, modes_here, 6, count, 4)
        .transpose(0, 1, 4, 2, 3)
        .reshape(num_vars, modes_here, 24, count)
    )
    surface = jnp.einsum("pq,vmqe->vmpe", lifting, unpooled, precision=HIGHEST)
    mode_index = first_mode + jnp.arange(modes_here, dtype=jnp.int32)
    wavenumber = jnp.where(mode_index == 1, total_modes // 2, mode_index // 2).astype(jnp.float32)
    damping = 1.0 + TIME_STEP * VISCOSITY * wavenumber * wavenumber
    return (state_local + TIME_STEP * (surface - divergence)) / damping[None, :, None, None]


def plain_body(state, metric, neighbour, orient, wall, rim):
    num_vars, local_modes, flat_size = state.shape
    num_nodes = 36
    local_elems = flat_size // num_nodes
    span_size = lax.axis_size("span")
    total_modes = local_modes * span_size
    share = local_elems // span_size
    state_nodes = node_major(state, num_vars, local_modes, num_nodes, local_elems)
    planes_in = lax.all_to_all(state, "span", split_axis=2, concat_axis=1, tiled=True)
    basis_table = spanwise_basis(total_modes)
    physical = jnp.einsum("mn,vmk->vnk", basis_table, planes_in, precision=HIGHEST)
    metric_part = lax.dynamic_slice_in_dim(metric, lax.axis_index("span") * share, share, axis=1)
    shape_here = (num_vars, total_modes, share, num_nodes)
    planar_div, edge_flux = planar_terms(
        (physical[0:1] * physical).reshape(shape_here),
        (physical[1:2] * physical).reshape(shape_here),
        metric_part,
    )
    volume_fields = jnp.concatenate(
        [planar_div.reshape(num_vars, total_modes, share * num_nodes), physical[2:3] * physical],
        axis=0,
    )
    volume_modal = jnp.einsum("mn,vnk->vmk", basis_table, volume_fields, precision=HIGHEST)
    edge_modal = jnp.einsum(
        "mn,vnk->vmk",
        basis_table,
        edge_flux.reshape(num_vars, total_modes, share * 24),
        precision=HIGHEST,
    )
    combined = volume_modal[0:4] + spanwise_derivative(volume_modal[4:8])
    div_flat, flux_flat = (
        lax.all_to_all(combined, "span", split_axis=1, concat_axis=2, tiled=True),
        lax.all_to_all(edge_modal, "span", split_axis=1, concat_axis=2, tiled=True),
    )
    divergence = node_major(div_flat, num_vars, local_modes, num_nodes, local_elems)
    normal_flux = node_major(flux_flat, num_vars, local_modes, 24, local_elems)
    own_q, own_flux = own_pools(state_nodes, normal_flux)
    upper_rim = jnp.stack([jnp.take(own_q, rim[1], axis=3), jnp.take(own_flux, rim[1], axis=3)])
    lower_rim = jnp.stack([jnp.take(own_q, rim[0], axis=3), jnp.take(own_flux, rim[0], axis=3)])
    from_lower = from_behind(upper_rim, "elem", 1)
    from_upper = from_behind(lower_rim, "elem", -1)
    first_mode = lax.axis_index("span") * local_modes
    result = update(
        state_nodes,
        divergence,
        own_q,
        own_flux,
        from_lower,
        from_upper,
        neighbour,
        orient,
        wall,
        metric,
        first_mode,
        total_modes,
    )
    return jnp.transpose(result, (0, 1, 3, 2)).reshape(num_vars, local_modes, flat_size)


def body(state, metric, neighbour, orient, wall, rim):
    num_vars, modes, flat_size = state.shape
    span = lax.axis_size("span")
    groups = lax.axis_size("elem")
    elems = flat_size // NODES
    rows = rim.shape[1]
    fits = (
        groups % 2 == 0
        and rows % span == 0
        and SUB == 2 * (elems // rows)
        and num_vars * modes == LANES
        and modes * 4 == LANES
        and span % 4 == 0
        and span & (span - 1) == 0
        and LANES % elems == 0
        and elems == SUB * span
        and elems % rows == 0
        and SUB % (elems // rows) == 0
        and flat_size % CHUNK == 0
    )
    if not fits:
        return plain_body(state, metric, neighbour, orient, wall, rim)
    return ordered_body(state, metric, neighbour, wall, rim)


def solution(mesh):
    placed = (
        P(None, "span", "elem"),
        P(None, "elem"),
        P("elem", None),
        P("elem", None),
        P("elem", None),
        P(None, "elem"),
    )
    return jax.shard_map(
        body, mesh=mesh, in_specs=placed, out_specs=P(None, "span", "elem"), check_vma=False
    )
```

```python
import functools
import math

import jax
import jax.numpy as jnp
import numpy as np
from jax import lax
from jax.experimental import pallas as pl
from jax.experimental.pallas import tpu as pltpu
from jax.sharding import PartitionSpec as P


TIME_STEP = 0.001
VISCOSITY = 0.02
PENALTY = 1.0
HIGHEST = lax.Precision.HIGHEST
SIDE = 6
NODES = SIDE * SIDE
LANES = 128
SUB = 8
CHUNK = 3 * LANES
RIM_NODES = [p for p in range(NODES) if p // SIDE in (0, 5) or p % SIDE in (0, 5)]
CORE_NODES = [p for p in range(NODES) if p not in RIM_NODES]
MID_NODES = [p for p in range(NODES) if p // SIDE not in (0, 5)]
END_NODES = [p for p in range(NODES) if p // SIDE in (0, 5)]


def gll_matrix():
    near_point = math.sqrt(1.0 / 3.0 - 2.0 * math.sqrt(7.0) / 21.0)
    far_point = math.sqrt(1.0 / 3.0 + 2.0 * math.sqrt(7.0) / 21.0)
    points = np.array([-1.0, -far_point, -near_point, near_point, far_point, 1.0])
    weights = np.array(
        [
            1.0
            / np.prod([points[column] - points[second] for second in range(6) if second != column])
            for column in range(6)
        ]
    )
    deriv = np.zeros((6, 6))
    for target in range(6):
        for source in range(6):
            if source != target:
                deriv[target, source] = (
                    weights[source] / weights[target] / (points[target] - points[source])
                )
        deriv[target, target] = -np.sum(deriv[target])
    return deriv


def basis_matrix(count):
    mode = np.arange(count)[:, None]
    plane = np.arange(count)[None, :]
    angle = (mode // 2 * plane % count) * (2.0 * math.pi / count)
    table = np.where(mode % 2 == 1, np.sin(angle), np.cos(angle)) * math.sqrt(2.0 / count)
    table = np.where(mode == 0, 1.0 / math.sqrt(count), table)
    return np.where(mode == 1, (1.0 - 2.0 * (plane % 2)) / math.sqrt(count), table)


def halves(table):
    table = np.asarray(table, np.float32)
    high = table.astype(jnp.bfloat16)
    low = (table - high.astype(np.float32)).astype(jnp.bfloat16)
    return high, low


def forward_tables(count):
    return halves(basis_matrix(count))


def backward_tables(count):
    basis = basis_matrix(count)
    wave = np.arange(count) // 2
    swapped = np.empty_like(basis)
    swapped[0::2] = wave[0::2, None] * basis[1::2]
    swapped[1::2] = -wave[1::2, None] * basis[0::2]
    damp_wave = np.where(np.arange(count) == 1, count // 2, wave).astype(np.float64)
    factor = TIME_STEP / (1.0 + TIME_STEP * VISCOSITY * damp_wave * damp_wave)
    return halves(factor[:, None] * np.concatenate([basis, -swapped], axis=1))


def split(value):
    high = value.astype(jnp.bfloat16)
    low = (value - high.astype(jnp.float32)).astype(jnp.bfloat16)
    return high, low


def mm(a, b):
    return lax.dot_general(a, b, (((1,), (0,)), ((), ())), preferred_element_type=jnp.float32)


def mm_nt(a, b):
    return lax.dot_general(a, b, (((1,), (1,)), ((), ())), preferred_element_type=jnp.float32)


def regroup(parts, lane):
    quarter = LANES // 4
    low_half = lane < 2 * quarter
    rolled = [pltpu.roll(part, 2 * quarter, 1) for part in parts]
    first = [
        jnp.where(low_half, parts[0], rolled[2]),
        jnp.where(low_half, parts[1], rolled[3]),
        jnp.where(low_half, rolled[0], parts[2]),
        jnp.where(low_half, rolled[1], parts[3]),
    ]
    even = lane // quarter % 2 == 0
    out = []
    for pair in (0, 2):
        a, b = first[pair], first[pair + 1]
        out.append(jnp.where(even, a, pltpu.roll(b, quarter, 1)))
        out.append(jnp.where(even, pltpu.roll(a, LANES - quarter, 1), b))
    return out


def move_nodes(nodes, elems, flat, pick, pick_sides, put):
    for at in range(0, len(nodes), 2):
        pair = nodes[at : at + 2]
        columns = [
            jnp.concatenate(split(flat[pl.ds(node, elems, stride=NODES), :]), axis=0)
            for node in pair
        ]
        chosen = pick_sides if any(node % SIDE in (0, 5) for node in pair) else pick
        moved = mm(chosen, jnp.concatenate(columns, axis=1))
        for half, node in enumerate(pair):
            put(at + half, node, moved[:, half * LANES : (half + 1) * LANES])


def spread_kernel(dims, near_any, wall_any, rim_any, metric_any, state_any, *refs):
    rows, cols, share, span = dims
    sends = refs[:span]
    pick_ref, facts_ref, flat, all_ref = refs[span : span + 4]
    halo_ref, bends_ref, near_ref, wall_ref, rim_ref, metric_ref, state_ref, sems = refs[span + 4 :]
    me = lax.axis_index("span")
    elems = rows * cols
    width = elems * NODES
    small = [
        pltpu.make_async_copy(source, target, sems.at[at])
        for at, (source, target) in enumerate(
            (
                (near_any, near_ref),
                (wall_any, wall_ref),
                (rim_any, rim_ref),
                (metric_any, metric_ref),
            )
        )
    ]
    large = [
        pltpu.make_async_copy(
            state_any.at[:, pl.ds(at, CHUNK)],
            state_ref.at[:, pl.ds(at, CHUNK)],
            sems.at[len(small) + at // CHUNK],
        )
        for at in range(0, width, CHUNK)
    ]
    for copy in small + large:
        copy.start()
    for copy in small:
        copy.wait()
    lane = lax.broadcasted_iota(jnp.int32, (1, LANES), 1) % elems
    lines = share // cols
    halo_ref[...] = jnp.zeros_like(halo_ref)
    bends_ref[...] = jnp.zeros_like(bends_ref)
    before = None
    for row in range(rows):
        cell = rim_ref[0, row] >> 2
        face = rim_ref[0, row] & 1
        here = []
        for col in range(cols):
            if row == 0:
                flip_y = wall_ref[3, cell]
            else:
                flip_y = jnp.where(near_ref[3, cell] >> 2 == before[col], 1, 0)
            here.append(cell)
            place = row * cols + col
            at = (place // share ^ me) * share + place % share
            chosen = jnp.where(lane == cell, 1.0, 0.0)
            pick_ref[pl.ds(at, 1), :] = chosen
            block, line = divmod(row, lines)
            if block % 2 and line == lines - 1 and block + 1 < rows // lines:
                far, bends = (block + 1) ^ me, (face, 1 - flip_y)
            elif block % 2 == 0 and line == 0 and block > 0:
                far, bends = (block - 1) ^ me, (face, flip_y)
            else:
                far = None
            for half in (0, cols) if far is not None else ():
                place_at = far * share + half + col
                halo_ref[pl.ds(place_at, 1), :] = chosen
                for kind, bend in enumerate(bends):
                    bends_ref[kind, pl.ds(place_at, 1), :] = jnp.full((1, LANES), bend, jnp.int32)
            facts = (
                metric_ref[0, cell],
                metric_ref[1, cell],
                face.astype(jnp.float32),
                flip_y.astype(jnp.float32),
            )
            for kind, fact in enumerate(facts):
                all_ref[kind, pl.ds(at, 1), :] = jnp.full((1, LANES), fact, jnp.float32)
            if col + 1 < cols:
                step = near_ref[face ^ 1, cell]
                cell = step >> 2
                face = step & 1
        before = here
    for at in range(0, width, LANES):
        if at % CHUNK == 0:
            large[at // CHUNK].wait()
        flat[pl.ds(at, LANES), :] = state_ref[:, pl.ds(at, LANES)].T
    facts_ref[...] = all_ref[:, :share]
    pick = pick_ref[...].astype(jnp.bfloat16)
    both = jnp.concatenate([pick, halo_ref[...].astype(jnp.bfloat16)], axis=0)
    edge = {}

    def put(at, node, mine):
        if node % SIDE in (0, 5):
            edge[divmod(node, SIDE)] = mine[elems:]
        for step in range(span):
            sends[step][pl.ds(at * share, share), :] = mine[step * share : (step + 1) * share]

    move_nodes(RIM_NODES, elems, flat, pick, both, put)
    bend_x = bends_ref[0] == 1
    bend_y = bends_ref[1] == 1
    trace = [jnp.where(bend_y, edge[t, 5], edge[t, 0]) for t in range(SIDE)]
    upper = lax.broadcasted_iota(jnp.int32, (elems, LANES), 0) % share < cols
    for t in range(0, SIDE, 2):
        one, two = (jnp.where(bend_x, trace[SIDE - 1 - s], trace[s]) for s in (t, t + 1))
        moved = jnp.where(upper, one, two)
        at = pl.ds(len(RIM_NODES) * share + t * cols, share)
        for step in range(span):
            sends[step][at, :] = moved[step * share : (step + 1) * share]


def spread_core_kernel(share, span, pick_ref, flat, odd_ref, *evens):
    pick = pick_ref[...].astype(jnp.bfloat16)
    size = len(CORE_NODES) * share

    def put(at, node, mine):
        for step in range(span):
            value = mine[step * share : (step + 1) * share]
            if step % 2:
                odd_ref[pl.ds(step // 2 * size + at * share, share), :] = value
            else:
                evens[step // 2][pl.ds(at * share, share), :] = value

    move_nodes(CORE_NODES, pick.shape[0], flat, pick, pick, put)


def along(trace, flip):
    return {t: jnp.where(flip, trace[SIDE - 1 - t], trace[t]) for t in trace}


def sides_x(value, flip_x, flip_y):
    low = {t: jnp.where(flip_x, value(5, t), value(0, t)) for t in range(SIDE)}
    high = {t: jnp.where(flip_x, value(0, t), value(5, t)) for t in range(SIDE)}
    return along(low, flip_y), along(high, flip_y)


def sides_y(value, flip_x, flip_y, wanted):
    low = {t: jnp.where(flip_y, value(t, 5), value(t, 0)) for t in wanted}
    high = {t: jnp.where(flip_y, value(t, 0), value(t, 5)) for t in wanted}
    return along(low, flip_x), along(high, flip_x)


def rim_reader(ref, tile, var):
    return lambda i, j: ref[tile, var, pl.ds(RIM_NODES.index(SIDE * i + j) * SUB, SUB), :]


def back(one, two, flip, flip_along):
    return along({t: jnp.where(flip, two[t], one[t]) for t in one}, flip_along)


def sign(value):
    return jnp.where(value < 0.0, -1.0, 1.0)


def to_planes(dims, me, high_ref, low_ref, takes, phys_ref):
    _, _, span, num_vars, modes = dims
    lane = lax.broadcasted_iota(jnp.int32, (1, LANES), 1)
    tables = []
    for ref in (high_ref, low_ref):
        tables.append(
            jnp.concatenate([ref[pl.ds((me ^ k) * modes, modes), :] for k in range(span)], axis=0)
        )
    pieces = []
    for group in range(span // 4):
        pieces.append(regroup([takes[4 * group + q][...] for q in range(4)], lane))
    stack = [jnp.concatenate([piece[var] for piece in pieces], axis=1) for var in range(num_vars)]
    high, low = split(jnp.concatenate(stack, axis=0))
    planes = mm(high, tables[0]) + mm(low, tables[0]) + mm(high, tables[1])
    size = takes[0].shape[0]
    for var in range(num_vars):
        for tile in range(span * modes // LANES):
            phys_ref[tile, var] = planes[
                var * size : (var + 1) * size, tile * LANES : (tile + 1) * LANES
            ]


def planes_kernel(dims, facts_ref, high_ref, low_ref, *refs):
    cols, share, span, num_vars, modes = dims
    takes = refs[:span]
    phys_ref, twin_ref, one_ref, two_ref = refs[span:]
    to_planes(dims, lax.axis_index("span"), high_ref, low_ref, takes, phys_ref)
    odd = lax.axis_index("elem") % 2 == 1
    lines = share // cols
    flip_x = facts_ref[2] > 0.5
    flip_y = facts_ref[3] > 0.5
    turn_x = sign(facts_ref[0]) * (1.0 - 2.0 * facts_ref[2])
    second = lax.axis_index("span") % 2 == 1
    turn_y = sign(facts_ref[1]) * (1.0 - 2.0 * facts_ref[3])
    turn_y = jnp.where(second, -turn_y, turn_y)
    inner = jnp.where(second, 1.0 - facts_ref[3], facts_ref[3]) > 0.5

    def toward_twin(value):
        return along({t: jnp.where(inner, value(t, 0), value(t, 5)) for t in range(SIDE)}, flip_x)

    for tile in range(span * modes // LANES):
        speed = sides_x(rim_reader(phys_ref, tile, 0), flip_x, flip_y)
        pace = toward_twin(rim_reader(phys_ref, tile, 1))
        pace = {t: 1.0 + turn_y * pace[t] for t in pace}
        for var in range(num_vars):
            trace = toward_twin(rim_reader(phys_ref, tile, var))
            for t in range(SIDE):
                give = pace[t] * trace[t]
                at = pl.ds(t * cols, cols)
                twin_ref[tile, var, at, :] = jnp.where(second, give[:cols], give[share - cols :])
            trace = sides_x(rim_reader(phys_ref, tile, var), flip_x, flip_y)
            for t in range(SIDE):
                low_x = (1.0 - turn_x * speed[0][t]) * trace[0][t]
                high_x = (1.0 + turn_x * speed[1][t]) * trace[1][t]
                for line in range(lines):
                    at = pl.ds(t * lines + line, 1)
                    up = high_x[(line + 1) * cols - 1 : (line + 1) * cols]
                    down = low_x[line * cols : line * cols + 1]
                    one_ref[tile, var, at, :] = jnp.where(odd, down, up)
                    two_ref[tile, var, at, :] = jnp.where(odd, up, down)


def to_modes(dims, me, high_ref, low_ref, rates):
    _, _, span, num_vars, modes = dims
    lane = lax.broadcasted_iota(jnp.int32, (1, LANES), 1)
    tables = []
    for ref in (high_ref, low_ref):
        tables.append(
            jnp.concatenate([ref[pl.ds((me ^ k) * modes, modes), :] for k in range(span)], axis=0)
        )
    size = rates[0].shape[0]
    high, low = split(jnp.concatenate(rates, axis=0))
    gain = mm_nt(high, tables[0]) + mm_nt(low, tables[0]) + mm_nt(high, tables[1])
    gains = [gain[var * size : (var + 1) * size] for var in range(num_vars)]
    out = []
    for group in range(span // 4):
        at = slice(group * LANES, (group + 1) * LANES)
        out += regroup([gain[:, at] for gain in gains], lane)
    return out


def derivative(values, wanted=tuple(range(SIDE))):
    deriv = gll_matrix()
    last = SIDE - 1
    plus = [values[j] + values[last - j] for j in range(SIDE // 2)]
    minus = [values[j] - values[last - j] for j in range(SIDE // 2)]
    out = [None] * SIDE
    for i in range(SIDE // 2):
        if i not in wanted:
            continue
        even, odd = None, None
        for j in range(SIDE // 2):
            a = minus[j] * float(0.5 * (deriv[i, j] - deriv[i, last - j]))
            b = plus[j] * float(0.5 * (deriv[i, j] + deriv[i, last - j]))
            even = a if even is None else even + a
            odd = b if odd is None else odd + b
        out[i] = even + odd
        out[last - i] = even - odd
    return out


class Faces:
    def __init__(self, dims, facts_ref, phys_ref, core_ref, twin_ref):
        cols, share, span, self.num_vars, modes = dims
        self.cols = cols
        self.phys_ref, self.core_ref, self.twin_ref = phys_ref, core_ref, twin_ref
        me = lax.axis_index("span")
        slot = lax.broadcasted_iota(jnp.int32, (SUB, LANES), 0)
        self.slot = slot
        self.flip_x = facts_ref[2] > 0.5
        self.flip_y = facts_ref[3] > 0.5
        self.scale_x = -facts_ref[0]
        self.scale_y = facts_ref[1]
        self.turn_x = sign(facts_ref[0]) * (1.0 - 2.0 * facts_ref[2])
        self.turn_y = sign(facts_ref[1]) * (1.0 - 2.0 * facts_ref[3])
        self.weight_x = 7.5 * jnp.abs(facts_ref[0])
        self.weight_y = 7.5 * jnp.abs(facts_ref[1])
        self.first_line = slot < cols
        self.turn_halo = jnp.where(self.first_line, self.turn_y, -self.turn_y)
        self.far = slot // cols == me % 2
        self.floor = jnp.logical_and(self.first_line, me == 0)
        self.roof = jnp.logical_and(jnp.logical_not(self.first_line), me == span - 1)

    def reader(self, tile, var):
        def read(i, j):
            node = SIDE * i + j
            ref = self.phys_ref if node in RIM_NODES else self.core_ref
            nodes = RIM_NODES if node in RIM_NODES else CORE_NODES
            return ref[tile, var, pl.ds(nodes.index(node) * SUB, SUB), :]

        return read

    def volume(self, tile, var, wanted):
        q, u, v = (self.reader(tile, at) for at in (var, 0, 1))
        total = {}
        for j in range(SIDE):
            slope = derivative([q(i, j) * u(i, j) for i in range(SIDE)], wanted)
            for i in wanted:
                total[i, j] = self.scale_x * slope[i]
        for i in wanted:
            slope = derivative([q(i, j) * v(i, j) for j in range(SIDE)])
            for j in range(SIDE):
                total[i, j] = total[i, j] - self.scale_y * slope[j]
        return total

    def pace_y(self, tile, wanted):
        speed = sides_y(self.reader(tile, 1), self.flip_x, self.flip_y, wanted)
        return [{t: self.turn_y * side[t] for t in wanted} for side in speed]

    def twice(self, ref, tile, var, at):
        row = ref[tile, var, pl.ds(at, self.cols), :]
        return jnp.concatenate([row] * (SUB // self.cols), axis=0)

    def far_row(self, tile, var, t):
        return self.twice(self.phys_ref, tile, var, len(RIM_NODES) * SUB + t * self.cols)

    def twin_row(self, tile, var, t):
        return self.twice(self.twin_ref, tile, var, t * self.cols)

    def far_pace(self, tile, wanted):
        return {t: 1.0 + self.turn_halo * self.far_row(tile, 1, t) for t in wanted}

    def faces_y(self, tile, var, pace, far_pace, wanted, total):
        mirror = 1.0 if var == self.num_vars - 1 else -1.0
        trace = sides_y(self.reader(tile, var), self.flip_x, self.flip_y, wanted)
        low, high = {}, {}
        for t in wanted:
            speed, value = pace[0][t], trace[0][t]
            own_low, give_low = -(speed + 1.0) * value, (1.0 - speed) * value
            speed, value = pace[1][t], trace[1][t]
            own_high, give_high = (speed - 1.0) * value, (1.0 + speed) * value
            outside = jnp.where(
                self.far, far_pace[t] * self.far_row(tile, var, t), self.twin_row(tile, var, t)
            )
            outside = jnp.where(self.floor, mirror * give_low, outside)
            outside = jnp.where(self.roof, mirror * give_high, outside)
            from_low = jnp.where(self.first_line, outside, pltpu.roll(give_high, self.cols, 0))
            from_high = jnp.where(
                self.first_line, pltpu.roll(give_low, SUB - self.cols, 0), outside
            )
            low[t] = self.weight_y * (own_low + from_low)
            high[t] = self.weight_y * (own_high + from_high)
        for j, one, two in ((0, low, high), (5, high, low)):
            side = back(one, two, self.flip_y, self.flip_x)
            for t in wanted:
                total[t, j] = total[t, j] + side[t]

    def pace_x(self, tile):
        speed = sides_x(self.reader(tile, 0), self.flip_x, self.flip_y)
        return [{t: self.turn_x * side[t] for t in side} for side in speed]

    def faces_x(self, tile, var, pace, total, rim):
        trace = sides_x(self.reader(tile, var), self.flip_x, self.flip_y)
        low, high = {}, {}
        for t in range(SIDE):
            speed, value = pace[0][t], trace[0][t]
            own_low, give_low = -(speed + 1.0) * value, (1.0 - speed) * value
            speed, value = pace[1][t], trace[1][t]
            own_high, give_high = (speed - 1.0) * value, (1.0 + speed) * value
            from_low, from_high = pltpu.roll(give_high, 1, 0), pltpu.roll(give_low, SUB - 1, 0)
            for line, (below, above) in enumerate(rim(t)):
                from_low = jnp.where(self.slot == line * self.cols, below, from_low)
                from_high = jnp.where(self.slot == (line + 1) * self.cols - 1, above, from_high)
            low[t] = self.weight_x * (own_low + from_low)
            high[t] = self.weight_x * (own_high + from_high)
        for i, one, two in ((0, low, high), (5, high, low)):
            side = back(one, two, self.flip_x, self.flip_y)
            for t in range(SIDE):
                total[i, t] = total[i, t] + side[t]


def unpaired(refs, size):
    takes = list(refs[:2])
    for ref in refs[2:]:
        takes += [ref.at[:size], ref.at[size:]]
    return takes


def store_rates(rate_ref, nodes, tile, var, count, total, q, w):
    for place, node in enumerate(nodes):
        i, j = divmod(node, SIDE)
        at = pl.ds(place * SUB, SUB)
        rate_ref[var, at, pl.ds(tile * LANES, LANES)] = total[i, j]
        rate_ref[var, at, pl.ds(count + tile * LANES, LANES)] = q(i, j) * w(i, j)


def rates_kernel(
    dims, facts_ref, there_high, there_low, high_ref, low_ref, phys_ref, twin_ref, *refs
):
    _, share, span, num_vars, modes = dims
    half = span // 2
    outs = refs[half + 1 : half + 1 + span]
    core_ref, rate_ref = refs[half + 1 + span :]
    takes = unpaired(refs[: half + 1], len(CORE_NODES) * share)
    me = lax.axis_index("span")
    to_planes(dims, me, there_high, there_low, takes, core_ref)
    count = span * modes
    faces = Faces(dims, facts_ref, phys_ref, core_ref, twin_ref)
    wanted = tuple(range(1, SIDE - 1))
    for tile in range(count // LANES):
        pace, far_pace = faces.pace_y(tile, wanted), faces.far_pace(tile, wanted)
        for var in range(num_vars):
            total = faces.volume(tile, var, wanted)
            faces.faces_y(tile, var, pace, far_pace, wanted, total)
            q, w = faces.reader(tile, var), faces.reader(tile, 2)
            store_rates(rate_ref, MID_NODES, tile, var, count, total, q, w)
    parts = to_modes(dims, me, high_ref, low_ref, [rate_ref[var] for var in range(num_vars)])
    for k in range(span):
        outs[k][...] = parts[k]


def edges_kernel(
    dims, facts_ref, high_ref, low_ref, phys_ref, core_ref, twin_ref, one_ref, two_ref, *refs
):
    cols, share, span, num_vars, modes = dims
    odd_ref, *evens, rate_ref = refs
    count = span * modes
    lines = share // cols
    odd = lax.axis_index("elem") % 2 == 1
    faces = Faces(dims, facts_ref, phys_ref, core_ref, twin_ref)
    wanted = (0, SIDE - 1)
    for tile in range(count // LANES):
        pace_x, pace_y = faces.pace_x(tile), faces.pace_y(tile, wanted)
        far_pace = faces.far_pace(tile, wanted)
        for var in range(num_vars):

            def rim(t, tile=tile, var=var):
                found = []
                for line in range(lines):
                    at = pl.ds(t * lines + line, 1)
                    one, two = one_ref[tile, var, at, :], two_ref[tile, var, at, :]
                    found.append((jnp.where(odd, one, two), jnp.where(odd, two, one)))
                return found

            total = faces.volume(tile, var, wanted)
            faces.faces_x(tile, var, pace_x, total, rim)
            faces.faces_y(tile, var, pace_y, far_pace, wanted, total)
            q, w = faces.reader(tile, var), faces.reader(tile, 2)
            store_rates(rate_ref, END_NODES, tile, var, count, total, q, w)
    me = lax.axis_index("span")
    parts = to_modes(dims, me, high_ref, low_ref, [rate_ref[var] for var in range(num_vars)])
    size = len(END_NODES) * share
    for k in range(span):
        if k % 2:
            odd_ref[pl.ds(k // 2 * size, size), :] = parts[k]
        else:
            evens[k // 2][...] = parts[k]


def put_back(nodes, share, elems, pick_ref, takes, flat):
    turned = pick_ref[...].T[:elems]
    pick = jnp.concatenate([turned] * (LANES // elems), axis=1).astype(jnp.bfloat16)
    for at in range(0, len(nodes), 2):
        columns = []
        for row in (at * share, (at + 1) * share):
            part = jnp.concatenate([take[pl.ds(row, share), :] for take in takes], axis=0)
            columns.append(jnp.concatenate(split(part), axis=0))
        moved = mm(pick, jnp.concatenate(columns, axis=1))
        flat[pl.ds(nodes[at], elems, stride=NODES), :] = moved[:, :LANES]
        flat[pl.ds(nodes[at + 1], elems, stride=NODES), :] = moved[:, LANES:]


def collect_kernel(dims, pick_ref, *refs):
    rows, cols, share, span, _ = dims
    put_back(MID_NODES, share, rows * cols, pick_ref, refs[:span], refs[span])


def finish_kernel(dims, pick_ref, state_ref, flat_in, *refs):
    rows, cols, share, span, modes = dims
    takes = unpaired(refs[: span // 2 + 1], len(END_NODES) * share)
    out_any, flat, out_ref, sems = refs[span // 2 + 1 :]
    elems = rows * cols
    count = span * modes
    put_back(END_NODES, share, elems, pick_ref, takes, flat)
    me = lax.axis_index("span")
    index = me * modes + lax.broadcasted_iota(jnp.int32, (LANES, 1), 0) % modes
    wave = jnp.where(index == 1, count // 2, index // 2).astype(jnp.float32)
    damping = 1.0 / (1.0 + TIME_STEP * VISCOSITY * wave * wave)
    copies = []
    for start in range(0, elems * NODES, CHUNK):
        for block in range(start, start + CHUNK, LANES):
            at = pl.ds(block, LANES)
            out_ref[:, at] = state_ref[:, at] * damping + flat[at, :].T
        at = pl.ds(start, CHUNK)
        copies.append(
            pltpu.make_async_copy(out_ref.at[:, at], out_any.at[:, at], sems.at[start // CHUNK])
        )
        copies[-1].start()
    for copy in copies:
        copy.wait()


def in_hbm(array):
    return pltpu.with_memory_space_constraint(array, pltpu.HBM)


def anywhere(count):
    return [pl.BlockSpec(memory_space=pltpu.HBM)] * count


def vmem(count):
    return [pl.BlockSpec(memory_space=pltpu.VMEM)] * count


PARAMS = pltpu.CompilerParams(vmem_limit_bytes=24 * 1024 * 1024)


def exchange(blocks, span):
    taken = {0: blocks[0]}
    for k in range(1, span):
        taken[k] = lax.ppermute(blocks[k], "span", [(s, s ^ k) for s in range(span)])
    return [taken[k] for k in range(span)]


def relayed(odds, evens, span):
    size = evens[0].shape[0]
    passed = lax.ppermute(odds, "span", [(s, s ^ 1) for s in range(span)])
    taken = [evens[0], passed[:size]]
    for at in range(1, span // 2):
        both = jnp.concatenate([evens[at], passed[at * size : (at + 1) * size]])
        both = lax.ppermute(both, "span", [(s, s ^ (2 * at)) for s in range(span)])
        taken.append(both)
    return taken


def ordered_body(state, metric, neighbour, wall, rim):
    num_vars, modes, flat_size = state.shape
    elems = flat_size // NODES
    span = lax.axis_size("span")
    groups = lax.axis_size("elem")
    share = elems // span
    rows = rim.shape[1]
    cols = elems // rows
    count = modes * span
    tiles = count // LANES
    lines = share // cols
    flat_state = state.reshape(num_vars * modes, flat_size)
    f32 = jnp.float32
    mid_part, end_part, rim_part, core_part = (
        jax.ShapeDtypeStruct((nodes * share, LANES), f32)
        for nodes in (len(MID_NODES), len(END_NODES), len(RIM_NODES) + SIDE // 2, len(CORE_NODES))
    )
    chunks = flat_size // CHUNK
    first = pl.pallas_call(
        functools.partial(spread_kernel, (rows, cols, share, span)),
        out_shape=[rim_part] * span
        + [
            jax.ShapeDtypeStruct((elems, LANES), f32),
            jax.ShapeDtypeStruct((4, share, LANES), f32),
            jax.ShapeDtypeStruct((flat_size, LANES), f32),
        ],
        in_specs=anywhere(5),
        out_specs=vmem(span + 3),
        scratch_shapes=[
            pltpu.VMEM((4, elems, LANES), f32),
            pltpu.VMEM((elems, LANES), f32),
            pltpu.VMEM((2, elems, LANES), jnp.int32),
            pltpu.SMEM(neighbour.T.shape, jnp.int32),
            pltpu.SMEM(wall.T.shape, jnp.int32),
            pltpu.SMEM(rim.shape, jnp.int32),
            pltpu.SMEM(metric.shape, f32),
            pltpu.VMEM(flat_state.shape, f32),
            pltpu.SemaphoreType.DMA((4 + chunks,)),
        ],
        compiler_params=PARAMS,
        name="spread",
    )(*[in_hbm(x) for x in (neighbour.T, wall.T, rim, metric, flat_state)])
    rim_takes = exchange(first[:span], span)
    pick, facts, turned = first[span:]
    spread_core = pl.pallas_call(
        functools.partial(spread_core_kernel, share, span),
        out_shape=[jax.ShapeDtypeStruct((span // 2 * core_part.shape[0], LANES), f32)]
        + [core_part] * (span // 2),
        in_specs=vmem(2),
        out_specs=vmem(1 + span // 2),
        compiler_params=PARAMS,
        name="spread_core",
    )
    odds, *evens = spread_core(pick, turned)
    core_takes = relayed(odds, evens, span)

    dims = (cols, share, span, num_vars, modes)
    forward = [jnp.asarray(t) for t in forward_tables(count)]
    backward = [jnp.asarray(t) for t in backward_tables(count)]
    line_shape = jax.ShapeDtypeStruct((tiles, num_vars, SIDE * lines, LANES), f32)
    planes = pl.pallas_call(
        functools.partial(planes_kernel, dims),
        out_shape=[
            jax.ShapeDtypeStruct((tiles, num_vars, rim_part.shape[0], LANES), f32),
            jax.ShapeDtypeStruct((tiles, num_vars, SIDE * cols, LANES), f32),
            line_shape,
            line_shape,
        ],
        in_specs=vmem(3 + span),
        out_specs=vmem(4),
        compiler_params=PARAMS,
        name="planes",
    )
    phys, twin, one, two = planes(facts, *forward, *rim_takes)
    twin = lax.ppermute(twin, "span", [(s, s ^ 1) for s in range(span)])
    one = lax.ppermute(one, "elem", [(g, g ^ 1) for g in range(groups)])
    two = lax.ppermute(
        two, "elem", [(g, (g - 1 if g % 2 == 0 else g + 1) % groups) for g in range(groups)]
    )

    rates = pl.pallas_call(
        functools.partial(rates_kernel, dims),
        out_shape=[mid_part] * span
        + [jax.ShapeDtypeStruct((tiles, num_vars, len(CORE_NODES) * share, LANES), f32)],
        in_specs=vmem(8 + span // 2),
        out_specs=vmem(span + 1),
        scratch_shapes=[pltpu.VMEM((num_vars, len(MID_NODES) * share, 2 * count), f32)],
        compiler_params=PARAMS,
        name="rates",
    )
    *mids, core = rates(facts, *forward, *backward, phys, twin, *core_takes)
    mid_takes = exchange(mids, span)
    edges = pl.pallas_call(
        functools.partial(edges_kernel, dims),
        out_shape=[jax.ShapeDtypeStruct((span // 2 * end_part.shape[0], LANES), f32)]
        + [end_part] * (span // 2),
        in_specs=vmem(8),
        out_specs=vmem(1 + span // 2),
        scratch_shapes=[pltpu.VMEM((num_vars, len(END_NODES) * share, 2 * count), f32)],
        compiler_params=PARAMS,
        name="edges",
    )
    odds, *evens = edges(facts, *backward, phys, core, twin, one, two)
    end_takes = relayed(odds, evens, span)

    dims = (rows, cols, share, span, modes)
    flat_shape = jax.ShapeDtypeStruct((flat_size, LANES), f32)
    collect = pl.pallas_call(
        functools.partial(collect_kernel, dims),
        out_shape=flat_shape,
        in_specs=vmem(1 + span),
        out_specs=vmem(1)[0],
        compiler_params=PARAMS,
        name="collect",
    )
    flat = collect(pick, *mid_takes)
    out, _ = pl.pallas_call(
        functools.partial(finish_kernel, dims),
        out_shape=[jax.ShapeDtypeStruct(flat_state.shape, f32), flat_shape],
        in_specs=vmem(4 + span // 2),
        out_specs=anywhere(1) + vmem(1),
        scratch_shapes=[
            pltpu.VMEM(flat_state.shape, f32),
            pltpu.SemaphoreType.DMA((chunks,)),
        ],
        input_output_aliases={2: 1},
        compiler_params=PARAMS,
        name="finish",
    )(pick, flat_state, flat, *end_takes)
    return out.reshape(state.shape)


def from_behind(value, axis, steps):
    count = lax.axis_size(axis)
    pairs = [(source, (source + steps) % count) for source in range(count)]
    return lax.ppermute(value, axis, pairs)


def gll_tables():
    near_point = math.sqrt(1.0 / 3.0 - 2.0 * math.sqrt(7.0) / 21.0)
    far_point = math.sqrt(1.0 / 3.0 + 2.0 * math.sqrt(7.0) / 21.0)
    points = np.array([-1.0, -far_point, -near_point, near_point, far_point, 1.0])
    weights = np.array(
        [
            1.0
            / np.prod([points[column] - points[second] for second in range(6) if second != column])
            for column in range(6)
        ]
    )
    deriv = np.zeros((6, 6))
    for target in range(6):
        for source in range(6):
            if source != target:
                deriv[target, source] = (
                    weights[source] / weights[target] / (points[target] - points[source])
                )
        deriv[target, target] = -np.sum(deriv[target])
    identity = np.eye(6)
    along_x = np.kron(deriv, identity)
    along_y = np.kron(identity, deriv)
    edge_nodes = np.array(
        [
            [offset for offset in range(6)],
            [30 + offset for offset in range(6)],
            [6 * offset for offset in range(6)],
            [6 * offset + 5 for offset in range(6)],
        ]
    ).reshape(-1)
    lifting = np.zeros((36, 24))
    lifting[edge_nodes, np.arange(24)] = 1.0
    return (
        jnp.asarray(along_x, jnp.float32),
        jnp.asarray(along_y, jnp.float32),
        edge_nodes,
        jnp.asarray(lifting, jnp.float32),
    )


def spanwise_basis(count):
    mode_index = jnp.arange(count, dtype=jnp.int32)
    planes = jnp.arange(count, dtype=jnp.int32)
    phase = mode_index[:, None] // 2 * planes[None, :] % count
    phase_angle = phase.astype(jnp.float32) * (2.0 * math.pi / count)
    odd_rows = (mode_index % 2 == 1)[:, None]
    basis_table = jnp.where(odd_rows, jnp.sin(phase_angle), jnp.cos(phase_angle)) * math.sqrt(
        2.0 / count
    )
    alternate = (1 - 2 * (planes % 2)).astype(jnp.float32) / math.sqrt(count)
    constant = jnp.ones((count,), jnp.float32) / math.sqrt(count)
    basis_table = jnp.where(mode_index[:, None] == 0, constant[None, :], basis_table)
    basis_table = jnp.where(mode_index[:, None] == 1, alternate[None, :], basis_table)
    return basis_table


def spanwise_derivative(modal):
    shape_in = modal.shape
    paired = modal.reshape(shape_in[0], shape_in[1] // 2, 2, shape_in[2])
    wavenumber = jnp.arange(shape_in[1] // 2, dtype=jnp.int32).astype(jnp.float32)[None, :, None]
    return jnp.stack([wavenumber * paired[:, :, 1], -wavenumber * paired[:, :, 0]], axis=2).reshape(
        shape_in
    )


def planar_terms(flux_x, flux_y, metric_part):
    along_x, along_y, edge_nodes, _ = gll_tables()
    scale_x = metric_part[0][:, None]
    scale_y = metric_part[1][:, None]
    grad_x = jnp.einsum("pq,vmeq->vmep", along_x, flux_x, precision=HIGHEST)
    grad_y = jnp.einsum("pq,vmeq->vmep", along_y, flux_y, precision=HIGHEST)
    planar = scale_x * grad_x + scale_y * grad_y
    sign_x = jnp.sign(scale_x)
    sign_y = jnp.sign(scale_y)
    edge_flux = jnp.concatenate(
        [
            -sign_x * flux_x[:, :, :, edge_nodes[0:6]],
            sign_x * flux_x[:, :, :, edge_nodes[6:12]],
            -sign_y * flux_y[:, :, :, edge_nodes[12:18]],
            sign_y * flux_y[:, :, :, edge_nodes[18:24]],
        ],
        axis=3,
    )
    return (planar, edge_flux)


def node_major(flat, num_vars, local_modes, nodes, local_elems):
    return jnp.transpose(flat.reshape(num_vars, local_modes, local_elems, nodes), (0, 1, 3, 2))


def trace_pool(traces):
    shape_in = traces.shape
    return (
        traces.reshape(shape_in[0], shape_in[1], 4, 6, shape_in[3])
        .transpose(0, 1, 3, 4, 2)
        .reshape(shape_in[0], shape_in[1], 6, 4 * shape_in[3])
    )


def own_pools(state_local, normal_flux):
    edge_nodes = gll_tables()[2]
    return (trace_pool(state_local[:, :, edge_nodes, :]), trace_pool(normal_flux))


def update(
    state_local,
    divergence,
    own_q,
    own_flux,
    from_lower,
    from_upper,
    neighbour,
    orient,
    wall,
    metric_local,
    first_mode,
    total_modes,
):
    lifting = gll_tables()[3]
    num_vars, modes_here, _, count = state_local.shape
    pool_q = jnp.concatenate([own_q, from_lower[0], from_upper[0]], axis=3)
    pool_flux = jnp.concatenate([own_flux, from_lower[1], from_upper[1]], axis=3)
    flat_index = neighbour.reshape(-1)
    other_q = jnp.take(pool_q, flat_index, axis=3)
    other_flux = jnp.take(pool_flux, flat_index, axis=3)
    flipped = orient.reshape(-1) == 1
    other_q = jnp.where(flipped, other_q[:, :, ::-1, :], other_q)
    other_flux = jnp.where(flipped, other_flux[:, :, ::-1, :], other_flux)
    mirror = jnp.array([-1.0, -1.0, -1.0, 1.0], jnp.float32).reshape(4, 1, 1, 1)
    walled = wall.reshape(-1) == 1
    other_q = jnp.where(walled, mirror * own_q, other_q)
    other_flux = jnp.where(walled, mirror * own_flux, other_flux)
    magnitude = (
        jnp.abs(
            jnp.stack([metric_local[0], metric_local[0], metric_local[1], metric_local[1]], axis=1)
        ).reshape(-1)
        * 15.0
    )
    surface_jump = magnitude * (0.5 * (own_flux + other_flux) - 0.5 * PENALTY * (own_q - other_q))
    unpooled = (
        surface_jump.reshape(num_vars, modes_here, 6, count, 4)
        .transpose(0, 1, 4, 2, 3)
        .reshape(num_vars, modes_here, 24, count)
    )
    surface = jnp.einsum("pq,vmqe->vmpe", lifting, unpooled, precision=HIGHEST)
    mode_index = first_mode + jnp.arange(modes_here, dtype=jnp.int32)
    wavenumber = jnp.where(mode_index == 1, total_modes // 2, mode_index // 2).astype(jnp.float32)
    damping = 1.0 + TIME_STEP * VISCOSITY * wavenumber * wavenumber
    return (state_local + TIME_STEP * (surface - divergence)) / damping[None, :, None, None]


def plain_body(state, metric, neighbour, orient, wall, rim):
    num_vars, local_modes, flat_size = state.shape
    num_nodes = 36
    local_elems = flat_size // num_nodes
    span_size = lax.axis_size("span")
    total_modes = local_modes * span_size
    share = local_elems // span_size
    state_nodes = node_major(state, num_vars, local_modes, num_nodes, local_elems)
    planes_in = lax.all_to_all(state, "span", split_axis=2, concat_axis=1, tiled=True)
    basis_table = spanwise_basis(total_modes)
    physical = jnp.einsum("mn,vmk->vnk", basis_table, planes_in, precision=HIGHEST)
    metric_part = lax.dynamic_slice_in_dim(metric, lax.axis_index("span") * share, share, axis=1)
    shape_here = (num_vars, total_modes, share, num_nodes)
    planar_div, edge_flux = planar_terms(
        (physical[0:1] * physical).reshape(shape_here),
        (physical[1:2] * physical).reshape(shape_here),
        metric_part,
    )
    volume_fields = jnp.concatenate(
        [planar_div.reshape(num_vars, total_modes, share * num_nodes), physical[2:3] * physical],
        axis=0,
    )
    volume_modal = jnp.einsum("mn,vnk->vmk", basis_table, volume_fields, precision=HIGHEST)
    edge_modal = jnp.einsum(
        "mn,vnk->vmk",
        basis_table,
        edge_flux.reshape(num_vars, total_modes, share * 24),
        precision=HIGHEST,
    )
    combined = volume_modal[0:4] + spanwise_derivative(volume_modal[4:8])
    div_flat, flux_flat = (
        lax.all_to_all(combined, "span", split_axis=1, concat_axis=2, tiled=True),
        lax.all_to_all(edge_modal, "span", split_axis=1, concat_axis=2, tiled=True),
    )
    divergence = node_major(div_flat, num_vars, local_modes, num_nodes, local_elems)
    normal_flux = node_major(flux_flat, num_vars, local_modes, 24, local_elems)
    own_q, own_flux = own_pools(state_nodes, normal_flux)
    upper_rim = jnp.stack([jnp.take(own_q, rim[1], axis=3), jnp.take(own_flux, rim[1], axis=3)])
    lower_rim = jnp.stack([jnp.take(own_q, rim[0], axis=3), jnp.take(own_flux, rim[0], axis=3)])
    from_lower = from_behind(upper_rim, "elem", 1)
    from_upper = from_behind(lower_rim, "elem", -1)
    first_mode = lax.axis_index("span") * local_modes
    result = update(
        state_nodes,
        divergence,
        own_q,
        own_flux,
        from_lower,
        from_upper,
        neighbour,
        orient,
        wall,
        metric,
        first_mode,
        total_modes,
    )
    return jnp.transpose(result, (0, 1, 3, 2)).reshape(num_vars, local_modes, flat_size)


def body(state, metric, neighbour, orient, wall, rim):
    num_vars, modes, flat_size = state.shape
    span = lax.axis_size("span")
    groups = lax.axis_size("elem")
    elems = flat_size // NODES
    rows = rim.shape[1]
    fits = (
        groups % 2 == 0
        and rows % span == 0
        and SUB == 2 * (elems // rows)
        and num_vars * modes == LANES
        and modes * 4 == LANES
        and span % 4 == 0
        and span & (span - 1) == 0
        and LANES % elems == 0
        and elems == SUB * span
        and elems % rows == 0
        and SUB % (elems // rows) == 0
        and flat_size % CHUNK == 0
    )
    if not fits:
        return plain_body(state, metric, neighbour, orient, wall, rim)
    return ordered_body(state, metric, neighbour, wall, rim)


def solution(mesh):
    placed = (
        P(None, "span", "elem"),
        P(None, "elem"),
        P("elem", None),
        P("elem", None),
        P("elem", None),
        P(None, "elem"),
    )
    return jax.shard_map(
        body, mesh=mesh, in_specs=placed, out_specs=P(None, "span", "elem"), check_vma=False
    )
```

```python
import functools
import math

import jax
import jax.numpy as jnp
import numpy as np
from jax import lax
from jax.experimental import pallas as pl
from jax.experimental.pallas import tpu as pltpu
from jax.sharding import PartitionSpec as P


TIME_STEP = 0.001
VISCOSITY = 0.02
PENALTY = 1.0
HIGHEST = lax.Precision.HIGHEST
SIDE = 6
NODES = SIDE * SIDE
LANES = 128
SUB = 8
CHUNK = 3 * LANES
FETCH = 6 * LANES
RIM_NODES = [p for p in range(NODES) if p // SIDE in (0, 5) or p % SIDE in (0, 5)]
CORE_NODES = [p for p in range(NODES) if p not in RIM_NODES]
MID_NODES = [p for p in range(NODES) if p // SIDE not in (0, 5)]
END_NODES = [p for p in range(NODES) if p // SIDE in (0, 5)]


def gll_matrix():
    near_point = math.sqrt(1.0 / 3.0 - 2.0 * math.sqrt(7.0) / 21.0)
    far_point = math.sqrt(1.0 / 3.0 + 2.0 * math.sqrt(7.0) / 21.0)
    points = np.array([-1.0, -far_point, -near_point, near_point, far_point, 1.0])
    weights = np.array(
        [
            1.0
            / np.prod([points[column] - points[second] for second in range(6) if second != column])
            for column in range(6)
        ]
    )
    deriv = np.zeros((6, 6))
    for target in range(6):
        for source in range(6):
            if source != target:
                deriv[target, source] = (
                    weights[source] / weights[target] / (points[target] - points[source])
                )
        deriv[target, target] = -np.sum(deriv[target])
    return deriv


def basis_matrix(count):
    mode = np.arange(count)[:, None]
    plane = np.arange(count)[None, :]
    angle = (mode // 2 * plane % count) * (2.0 * math.pi / count)
    table = np.where(mode % 2 == 1, np.sin(angle), np.cos(angle)) * math.sqrt(2.0 / count)
    table = np.where(mode == 0, 1.0 / math.sqrt(count), table)
    return np.where(mode == 1, (1.0 - 2.0 * (plane % 2)) / math.sqrt(count), table)


def halves(table):
    table = np.asarray(table, np.float32)
    high = table.astype(jnp.bfloat16)
    low = (table - high.astype(np.float32)).astype(jnp.bfloat16)
    return high, low


def forward_tables(count):
    return halves(basis_matrix(count))


def backward_tables(count):
    basis = basis_matrix(count)
    wave = np.arange(count) // 2
    swapped = np.empty_like(basis)
    swapped[0::2] = wave[0::2, None] * basis[1::2]
    swapped[1::2] = -wave[1::2, None] * basis[0::2]
    damp_wave = np.where(np.arange(count) == 1, count // 2, wave).astype(np.float64)
    factor = TIME_STEP / (1.0 + TIME_STEP * VISCOSITY * damp_wave * damp_wave)
    return halves(factor[:, None] * np.concatenate([basis, -swapped], axis=1))


def split(value):
    high = value.astype(jnp.bfloat16)
    low = (value - high.astype(jnp.float32)).astype(jnp.bfloat16)
    return high, low


def mm(a, b):
    return lax.dot_general(a, b, (((1,), (0,)), ((), ())), preferred_element_type=jnp.float32)


def mm_nt(a, b):
    return lax.dot_general(a, b, (((1,), (1,)), ((), ())), preferred_element_type=jnp.float32)


def regroup(parts, lane):
    quarter = LANES // 4
    low_half = lane < 2 * quarter
    rolled = [pltpu.roll(part, 2 * quarter, 1) for part in parts]
    first = [
        jnp.where(low_half, parts[0], rolled[2]),
        jnp.where(low_half, parts[1], rolled[3]),
        jnp.where(low_half, rolled[0], parts[2]),
        jnp.where(low_half, rolled[1], parts[3]),
    ]
    even = lane // quarter % 2 == 0
    out = []
    for pair in (0, 2):
        a, b = first[pair], first[pair + 1]
        out.append(jnp.where(even, a, pltpu.roll(b, quarter, 1)))
        out.append(jnp.where(even, pltpu.roll(a, LANES - quarter, 1), b))
    return out


def move_nodes(nodes, elems, flat, pick, pick_sides, put):
    for at in range(0, len(nodes), 2):
        pair = nodes[at : at + 2]
        columns = [
            jnp.concatenate(split(flat[pl.ds(node, elems, stride=NODES), :]), axis=0)
            for node in pair
        ]
        chosen = pick_sides if any(node % SIDE in (0, 5) for node in pair) else pick
        moved = mm(chosen, jnp.concatenate(columns, axis=1))
        for half, node in enumerate(pair):
            put(at + half, node, moved[:, half * LANES : (half + 1) * LANES])


def spread_kernel(dims, near_any, wall_any, rim_any, metric_any, state_any, *refs):
    rows, cols, share, span = dims
    sends = refs[:span]
    pick_ref, facts_ref, flat, all_ref = refs[span : span + 4]
    halo_ref, bends_ref, near_ref, wall_ref, rim_ref, metric_ref, state_ref, sems = refs[span + 4 :]
    me = lax.axis_index("span")
    elems = rows * cols
    width = elems * NODES
    small = [
        pltpu.make_async_copy(source, target, sems.at[at])
        for at, (source, target) in enumerate(
            (
                (near_any, near_ref),
                (wall_any, wall_ref),
                (rim_any, rim_ref),
                (metric_any, metric_ref),
            )
        )
    ]
    large = [
        pltpu.make_async_copy(
            state_any.at[:, pl.ds(at, FETCH)],
            state_ref.at[:, pl.ds(at, FETCH)],
            sems.at[len(small) + at // FETCH],
        )
        for at in range(0, width, FETCH)
    ]
    for copy in small + large:
        copy.start()
    for copy in small:
        copy.wait()
    lane = lax.broadcasted_iota(jnp.int32, (1, LANES), 1) % elems
    lines = share // cols
    halo_ref[...] = jnp.zeros_like(halo_ref)
    bends_ref[...] = jnp.zeros_like(bends_ref)
    before = None
    for row in range(rows):
        cell = rim_ref[0, row] >> 2
        face = rim_ref[0, row] & 1
        here = []
        for col in range(cols):
            if row == 0:
                flip_y = wall_ref[3, cell]
            else:
                flip_y = jnp.where(near_ref[3, cell] >> 2 == before[col], 1, 0)
            here.append(cell)
            place = row * cols + col
            at = (place // share ^ me) * share + place % share
            chosen = jnp.where(lane == cell, 1.0, 0.0)
            pick_ref[pl.ds(at, 1), :] = chosen
            block, line = divmod(row, lines)
            if block % 2 and line == lines - 1 and block + 1 < rows // lines:
                far, bends = (block + 1) ^ me, (face, 1 - flip_y)
            elif block % 2 == 0 and line == 0 and block > 0:
                far, bends = (block - 1) ^ me, (face, flip_y)
            else:
                far = None
            for half in (0, cols) if far is not None else ():
                place_at = far * share + half + col
                halo_ref[pl.ds(place_at, 1), :] = chosen
                for kind, bend in enumerate(bends):
                    bends_ref[kind, pl.ds(place_at, 1), :] = jnp.full((1, LANES), bend, jnp.int32)
            facts = (
                metric_ref[0, cell],
                metric_ref[1, cell],
                face.astype(jnp.float32),
                flip_y.astype(jnp.float32),
            )
            for kind, fact in enumerate(facts):
                all_ref[kind, pl.ds(at, 1), :] = jnp.full((1, LANES), fact, jnp.float32)
            if col + 1 < cols:
                step = near_ref[face ^ 1, cell]
                cell = step >> 2
                face = step & 1
        before = here
    for at in range(0, width, LANES):
        if at % FETCH == 0:
            large[at // FETCH].wait()
        flat[pl.ds(at, LANES), :] = state_ref[:, pl.ds(at, LANES)].T
    facts_ref[...] = all_ref[:, :share]
    pick = pick_ref[...].astype(jnp.bfloat16)
    both = jnp.concatenate([pick, halo_ref[...].astype(jnp.bfloat16)], axis=0)
    edge = {}

    def put(at, node, mine):
        if node % SIDE in (0, 5):
            edge[divmod(node, SIDE)] = mine[elems:]
        for step in range(span):
            sends[step][pl.ds(at * share, share), :] = mine[step * share : (step + 1) * share]

    move_nodes(RIM_NODES, elems, flat, pick, both, put)
    bend_x = bends_ref[0] == 1
    bend_y = bends_ref[1] == 1
    trace = [jnp.where(bend_y, edge[t, 5], edge[t, 0]) for t in range(SIDE)]
    upper = lax.broadcasted_iota(jnp.int32, (elems, LANES), 0) % share < cols
    for t in range(0, SIDE, 2):
        one, two = (jnp.where(bend_x, trace[SIDE - 1 - s], trace[s]) for s in (t, t + 1))
        moved = jnp.where(upper, one, two)
        at = pl.ds(len(RIM_NODES) * share + t * cols, share)
        for step in range(span):
            sends[step][at, :] = moved[step * share : (step + 1) * share]


def spread_core_kernel(share, span, pick_ref, flat, odd_ref, *evens):
    pick = pick_ref[...].astype(jnp.bfloat16)
    size = len(CORE_NODES) * share

    def put(at, node, mine):
        for step in range(span):
            value = mine[step * share : (step + 1) * share]
            if step % 2:
                odd_ref[pl.ds(step // 2 * size + at * share, share), :] = value
            else:
                evens[step // 2][pl.ds(at * share, share), :] = value

    move_nodes(CORE_NODES, pick.shape[0], flat, pick, pick, put)


def along(trace, flip):
    return {t: jnp.where(flip, trace[SIDE - 1 - t], trace[t]) for t in trace}


def sides_x(value, flip_x, flip_y):
    low = {t: jnp.where(flip_x, value(5, t), value(0, t)) for t in range(SIDE)}
    high = {t: jnp.where(flip_x, value(0, t), value(5, t)) for t in range(SIDE)}
    return along(low, flip_y), along(high, flip_y)


def sides_y(value, flip_x, flip_y, wanted):
    low = {t: jnp.where(flip_y, value(t, 5), value(t, 0)) for t in wanted}
    high = {t: jnp.where(flip_y, value(t, 0), value(t, 5)) for t in wanted}
    return along(low, flip_x), along(high, flip_x)


def rim_reader(ref, tile, var):
    return lambda i, j: ref[tile, var, pl.ds(RIM_NODES.index(SIDE * i + j) * SUB, SUB), :]


def back(one, two, flip, flip_along):
    return along({t: jnp.where(flip, two[t], one[t]) for t in one}, flip_along)


def sign(value):
    return jnp.where(value < 0.0, -1.0, 1.0)


def to_planes(dims, me, high_ref, low_ref, takes, phys_ref):
    _, _, span, num_vars, modes = dims
    lane = lax.broadcasted_iota(jnp.int32, (1, LANES), 1)
    tables = []
    for ref in (high_ref, low_ref):
        tables.append(
            jnp.concatenate([ref[pl.ds((me ^ k) * modes, modes), :] for k in range(span)], axis=0)
        )
    pieces = []
    for group in range(span // 4):
        pieces.append(regroup([takes[4 * group + q][...] for q in range(4)], lane))
    stack = [jnp.concatenate([piece[var] for piece in pieces], axis=1) for var in range(num_vars)]
    high, low = split(jnp.concatenate(stack, axis=0))
    planes = mm(high, tables[0]) + mm(low, tables[0]) + mm(high, tables[1])
    size = takes[0].shape[0]
    for var in range(num_vars):
        for tile in range(span * modes // LANES):
            phys_ref[tile, var] = planes[
                var * size : (var + 1) * size, tile * LANES : (tile + 1) * LANES
            ]


def planes_kernel(dims, facts_ref, high_ref, low_ref, *refs):
    cols, share, span, num_vars, modes = dims
    takes = refs[:span]
    phys_ref, twin_ref, one_ref, two_ref = refs[span:]
    to_planes(dims, lax.axis_index("span"), high_ref, low_ref, takes, phys_ref)
    odd = lax.axis_index("elem") % 2 == 1
    lines = share // cols
    flip_x = facts_ref[2] > 0.5
    flip_y = facts_ref[3] > 0.5
    turn_x = sign(facts_ref[0]) * (1.0 - 2.0 * facts_ref[2])
    second = lax.axis_index("span") % 2 == 1
    turn_y = sign(facts_ref[1]) * (1.0 - 2.0 * facts_ref[3])
    turn_y = jnp.where(second, -turn_y, turn_y)
    inner = jnp.where(second, 1.0 - facts_ref[3], facts_ref[3]) > 0.5

    def toward_twin(value):
        return along({t: jnp.where(inner, value(t, 0), value(t, 5)) for t in range(SIDE)}, flip_x)

    for tile in range(span * modes // LANES):
        speed = sides_x(rim_reader(phys_ref, tile, 0), flip_x, flip_y)
        pace = toward_twin(rim_reader(phys_ref, tile, 1))
        pace = {t: 1.0 + turn_y * pace[t] for t in pace}
        for var in range(num_vars):
            trace = toward_twin(rim_reader(phys_ref, tile, var))
            for t in range(SIDE):
                give = pace[t] * trace[t]
                at = pl.ds(t * cols, cols)
                twin_ref[tile, var, at, :] = jnp.where(second, give[:cols], give[share - cols :])
            trace = sides_x(rim_reader(phys_ref, tile, var), flip_x, flip_y)
            for t in range(SIDE):
                low_x = (1.0 - turn_x * speed[0][t]) * trace[0][t]
                high_x = (1.0 + turn_x * speed[1][t]) * trace[1][t]
                for line in range(lines):
                    at = pl.ds(t * lines + line, 1)
                    up = high_x[(line + 1) * cols - 1 : (line + 1) * cols]
                    down = low_x[line * cols : line * cols + 1]
                    one_ref[tile, var, at, :] = jnp.where(odd, down, up)
                    two_ref[tile, var, at, :] = jnp.where(odd, up, down)


def mode_tables(dims, me, high_ref, low_ref):
    _, _, span, _, modes = dims
    return [
        jnp.concatenate([ref[pl.ds((me ^ k) * modes, modes), :] for k in range(span)], axis=0)
        for ref in (high_ref, low_ref)
    ]


def to_modes(tables, rate):
    high, low = split(rate)
    return mm_nt(high, tables[0]) + mm_nt(low, tables[0]) + mm_nt(high, tables[1])


def by_target(dims, gains):
    lane = lax.broadcasted_iota(jnp.int32, (1, LANES), 1)
    out = []
    for group in range(dims[2] // 4):
        at = slice(group * LANES, (group + 1) * LANES)
        out += regroup([gain[:, at] for gain in gains], lane)
    return out


def derivative(values, wanted=tuple(range(SIDE))):
    deriv = gll_matrix()
    last = SIDE - 1
    plus = [values[j] + values[last - j] for j in range(SIDE // 2)]
    minus = [values[j] - values[last - j] for j in range(SIDE // 2)]
    out = [None] * SIDE
    for i in range(SIDE // 2):
        if i not in wanted:
            continue
        even, odd = None, None
        for j in range(SIDE // 2):
            a = minus[j] * float(0.5 * (deriv[i, j] - deriv[i, last - j]))
            b = plus[j] * float(0.5 * (deriv[i, j] + deriv[i, last - j]))
            even = a if even is None else even + a
            odd = b if odd is None else odd + b
        out[i] = even + odd
        out[last - i] = even - odd
    return out


class Faces:
    def __init__(self, dims, facts_ref, phys_ref, core_ref, twin_ref):
        cols, share, span, self.num_vars, modes = dims
        self.cols = cols
        self.phys_ref, self.core_ref, self.twin_ref = phys_ref, core_ref, twin_ref
        me = lax.axis_index("span")
        slot = lax.broadcasted_iota(jnp.int32, (SUB, LANES), 0)
        self.slot = slot
        self.flip_x = facts_ref[2] > 0.5
        self.flip_y = facts_ref[3] > 0.5
        self.scale_x = -facts_ref[0]
        self.scale_y = facts_ref[1]
        self.turn_x = sign(facts_ref[0]) * (1.0 - 2.0 * facts_ref[2])
        self.turn_y = sign(facts_ref[1]) * (1.0 - 2.0 * facts_ref[3])
        self.weight_x = 7.5 * jnp.abs(facts_ref[0])
        self.weight_y = 7.5 * jnp.abs(facts_ref[1])
        self.first_line = slot < cols
        self.turn_halo = jnp.where(self.first_line, self.turn_y, -self.turn_y)
        self.far = slot // cols == me % 2
        self.floor = jnp.logical_and(self.first_line, me == 0)
        self.roof = jnp.logical_and(jnp.logical_not(self.first_line), me == span - 1)

    def reader(self, tile, var):
        def read(i, j):
            node = SIDE * i + j
            ref = self.phys_ref if node in RIM_NODES else self.core_ref
            nodes = RIM_NODES if node in RIM_NODES else CORE_NODES
            return ref[tile, var, pl.ds(nodes.index(node) * SUB, SUB), :]

        return read

    def volume(self, tile, var, wanted):
        q, u, v = (self.reader(tile, at) for at in (var, 0, 1))
        total = {}
        for j in range(SIDE):
            slope = derivative([q(i, j) * u(i, j) for i in range(SIDE)], wanted)
            for i in wanted:
                total[i, j] = self.scale_x * slope[i]
        for i in wanted:
            slope = derivative([q(i, j) * v(i, j) for j in range(SIDE)])
            for j in range(SIDE):
                total[i, j] = total[i, j] - self.scale_y * slope[j]
        return total

    def pace_y(self, tile, wanted):
        speed = sides_y(self.reader(tile, 1), self.flip_x, self.flip_y, wanted)
        return [{t: self.turn_y * side[t] for t in wanted} for side in speed]

    def twice(self, ref, tile, var, at):
        row = ref[tile, var, pl.ds(at, self.cols), :]
        return jnp.concatenate([row] * (SUB // self.cols), axis=0)

    def far_row(self, tile, var, t):
        return self.twice(self.phys_ref, tile, var, len(RIM_NODES) * SUB + t * self.cols)

    def twin_row(self, tile, var, t):
        return self.twice(self.twin_ref, tile, var, t * self.cols)

    def far_pace(self, tile, wanted):
        return {t: 1.0 + self.turn_halo * self.far_row(tile, 1, t) for t in wanted}

    def faces_y(self, tile, var, pace, far_pace, wanted, total):
        mirror = 1.0 if var == self.num_vars - 1 else -1.0
        trace = sides_y(self.reader(tile, var), self.flip_x, self.flip_y, wanted)
        low, high = {}, {}
        for t in wanted:
            speed, value = pace[0][t], trace[0][t]
            own_low, give_low = -(speed + 1.0) * value, (1.0 - speed) * value
            speed, value = pace[1][t], trace[1][t]
            own_high, give_high = (speed - 1.0) * value, (1.0 + speed) * value
            outside = jnp.where(
                self.far, far_pace[t] * self.far_row(tile, var, t), self.twin_row(tile, var, t)
            )
            outside = jnp.where(self.floor, mirror * give_low, outside)
            outside = jnp.where(self.roof, mirror * give_high, outside)
            from_low = jnp.where(self.first_line, outside, pltpu.roll(give_high, self.cols, 0))
            from_high = jnp.where(
                self.first_line, pltpu.roll(give_low, SUB - self.cols, 0), outside
            )
            low[t] = self.weight_y * (own_low + from_low)
            high[t] = self.weight_y * (own_high + from_high)
        for j, one, two in ((0, low, high), (5, high, low)):
            side = back(one, two, self.flip_y, self.flip_x)
            for t in wanted:
                total[t, j] = total[t, j] + side[t]

    def pace_x(self, tile):
        speed = sides_x(self.reader(tile, 0), self.flip_x, self.flip_y)
        return [{t: self.turn_x * side[t] for t in side} for side in speed]

    def faces_x(self, tile, var, pace, total, rim):
        trace = sides_x(self.reader(tile, var), self.flip_x, self.flip_y)
        low, high = {}, {}
        for t in range(SIDE):
            speed, value = pace[0][t], trace[0][t]
            own_low, give_low = -(speed + 1.0) * value, (1.0 - speed) * value
            speed, value = pace[1][t], trace[1][t]
            own_high, give_high = (speed - 1.0) * value, (1.0 + speed) * value
            from_low, from_high = pltpu.roll(give_high, 1, 0), pltpu.roll(give_low, SUB - 1, 0)
            for line, (below, above) in enumerate(rim(t)):
                from_low = jnp.where(self.slot == line * self.cols, below, from_low)
                from_high = jnp.where(self.slot == (line + 1) * self.cols - 1, above, from_high)
            low[t] = self.weight_x * (own_low + from_low)
            high[t] = self.weight_x * (own_high + from_high)
        for i, one, two in ((0, low, high), (5, high, low)):
            side = back(one, two, self.flip_x, self.flip_y)
            for t in range(SIDE):
                total[i, t] = total[i, t] + side[t]


def unpaired(refs, size):
    takes = list(refs[:2])
    for ref in refs[2:]:
        takes += [ref.at[:size], ref.at[size:]]
    return takes


def store_rates(rate_ref, nodes, tile, var, count, total, q, w):
    for place, node in enumerate(nodes):
        i, j = divmod(node, SIDE)
        at = pl.ds(place * SUB, SUB)
        rate_ref[var, at, pl.ds(tile * LANES, LANES)] = total[i, j]
        rate_ref[var, at, pl.ds(count + tile * LANES, LANES)] = q(i, j) * w(i, j)


def rates_kernel(
    dims, facts_ref, there_high, there_low, high_ref, low_ref, phys_ref, twin_ref, *refs
):
    _, share, span, num_vars, modes = dims
    half = span // 2
    outs = refs[half + 1 : half + 1 + span]
    core_ref, rate_ref = refs[half + 1 + span :]
    takes = unpaired(refs[: half + 1], len(CORE_NODES) * share)
    me = lax.axis_index("span")
    to_planes(dims, me, there_high, there_low, takes, core_ref)
    count = span * modes
    faces = Faces(dims, facts_ref, phys_ref, core_ref, twin_ref)
    wanted = tuple(range(1, SIDE - 1))
    paces = [
        (faces.pace_y(tile, wanted), faces.far_pace(tile, wanted)) for tile in range(count // LANES)
    ]
    tables = mode_tables(dims, me, high_ref, low_ref)
    gains = []
    for var in range(num_vars):
        for tile in range(count // LANES):
            total = faces.volume(tile, var, wanted)
            faces.faces_y(tile, var, *paces[tile], wanted, total)
            q, w = faces.reader(tile, var), faces.reader(tile, 2)
            store_rates(rate_ref, MID_NODES, tile, var, count, total, q, w)
        gains.append(to_modes(tables, rate_ref[var]))
    for k, part in enumerate(by_target(dims, gains)):
        outs[k][...] = part


def edges_kernel(
    dims, facts_ref, high_ref, low_ref, phys_ref, core_ref, twin_ref, one_ref, two_ref, *refs
):
    cols, share, span, num_vars, modes = dims
    odd_ref, *evens, rate_ref = refs
    count = span * modes
    lines = share // cols
    odd = lax.axis_index("elem") % 2 == 1
    faces = Faces(dims, facts_ref, phys_ref, core_ref, twin_ref)
    wanted = (0, SIDE - 1)
    for tile in range(count // LANES):
        pace_x, pace_y = faces.pace_x(tile), faces.pace_y(tile, wanted)
        far_pace = faces.far_pace(tile, wanted)
        for var in range(num_vars):

            def rim(t, tile=tile, var=var):
                found = []
                for line in range(lines):
                    at = pl.ds(t * lines + line, 1)
                    one, two = one_ref[tile, var, at, :], two_ref[tile, var, at, :]
                    found.append((jnp.where(odd, one, two), jnp.where(odd, two, one)))
                return found

            total = faces.volume(tile, var, wanted)
            faces.faces_x(tile, var, pace_x, total, rim)
            faces.faces_y(tile, var, pace_y, far_pace, wanted, total)
            q, w = faces.reader(tile, var), faces.reader(tile, 2)
            store_rates(rate_ref, END_NODES, tile, var, count, total, q, w)
    tables = mode_tables(dims, lax.axis_index("span"), high_ref, low_ref)
    rows = len(END_NODES) * share
    gain = to_modes(tables, jnp.concatenate([rate_ref[var] for var in range(num_vars)], axis=0))
    parts = by_target(dims, [gain[var * rows : (var + 1) * rows] for var in range(num_vars)])
    size = len(END_NODES) * share
    for k in range(span):
        if k % 2:
            odd_ref[pl.ds(k // 2 * size, size), :] = parts[k]
        else:
            evens[k // 2][...] = parts[k]


def put_back(nodes, share, elems, pick_ref, takes, flat):
    turned = pick_ref[...].T[:elems]
    pick = jnp.concatenate([turned] * (LANES // elems), axis=1).astype(jnp.bfloat16)
    for at in range(0, len(nodes), 2):
        columns = []
        for row in (at * share, (at + 1) * share):
            part = jnp.concatenate([take[pl.ds(row, share), :] for take in takes], axis=0)
            columns.append(jnp.concatenate(split(part), axis=0))
        moved = mm(pick, jnp.concatenate(columns, axis=1))
        flat[pl.ds(nodes[at], elems, stride=NODES), :] = moved[:, :LANES]
        flat[pl.ds(nodes[at + 1], elems, stride=NODES), :] = moved[:, LANES:]


def collect_kernel(dims, pick_ref, *refs):
    rows, cols, share, span, _ = dims
    put_back(MID_NODES, share, rows * cols, pick_ref, refs[:span], refs[span])


def finish_kernel(dims, pick_ref, state_ref, flat_in, *refs):
    rows, cols, share, span, modes = dims
    takes = unpaired(refs[: span // 2 + 1], len(END_NODES) * share)
    out_any, flat, out_ref, sems = refs[span // 2 + 1 :]
    elems = rows * cols
    count = span * modes
    put_back(END_NODES, share, elems, pick_ref, takes, flat)
    me = lax.axis_index("span")
    index = me * modes + lax.broadcasted_iota(jnp.int32, (LANES, 1), 0) % modes
    wave = jnp.where(index == 1, count // 2, index // 2).astype(jnp.float32)
    damping = 1.0 / (1.0 + TIME_STEP * VISCOSITY * wave * wave)
    copies = []
    for start in range(0, elems * NODES, CHUNK):
        for block in range(start, start + CHUNK, LANES):
            at = pl.ds(block, LANES)
            out_ref[:, at] = state_ref[:, at] * damping + flat[at, :].T
        at = pl.ds(start, CHUNK)
        copies.append(
            pltpu.make_async_copy(out_ref.at[:, at], out_any.at[:, at], sems.at[start // CHUNK])
        )
        copies[-1].start()
    for copy in copies:
        copy.wait()


def in_hbm(array):
    return pltpu.with_memory_space_constraint(array, pltpu.HBM)


def anywhere(count):
    return [pl.BlockSpec(memory_space=pltpu.HBM)] * count


def vmem(count):
    return [pl.BlockSpec(memory_space=pltpu.VMEM)] * count


PARAMS = pltpu.CompilerParams(vmem_limit_bytes=24 * 1024 * 1024)


def exchange(blocks, span):
    taken = {0: blocks[0]}
    for k in range(1, span):
        taken[k] = lax.ppermute(blocks[k], "span", [(s, s ^ k) for s in range(span)])
    return [taken[k] for k in range(span)]


def relayed(odds, evens, span):
    size = evens[0].shape[0]
    passed = lax.ppermute(odds, "span", [(s, s ^ 1) for s in range(span)])
    taken = [evens[0], passed[:size]]
    for at in range(1, span // 2):
        both = jnp.concatenate([evens[at], passed[at * size : (at + 1) * size]])
        both = lax.ppermute(both, "span", [(s, s ^ (2 * at)) for s in range(span)])
        taken.append(both)
    return taken


def ordered_body(state, metric, neighbour, wall, rim):
    num_vars, modes, flat_size = state.shape
    elems = flat_size // NODES
    span = lax.axis_size("span")
    groups = lax.axis_size("elem")
    share = elems // span
    rows = rim.shape[1]
    cols = elems // rows
    count = modes * span
    tiles = count // LANES
    lines = share // cols
    flat_state = state.reshape(num_vars * modes, flat_size)
    f32 = jnp.float32
    mid_part, end_part, rim_part, core_part = (
        jax.ShapeDtypeStruct((nodes * share, LANES), f32)
        for nodes in (len(MID_NODES), len(END_NODES), len(RIM_NODES) + SIDE // 2, len(CORE_NODES))
    )
    chunks = flat_size // CHUNK
    first = pl.pallas_call(
        functools.partial(spread_kernel, (rows, cols, share, span)),
        out_shape=[rim_part] * span
        + [
            jax.ShapeDtypeStruct((elems, LANES), f32),
            jax.ShapeDtypeStruct((4, share, LANES), f32),
            jax.ShapeDtypeStruct((flat_size, LANES), f32),
        ],
        in_specs=anywhere(5),
        out_specs=vmem(span + 3),
        scratch_shapes=[
            pltpu.VMEM((4, elems, LANES), f32),
            pltpu.VMEM((elems, LANES), f32),
            pltpu.VMEM((2, elems, LANES), jnp.int32),
            pltpu.SMEM(neighbour.T.shape, jnp.int32),
            pltpu.SMEM(wall.T.shape, jnp.int32),
            pltpu.SMEM(rim.shape, jnp.int32),
            pltpu.SMEM(metric.shape, f32),
            pltpu.VMEM(flat_state.shape, f32),
            pltpu.SemaphoreType.DMA((4 + flat_size // FETCH,)),
        ],
        compiler_params=PARAMS,
        name="spread",
    )(*[in_hbm(x) for x in (neighbour.T, wall.T, rim, metric, flat_state)])
    rim_takes = exchange(first[:span], span)
    pick, facts, turned = first[span:]
    spread_core = pl.pallas_call(
        functools.partial(spread_core_kernel, share, span),
        out_shape=[jax.ShapeDtypeStruct((span // 2 * core_part.shape[0], LANES), f32)]
        + [core_part] * (span // 2),
        in_specs=vmem(2),
        out_specs=vmem(1 + span // 2),
        compiler_params=PARAMS,
        name="spread_core",
    )
    odds, *evens = spread_core(pick, turned)
    core_takes = relayed(odds, evens, span)

    dims = (cols, share, span, num_vars, modes)
    forward = [jnp.asarray(t) for t in forward_tables(count)]
    backward = [jnp.asarray(t) for t in backward_tables(count)]
    line_shape = jax.ShapeDtypeStruct((tiles, num_vars, SIDE * lines, LANES), f32)
    planes = pl.pallas_call(
        functools.partial(planes_kernel, dims),
        out_shape=[
            jax.ShapeDtypeStruct((tiles, num_vars, rim_part.shape[0], LANES), f32),
            jax.ShapeDtypeStruct((tiles, num_vars, SIDE * cols, LANES), f32),
            line_shape,
            line_shape,
        ],
        in_specs=vmem(3 + span),
        out_specs=vmem(4),
        compiler_params=PARAMS,
        name="planes",
    )
    phys, twin, one, two = planes(facts, *forward, *rim_takes)
    twin = lax.ppermute(twin, "span", [(s, s ^ 1) for s in range(span)])
    one = lax.ppermute(one, "elem", [(g, g ^ 1) for g in range(groups)])
    two = lax.ppermute(
        two, "elem", [(g, (g - 1 if g % 2 == 0 else g + 1) % groups) for g in range(groups)]
    )

    rates = pl.pallas_call(
        functools.partial(rates_kernel, dims),
        out_shape=[mid_part] * span
        + [jax.ShapeDtypeStruct((tiles, num_vars, len(CORE_NODES) * share, LANES), f32)],
        in_specs=vmem(8 + span // 2),
        out_specs=vmem(span + 1),
        scratch_shapes=[pltpu.VMEM((num_vars, len(MID_NODES) * share, 2 * count), f32)],
        compiler_params=PARAMS,
        name="rates",
    )
    *mids, core = rates(facts, *forward, *backward, phys, twin, *core_takes)
    mid_takes = exchange(mids, span)
    edges = pl.pallas_call(
        functools.partial(edges_kernel, dims),
        out_shape=[jax.ShapeDtypeStruct((span // 2 * end_part.shape[0], LANES), f32)]
        + [end_part] * (span // 2),
        in_specs=vmem(8),
        out_specs=vmem(1 + span // 2),
        scratch_shapes=[pltpu.VMEM((num_vars, len(END_NODES) * share, 2 * count), f32)],
        compiler_params=PARAMS,
        name="edges",
    )
    odds, *evens = edges(facts, *backward, phys, core, twin, one, two)
    end_takes = relayed(odds, evens, span)

    dims = (rows, cols, share, span, modes)
    flat_shape = jax.ShapeDtypeStruct((flat_size, LANES), f32)
    collect = pl.pallas_call(
        functools.partial(collect_kernel, dims),
        out_shape=flat_shape,
        in_specs=vmem(1 + span),
        out_specs=vmem(1)[0],
        compiler_params=PARAMS,
        name="collect",
    )
    flat = collect(pick, *mid_takes)
    out, _ = pl.pallas_call(
        functools.partial(finish_kernel, dims),
        out_shape=[jax.ShapeDtypeStruct(flat_state.shape, f32), flat_shape],
        in_specs=vmem(4 + span // 2),
        out_specs=anywhere(1) + vmem(1),
        scratch_shapes=[
            pltpu.VMEM(flat_state.shape, f32),
            pltpu.SemaphoreType.DMA((chunks,)),
        ],
        input_output_aliases={2: 1},
        compiler_params=PARAMS,
        name="finish",
    )(pick, flat_state, flat, *end_takes)
    return out.reshape(state.shape)


def from_behind(value, axis, steps):
    count = lax.axis_size(axis)
    pairs = [(source, (source + steps) % count) for source in range(count)]
    return lax.ppermute(value, axis, pairs)


def gll_tables():
    near_point = math.sqrt(1.0 / 3.0 - 2.0 * math.sqrt(7.0) / 21.0)
    far_point = math.sqrt(1.0 / 3.0 + 2.0 * math.sqrt(7.0) / 21.0)
    points = np.array([-1.0, -far_point, -near_point, near_point, far_point, 1.0])
    weights = np.array(
        [
            1.0
            / np.prod([points[column] - points[second] for second in range(6) if second != column])
            for column in range(6)
        ]
    )
    deriv = np.zeros((6, 6))
    for target in range(6):
        for source in range(6):
            if source != target:
                deriv[target, source] = (
                    weights[source] / weights[target] / (points[target] - points[source])
                )
        deriv[target, target] = -np.sum(deriv[target])
    identity = np.eye(6)
    along_x = np.kron(deriv, identity)
    along_y = np.kron(identity, deriv)
    edge_nodes = np.array(
        [
            [offset for offset in range(6)],
            [30 + offset for offset in range(6)],
            [6 * offset for offset in range(6)],
            [6 * offset + 5 for offset in range(6)],
        ]
    ).reshape(-1)
    lifting = np.zeros((36, 24))
    lifting[edge_nodes, np.arange(24)] = 1.0
    return (
        jnp.asarray(along_x, jnp.float32),
        jnp.asarray(along_y, jnp.float32),
        edge_nodes,
        jnp.asarray(lifting, jnp.float32),
    )


def spanwise_basis(count):
    mode_index = jnp.arange(count, dtype=jnp.int32)
    planes = jnp.arange(count, dtype=jnp.int32)
    phase = mode_index[:, None] // 2 * planes[None, :] % count
    phase_angle = phase.astype(jnp.float32) * (2.0 * math.pi / count)
    odd_rows = (mode_index % 2 == 1)[:, None]
    basis_table = jnp.where(odd_rows, jnp.sin(phase_angle), jnp.cos(phase_angle)) * math.sqrt(
        2.0 / count
    )
    alternate = (1 - 2 * (planes % 2)).astype(jnp.float32) / math.sqrt(count)
    constant = jnp.ones((count,), jnp.float32) / math.sqrt(count)
    basis_table = jnp.where(mode_index[:, None] == 0, constant[None, :], basis_table)
    basis_table = jnp.where(mode_index[:, None] == 1, alternate[None, :], basis_table)
    return basis_table


def spanwise_derivative(modal):
    shape_in = modal.shape
    paired = modal.reshape(shape_in[0], shape_in[1] // 2, 2, shape_in[2])
    wavenumber = jnp.arange(shape_in[1] // 2, dtype=jnp.int32).astype(jnp.float32)[None, :, None]
    return jnp.stack([wavenumber * paired[:, :, 1], -wavenumber * paired[:, :, 0]], axis=2).reshape(
        shape_in
    )


def planar_terms(flux_x, flux_y, metric_part):
    along_x, along_y, edge_nodes, _ = gll_tables()
    scale_x = metric_part[0][:, None]
    scale_y = metric_part[1][:, None]
    grad_x = jnp.einsum("pq,vmeq->vmep", along_x, flux_x, precision=HIGHEST)
    grad_y = jnp.einsum("pq,vmeq->vmep", along_y, flux_y, precision=HIGHEST)
    planar = scale_x * grad_x + scale_y * grad_y
    sign_x = jnp.sign(scale_x)
    sign_y = jnp.sign(scale_y)
    edge_flux = jnp.concatenate(
        [
            -sign_x * flux_x[:, :, :, edge_nodes[0:6]],
            sign_x * flux_x[:, :, :, edge_nodes[6:12]],
            -sign_y * flux_y[:, :, :, edge_nodes[12:18]],
            sign_y * flux_y[:, :, :, edge_nodes[18:24]],
        ],
        axis=3,
    )
    return (planar, edge_flux)


def node_major(flat, num_vars, local_modes, nodes, local_elems):
    return jnp.transpose(flat.reshape(num_vars, local_modes, local_elems, nodes), (0, 1, 3, 2))


def trace_pool(traces):
    shape_in = traces.shape
    return (
        traces.reshape(shape_in[0], shape_in[1], 4, 6, shape_in[3])
        .transpose(0, 1, 3, 4, 2)
        .reshape(shape_in[0], shape_in[1], 6, 4 * shape_in[3])
    )


def own_pools(state_local, normal_flux):
    edge_nodes = gll_tables()[2]
    return (trace_pool(state_local[:, :, edge_nodes, :]), trace_pool(normal_flux))


def update(
    state_local,
    divergence,
    own_q,
    own_flux,
    from_lower,
    from_upper,
    neighbour,
    orient,
    wall,
    metric_local,
    first_mode,
    total_modes,
):
    lifting = gll_tables()[3]
    num_vars, modes_here, _, count = state_local.shape
    pool_q = jnp.concatenate([own_q, from_lower[0], from_upper[0]], axis=3)
    pool_flux = jnp.concatenate([own_flux, from_lower[1], from_upper[1]], axis=3)
    flat_index = neighbour.reshape(-1)
    other_q = jnp.take(pool_q, flat_index, axis=3)
    other_flux = jnp.take(pool_flux, flat_index, axis=3)
    flipped = orient.reshape(-1) == 1
    other_q = jnp.where(flipped, other_q[:, :, ::-1, :], other_q)
    other_flux = jnp.where(flipped, other_flux[:, :, ::-1, :], other_flux)
    mirror = jnp.array([-1.0, -1.0, -1.0, 1.0], jnp.float32).reshape(4, 1, 1, 1)
    walled = wall.reshape(-1) == 1
    other_q = jnp.where(walled, mirror * own_q, other_q)
    other_flux = jnp.where(walled, mirror * own_flux, other_flux)
    magnitude = (
        jnp.abs(
            jnp.stack([metric_local[0], metric_local[0], metric_local[1], metric_local[1]], axis=1)
        ).reshape(-1)
        * 15.0
    )
    surface_jump = magnitude * (0.5 * (own_flux + other_flux) - 0.5 * PENALTY * (own_q - other_q))
    unpooled = (
        surface_jump.reshape(num_vars, modes_here, 6, count, 4)
        .transpose(0, 1, 4, 2, 3)
        .reshape(num_vars, modes_here, 24, count)
    )
    surface = jnp.einsum("pq,vmqe->vmpe", lifting, unpooled, precision=HIGHEST)
    mode_index = first_mode + jnp.arange(modes_here, dtype=jnp.int32)
    wavenumber = jnp.where(mode_index == 1, total_modes // 2, mode_index // 2).astype(jnp.float32)
    damping = 1.0 + TIME_STEP * VISCOSITY * wavenumber * wavenumber
    return (state_local + TIME_STEP * (surface - divergence)) / damping[None, :, None, None]


def plain_body(state, metric, neighbour, orient, wall, rim):
    num_vars, local_modes, flat_size = state.shape
    num_nodes = 36
    local_elems = flat_size // num_nodes
    span_size = lax.axis_size("span")
    total_modes = local_modes * span_size
    share = local_elems // span_size
    state_nodes = node_major(state, num_vars, local_modes, num_nodes, local_elems)
    planes_in = lax.all_to_all(state, "span", split_axis=2, concat_axis=1, tiled=True)
    basis_table = spanwise_basis(total_modes)
    physical = jnp.einsum("mn,vmk->vnk", basis_table, planes_in, precision=HIGHEST)
    metric_part = lax.dynamic_slice_in_dim(metric, lax.axis_index("span") * share, share, axis=1)
    shape_here = (num_vars, total_modes, share, num_nodes)
    planar_div, edge_flux = planar_terms(
        (physical[0:1] * physical).reshape(shape_here),
        (physical[1:2] * physical).reshape(shape_here),
        metric_part,
    )
    volume_fields = jnp.concatenate(
        [planar_div.reshape(num_vars, total_modes, share * num_nodes), physical[2:3] * physical],
        axis=0,
    )
    volume_modal = jnp.einsum("mn,vnk->vmk", basis_table, volume_fields, precision=HIGHEST)
    edge_modal = jnp.einsum(
        "mn,vnk->vmk",
        basis_table,
        edge_flux.reshape(num_vars, total_modes, share * 24),
        precision=HIGHEST,
    )
    combined = volume_modal[0:4] + spanwise_derivative(volume_modal[4:8])
    div_flat, flux_flat = (
        lax.all_to_all(combined, "span", split_axis=1, concat_axis=2, tiled=True),
        lax.all_to_all(edge_modal, "span", split_axis=1, concat_axis=2, tiled=True),
    )
    divergence = node_major(div_flat, num_vars, local_modes, num_nodes, local_elems)
    normal_flux = node_major(flux_flat, num_vars, local_modes, 24, local_elems)
    own_q, own_flux = own_pools(state_nodes, normal_flux)
    upper_rim = jnp.stack([jnp.take(own_q, rim[1], axis=3), jnp.take(own_flux, rim[1], axis=3)])
    lower_rim = jnp.stack([jnp.take(own_q, rim[0], axis=3), jnp.take(own_flux, rim[0], axis=3)])
    from_lower = from_behind(upper_rim, "elem", 1)
    from_upper = from_behind(lower_rim, "elem", -1)
    first_mode = lax.axis_index("span") * local_modes
    result = update(
        state_nodes,
        divergence,
        own_q,
        own_flux,
        from_lower,
        from_upper,
        neighbour,
        orient,
        wall,
        metric,
        first_mode,
        total_modes,
    )
    return jnp.transpose(result, (0, 1, 3, 2)).reshape(num_vars, local_modes, flat_size)


def body(state, metric, neighbour, orient, wall, rim):
    num_vars, modes, flat_size = state.shape
    span = lax.axis_size("span")
    groups = lax.axis_size("elem")
    elems = flat_size // NODES
    rows = rim.shape[1]
    fits = (
        groups % 2 == 0
        and rows % span == 0
        and SUB == 2 * (elems // rows)
        and num_vars * modes == LANES
        and modes * 4 == LANES
        and span % 4 == 0
        and span & (span - 1) == 0
        and LANES % elems == 0
        and elems == SUB * span
        and elems % rows == 0
        and SUB % (elems // rows) == 0
        and flat_size % CHUNK == 0
        and flat_size % FETCH == 0
    )
    if not fits:
        return plain_body(state, metric, neighbour, orient, wall, rim)
    return ordered_body(state, metric, neighbour, wall, rim)


def solution(mesh):
    placed = (
        P(None, "span", "elem"),
        P(None, "elem"),
        P("elem", None),
        P("elem", None),
        P("elem", None),
        P(None, "elem"),
    )
    return jax.shard_map(
        body, mesh=mesh, in_specs=placed, out_specs=P(None, "span", "elem"), check_vma=False
    )
```
